256 devices in a mesh: build: 2 (over y_lo), test: 8 (over x, core), stmt: 16 (over y_hi, z).
Axes of the slice: x: 4, y: 4 (y_hi: 2, y_lo: 2; y = y_hi * 2 + y_lo), z: 8, core: 2. Of those that a mesh axis runs over, the one named last changes fastest.
Arguments:
- tile_values: bfloat16 [2, 8, 16, 2, 128, 128, 128], P('build', 'test', 'stmt'), may hold values from -6 to 6
- tile_test: int32 [2, 8, 16, 2], P('build', 'test', 'stmt'), may hold values from 0 to 3, as said below
- tile_stmt: int32 [2, 8, 16, 2], P('build', 'test', 'stmt'), may hold values from 0 to 1, as said below
- tile_build: int32 [2, 8, 16, 2], P('build', 'test', 'stmt'), may hold values from 0 to 5, as said below
- tile_count: int32 [2, 8, 16], P('build', 'test', 'stmt'), may hold values from 0 to 2, as said below
- test_factor: bfloat16 [8, 512, 256], P('test', ('build', 'stmt')), may hold values from -0.027063294 to 0.027063294
- build_factor: bfloat16 [2, 768, 256], P('build', ('test', 'stmt')), may hold values from -0.027063294 to 0.027063294
Outputs:
- stmt_factor: float32 [16, 256, 256], P('stmt', ('build', 'test'))
The draws below stay inside these ranges and needn't reach their ends.
Inputs may be any that keep to these rules, and one draw needn't show every extreme that they name: `tile_count`: slots from this count on hold padding: their values and block numbers must not contribute. Some grid position has every slot live and some has none. `tile_test`: test block of a slot; the largest block is named in every draw. `tile_stmt`: statement block of a slot; the largest block is named in every draw. `tile_build`: build block of a slot; the largest block is named in every draw.
All inputs are finite; a program needn't handle non-finite values.
Results may differ from the reference program's by a relative error of at most 0.003.
Values may be sent and summed in bfloat16 or wider, within the bound.
A program may use at most 64 MiB of HBM per device.

```python
import jax
import jax.numpy as jnp
from jax import lax

R = 256
TILE = 128
CAP = 2
TB = 4
SB = 2
BB = 6
N_BUILD = 2
N_TEST = 8
N_STMT = 16


def forced_blocks(key, dims_shape, upper_bound):
    key_one, key_two = jax.random.split(key)
    drawn_values = jax.random.randint(key_one, dims_shape, 0, upper_bound, dtype=jnp.int32)
    flat_draw = drawn_values.reshape(-1)
    spot_index = jax.random.randint(key_two, (), 0, flat_draw.shape[0], dtype=jnp.int32)
    return flat_draw.at[spot_index].set(upper_bound - 1).reshape(dims_shape)


def correlated_factor(key, dims_shape):
    base_scale = float(TB * TILE * N_TEST * BB * N_BUILD) ** (-0.5)
    key_one, key_two, key_three = jax.random.split(key, 3)
    rows_shape = dims_shape[:-1] + (1,)
    noise_part = jax.random.normal(key_one, dims_shape, jnp.float32)
    common = jax.random.normal(key_two, rows_shape, jnp.float32)
    offset = jax.random.uniform(key_three, (dims_shape[-1],), jnp.float32, 0.1, 0.3)
    row_scale = jnp.ones(rows_shape, jnp.float32)
    values = base_scale * row_scale * (0.85 * noise_part + 0.45 * common + offset)
    return jnp.clip(values, -6.0 * base_scale, 6.0 * base_scale)


def draw_test_factor(key, part):
    return correlated_factor(jax.random.fold_in(key, 21), (N_TEST, TB * TILE, R)).astype(jnp.bfloat16)


def draw_build_factor(key, part):
    return correlated_factor(jax.random.fold_in(key, 22), (N_BUILD, BB * TILE, R)).astype(jnp.bfloat16)


def draw_tile_test(key, part):
    return forced_blocks(jax.random.fold_in(key, 11), (N_BUILD, N_TEST, N_STMT, CAP), TB)


def draw_tile_stmt(key, part):
    return forced_blocks(jax.random.fold_in(key, 12), (N_BUILD, N_TEST, N_STMT, CAP), SB)


def draw_tile_build(key, part):
    return forced_blocks(jax.random.fold_in(key, 13), (N_BUILD, N_TEST, N_STMT, CAP), BB)


def draw_tile_count(key, part):
    key_one, key_two, key_three = jax.random.split(jax.random.fold_in(key, 14), 3)
    dims_shape = (N_BUILD, N_TEST, N_STMT)
    slot_level = jax.random.randint(key_one, dims_shape, 0, CAP + 1, dtype=jnp.int32)
    slot_active = jax.random.randint(key_two, dims_shape, 0, 2, dtype=jnp.int32)
    flat_draw = (slot_level * slot_active).reshape(-1)
    total_cells = flat_draw.shape[0]
    spot_index = jax.random.randint(key_three, (), 0, total_cells, dtype=jnp.int32)
    flat_draw = flat_draw.at[spot_index].set(CAP)
    flat_draw = flat_draw.at[(spot_index + 1) % total_cells].set(0)
    return flat_draw.reshape(dims_shape)


def steps_of(key, dims, shards, low, largest):
    def one(axis_at, shards_of):
        steps = jax.random.uniform(jax.random.fold_in(jax.random.fold_in(key, 6), axis_at), (shards_of,), jnp.float32, low / len(shards), largest / len(shards))
        return jnp.repeat(jnp.exp(steps), dims[axis_at] // shards_of).reshape((-1,) + (1,) * (len(dims) - axis_at - 1))

    level = one(*shards[0])
    for cut in shards[1:]:
        level = level * one(*cut)
    return level


def normal_values(rng, dims, width, most, cuts=(), kind=jnp.bfloat16):
    loudness = steps_of(rng, dims, cuts, -0.22, 0.18) if cuts else 1.0
    values = jax.random.normal(rng, dims, jnp.float32) * width * loudness
    return jnp.minimum(jnp.maximum(values, -most), most).astype(kind)


def setup_inputs(seed: int = 0) -> dict:
    splits = jax.random.split(jax.random.key(seed), 8)
    return {
        "tile_values": normal_values(splits[0], (N_BUILD, N_TEST, N_STMT, CAP, TILE, TILE, TILE), 1.0, 6.0, ((0, 2), (1, 8), (2, 16))),
        "tile_test": draw_tile_test(jax.random.fold_in(splits[7], 71), 0),
        "tile_stmt": draw_tile_stmt(jax.random.fold_in(splits[7], 71), 0),
        "tile_build": draw_tile_build(jax.random.fold_in(splits[7], 71), 0),
        "tile_count": draw_tile_count(jax.random.fold_in(splits[7], 71), 0),
        "test_factor": draw_test_factor(jax.random.fold_in(splits[7], 71), 0),
        "build_factor": draw_build_factor(jax.random.fold_in(splits[7], 71), 0),
    }


def reference(tile_values, tile_test, tile_stmt, tile_build, tile_count, test_factor, build_factor):
    count_build, count_test, count_stmt, slot_total, tile_width = tile_values.shape[:5]
    rank_width = test_factor.shape[-1]
    slice_rows = SB * TILE
    initial = jnp.zeros((count_stmt * slice_rows, rank_width), jnp.float32)
    zero_index = jnp.int32(0)

    def step_fn(running_sum, item_index):
        device_pos = item_index // slot_total
        slot_index = item_index % slot_total
        build_pos = device_pos // (count_test * count_stmt)
        test_pos = device_pos // count_stmt % count_test
        stmt_pos = device_pos % count_stmt

        def compute(accum):
            tile_block = lax.dynamic_slice(tile_values, (build_pos, test_pos, stmt_pos, slot_index, zero_index, zero_index, zero_index), (1, 1, 1, 1, tile_width, tile_width, tile_width))[0, 0, 0, 0].astype(jnp.float32)
            test_number = tile_test[build_pos, test_pos, stmt_pos, slot_index]
            build_number = tile_build[build_pos, test_pos, stmt_pos, slot_index]
            stmt_number = tile_stmt[build_pos, test_pos, stmt_pos, slot_index]
            test_block = lax.dynamic_slice(test_factor, (test_pos, (test_number * tile_width).astype(jnp.int32), zero_index), (1, tile_width, rank_width))[0].astype(jnp.float32)
            build_block = lax.dynamic_slice(build_factor, (build_pos, (build_number * tile_width).astype(jnp.int32), zero_index), (1, tile_width, rank_width))[0].astype(jnp.float32)
            khatri_rao = (test_block[:, None, :] * build_block[None, :, :]).astype(jnp.bfloat16).astype(jnp.float32)
            term = jnp.einsum('ijk,ikr->jr', tile_block, khatri_rao, precision=lax.Precision.HIGHEST)
            start_row = (stmt_pos * slice_rows + stmt_number * tile_width).astype(jnp.int32)
            current = lax.dynamic_slice_in_dim(accum, start_row, tile_width, 0)
            return lax.dynamic_update_slice_in_dim(accum, current + term, start_row, 0)
        live_slot = slot_index < tile_count[build_pos, test_pos, stmt_pos]
        return (lax.cond(live_slot, compute, lambda accum: accum, running_sum), None)
    item_total = count_build * count_test * count_stmt * slot_total
    mttkrp, unused = lax.scan(step_fn, initial, jnp.arange(item_total, dtype=jnp.int32))
    test_rows = test_factor.reshape(-1, rank_width)
    build_rows = build_factor.reshape(-1, rank_width)
    gram_test = jnp.dot(test_rows.T.astype(jnp.float32), test_rows.astype(jnp.float32), preferred_element_type=jnp.float32)
    gram_build = jnp.dot(build_rows.T.astype(jnp.float32), build_rows.astype(jnp.float32), preferred_element_type=jnp.float32)
    gram = gram_test * gram_build
    lower = jnp.linalg.cholesky(gram)
    halfway = lax.linalg.triangular_solve(lower, mttkrp, left_side=False, lower=True, transpose_a=True)
    solved = lax.linalg.triangular_solve(lower, halfway, left_side=False, lower=True, transpose_a=False)
    return solved.reshape(count_stmt, slice_rows, rank_width)
```

```python
import jax
import jax.numpy as jnp
from jax import lax
from jax.sharding import PartitionSpec as P

TILE = 128
SB = 2
ALL = ("build", "test", "stmt")


def shards(tile_values, tile_test, tile_stmt, tile_build, tile_count, test_factor, build_factor):
    test_rows = test_factor[0]
    build_rows = build_factor[0]
    local_grams = jnp.stack(
        [
            lax.dot_general(test_rows, test_rows, (((0,), (0,)), ((), ())), preferred_element_type=jnp.float32),
            lax.dot_general(build_rows, build_rows, (((0,), (0,)), ((), ())), preferred_element_type=jnp.float32),
        ]
    )
    grams = lax.psum(local_grams, ALL)
    gram = grams[0] * grams[1]
    lower = jnp.linalg.cholesky(gram)

    test_slab = lax.all_gather(test_rows, ("build", "stmt"), axis=0, tiled=True)
    build_slab = lax.all_gather(build_rows, ("test", "stmt"), axis=0, tiled=True)
    slot_values = tile_values[0, 0, 0]
    slot_tests = tile_test[0, 0, 0]
    slot_stmts = tile_stmt[0, 0, 0]
    slot_builds = tile_build[0, 0, 0]
    live_count = tile_count[0, 0, 0]
    tile_width = slot_values.shape[-1]
    rank_width = test_slab.shape[1]
    running_sum = jnp.zeros((SB * TILE, rank_width), jnp.float32)
    for slot_index in range(slot_values.shape[0]):
        test_block = lax.dynamic_slice_in_dim(
            test_slab, slot_tests[slot_index] * tile_width, tile_width, 0
        ).astype(jnp.float32)
        build_block = lax.dynamic_slice_in_dim(
            build_slab, slot_builds[slot_index] * tile_width, tile_width, 0
        ).astype(jnp.float32)
        khatri_rao = (test_block[:, None, :] * build_block[None, :, :]).astype(jnp.bfloat16)
        term = jnp.einsum(
            "ijk,ikr->jr", slot_values[slot_index], khatri_rao, preferred_element_type=jnp.float32
        )
        live_weight = (slot_index < live_count).astype(jnp.float32)
        accumulate_term = term * live_weight
        start_row = slot_stmts[slot_index] * tile_width
        current = lax.dynamic_slice_in_dim(running_sum, start_row, tile_width, 0)
        running_sum = lax.dynamic_update_slice_in_dim(
            running_sum, current + accumulate_term, start_row, 0
        )
    owned_sums = lax.psum_scatter(running_sum, ("build", "test"), scatter_dimension=0, tiled=True)
    halfway = lax.linalg.triangular_solve(
        lower, owned_sums, left_side=False, lower=True, transpose_a=True
    )
    solved = lax.linalg.triangular_solve(
        lower, halfway, left_side=False, lower=True, transpose_a=False
    )
    return solved[None]


def solution(mesh):
    return jax.shard_map(
        shards,
        mesh=mesh,
        in_specs=(
            P("build", "test", "stmt", None, None, None, None),
            P("build", "test", "stmt", None),
            P("build", "test", "stmt", None),
            P("build", "test", "stmt", None),
            P("build", "test", "stmt"),
            P("test", ("build", "stmt"), None),
            P("build", ("test", "stmt"), None),
        ),
        out_specs=P("stmt", ("build", "test"), None),
        check_vma=False,
    )
```

```python
import functools

import jax
import jax.numpy as jnp
from jax import lax
from jax.experimental import pallas as pl
from jax.experimental.pallas import tpu as pltpu
from jax.sharding import PartitionSpec as P

TILE = 128
SB = 2
MESH = pl.DeviceIdType.MESH


def gather_kernel(n_build, n_test, n_stmt, test_in, build_in, test_out, build_out,
                  test_scr, build_scr, test_send, test_recv, build_send, build_recv):
    b = lax.axis_index("build")
    t = lax.axis_index("test")
    s = lax.axis_index("stmt")
    my_p = b * n_stmt + s
    my_q = t * n_stmt + s

    def test_out_copy(p):
        return pltpu.make_async_remote_copy(
            src_ref=test_in, dst_ref=test_scr.at[my_p], send_sem=test_send.at[p],
            recv_sem=test_recv.at[my_p], device_id=(p // n_stmt, t, p % n_stmt),
            device_id_type=MESH)

    def test_in_copy(p):
        return pltpu.make_async_remote_copy(
            src_ref=test_in, dst_ref=test_scr.at[p], send_sem=test_send.at[p],
            recv_sem=test_recv.at[p], device_id=(p // n_stmt, t, p % n_stmt),
            device_id_type=MESH)

    def build_out_copy(q):
        return pltpu.make_async_remote_copy(
            src_ref=build_in, dst_ref=build_scr.at[my_q], send_sem=build_send.at[q],
            recv_sem=build_recv.at[my_q], device_id=(b, q // n_stmt, q % n_stmt),
            device_id_type=MESH)

    def build_in_copy(q):
        return pltpu.make_async_remote_copy(
            src_ref=build_in, dst_ref=build_scr.at[q], send_sem=build_send.at[q],
            recv_sem=build_recv.at[q], device_id=(b, q // n_stmt, q % n_stmt),
            device_id_type=MESH)

    def start_test(p, carry):
        @pl.when(p != my_p)
        def _():
            test_out_copy(p).start()
        return carry

    def start_build(q, carry):
        @pl.when(q != my_q)
        def _():
            build_out_copy(q).start()
        return carry

    lax.fori_loop(0, n_build * n_stmt, start_test, 0)
    lax.fori_loop(0, n_test * n_stmt, start_build, 0)
    test_scr[pl.ds(my_p, 1)] = test_in[...][None]
    build_scr[pl.ds(my_q, 1)] = build_in[...][None]

    def wait_test(p, carry):
        @pl.when(p != my_p)
        def _():
            test_out_copy(p).wait_send()
            test_in_copy(p).wait_recv()
        return carry

    def wait_build(q, carry):
        @pl.when(q != my_q)
        def _():
            build_out_copy(q).wait_send()
            build_in_copy(q).wait_recv()
        return carry

    lax.fori_loop(0, n_build * n_stmt, wait_test, 0)
    lax.fori_loop(0, n_test * n_stmt, wait_build, 0)
    test_out[...] = test_scr[...]
    build_out[...] = build_scr[...]


def gather_factors(test_rows, build_rows):
    n_build = lax.axis_size("build")
    n_test = lax.axis_size("test")
    n_stmt = lax.axis_size("stmt")
    n_p = n_build * n_stmt
    n_q = n_test * n_stmt
    vmem = pl.BlockSpec(memory_space=pltpu.VMEM)
    test_pieces, build_pieces = pl.pallas_call(
        functools.partial(gather_kernel, n_build, n_test, n_stmt),
        out_shape=(
            jax.ShapeDtypeStruct((n_p, *test_rows.shape), test_rows.dtype),
            jax.ShapeDtypeStruct((n_q, *build_rows.shape), build_rows.dtype),
        ),
        in_specs=[vmem, vmem],
        out_specs=(vmem, vmem),
        scratch_shapes=[
            pltpu.VMEM((n_p, *test_rows.shape), test_rows.dtype),
            pltpu.VMEM((n_q, *build_rows.shape), build_rows.dtype),
            pltpu.SemaphoreType.DMA((n_p,)),
            pltpu.SemaphoreType.DMA((n_p,)),
            pltpu.SemaphoreType.DMA((n_q,)),
            pltpu.SemaphoreType.DMA((n_q,)),
        ],
        compiler_params=pltpu.CompilerParams(has_side_effects=True),
    )(test_rows, build_rows)
    return (
        test_pieces.reshape(-1, test_rows.shape[-1]),
        build_pieces.reshape(-1, build_rows.shape[-1]),
    )


def copy_for_each(x, axis):
    copies = jnp.broadcast_to(x, (lax.axis_size(axis), *x.shape))
    return lax.all_to_all(copies, axis, split_axis=0, concat_axis=0, tiled=True)


def over_copies(x, axis):
    everything = copy_for_each(x, axis)
    return jnp.sum(everything, axis=0)


def shards(tile_values, tile_test, tile_stmt, tile_build, tile_count, test_factor, build_factor):
    test_slab, build_slab = gather_factors(test_factor[0], build_factor[0])
    slot_values = tile_values[0, 0, 0]
    slot_tests = tile_test[0, 0, 0]
    slot_stmts = tile_stmt[0, 0, 0]
    slot_builds = tile_build[0, 0, 0]
    live_count = tile_count[0, 0, 0]
    tile_width = slot_values.shape[-1]
    rank_width = test_slab.shape[1]
    running_sum = jnp.zeros((SB * TILE, rank_width), jnp.float32)
    for slot_index in range(slot_values.shape[0]):
        test_block = lax.dynamic_slice_in_dim(
            test_slab, slot_tests[slot_index] * tile_width, tile_width, 0
        ).astype(jnp.float32)
        build_block = lax.dynamic_slice_in_dim(
            build_slab, slot_builds[slot_index] * tile_width, tile_width, 0
        ).astype(jnp.float32)
        khatri_rao = (test_block[:, None, :] * build_block[None, :, :]).astype(jnp.bfloat16)
        term = jnp.einsum(
            "ijk,ikr->jr", slot_values[slot_index], khatri_rao, preferred_element_type=jnp.float32
        )
        live_weight = (slot_index < live_count).astype(jnp.float32)
        accumulate_term = term * live_weight
        start_row = slot_stmts[slot_index] * tile_width
        current = lax.dynamic_slice_in_dim(running_sum, start_row, tile_width, 0)
        running_sum = lax.dynamic_update_slice_in_dim(
            running_sum, current + accumulate_term, start_row, 0
        )
    owned_sums = lax.psum_scatter(running_sum, ("build", "test"), scatter_dimension=0, tiled=True)
    slab_test_gram = jnp.dot(test_slab.T, test_slab, preferred_element_type=jnp.float32)
    slab_build_gram = jnp.dot(build_slab.T, build_slab, preferred_element_type=jnp.float32)
    gram_test = over_copies(slab_test_gram, "test")
    gram_build = over_copies(slab_build_gram, "build")
    gram = gram_test * gram_build
    lower = jnp.linalg.cholesky(gram)
    halfway = lax.linalg.triangular_solve(
        lower, owned_sums, left_side=False, lower=True, transpose_a=True
    )
    solved = lax.linalg.triangular_solve(
        lower, halfway, left_side=False, lower=True, transpose_a=False
    )
    return solved[None]


def solution(mesh):
    return jax.shard_map(
        shards,
        mesh=mesh,
        in_specs=(
            P("build", "test", "stmt", None, None, None, None),
            P("build", "test", "stmt", None),
            P("build", "test", "stmt", None),
            P("build", "test", "stmt", None),
            P("build", "test", "stmt"),
            P("test", ("build", "stmt"), None),
            P("build", ("test", "stmt"), None),
        ),
        out_specs=P("stmt", ("build", "test"), None),
        check_vma=False,
    )
```

```python
import functools

import jax
import jax.numpy as jnp
from jax import lax
from jax.experimental import pallas as pl
from jax.experimental.pallas import tpu as pltpu
from jax.sharding import PartitionSpec as P

TILE = 128
SB = 2
MESH = pl.DeviceIdType.MESH


def gather_kernel(n_build, n_test, n_stmt, test_in, build_in, test_out, build_out,
                  test_scr, build_scr, test_send, test_recv, build_send, build_recv):
    b = lax.axis_index("build")
    t = lax.axis_index("test")
    s = lax.axis_index("stmt")
    my_p = b * n_stmt + s
    my_q = t * n_stmt + s

    def test_out_copy(p):
        return pltpu.make_async_remote_copy(
            src_ref=test_in, dst_ref=test_scr.at[my_p], send_sem=test_send.at[p],
            recv_sem=test_recv.at[my_p], device_id=(p // n_stmt, t, p % n_stmt),
            device_id_type=MESH)

    def test_in_copy(p):
        return pltpu.make_async_remote_copy(
            src_ref=test_in, dst_ref=test_scr.at[p], send_sem=test_send.at[p],
            recv_sem=test_recv.at[p], device_id=(p // n_stmt, t, p % n_stmt),
            device_id_type=MESH)

    def build_out_copy(q):
        return pltpu.make_async_remote_copy(
            src_ref=build_in, dst_ref=build_scr.at[my_q], send_sem=build_send.at[q],
            recv_sem=build_recv.at[my_q], device_id=(b, q // n_stmt, q % n_stmt),
            device_id_type=MESH)

    def build_in_copy(q):
        return pltpu.make_async_remote_copy(
            src_ref=build_in, dst_ref=build_scr.at[q], send_sem=build_send.at[q],
            recv_sem=build_recv.at[q], device_id=(b, q // n_stmt, q % n_stmt),
            device_id_type=MESH)

    def start_test(p, carry):
        @pl.when(p != my_p)
        def _():
            test_out_copy(p).start()
        return carry

    def start_build(q, carry):
        @pl.when(q != my_q)
        def _():
            build_out_copy(q).start()
        return carry

    lax.fori_loop(0, n_build * n_stmt, start_test, 0)
    lax.fori_loop(0, n_test * n_stmt, start_build, 0)
    test_scr[pl.ds(my_p, 1)] = test_in[...][None]
    build_scr[pl.ds(my_q, 1)] = build_in[...][None]

    def wait_test(p, carry):
        @pl.when(p != my_p)
        def _():
            test_out_copy(p).wait_send()
            test_in_copy(p).wait_recv()
        return carry

    def wait_build(q, carry):
        @pl.when(q != my_q)
        def _():
            build_out_copy(q).wait_send()
            build_in_copy(q).wait_recv()
        return carry

    lax.fori_loop(0, n_build * n_stmt, wait_test, 0)
    lax.fori_loop(0, n_test * n_stmt, wait_build, 0)
    test_out[...] = test_scr[...]
    build_out[...] = build_scr[...]


def gather_factors(test_rows, build_rows):
    n_build = lax.axis_size("build")
    n_test = lax.axis_size("test")
    n_stmt = lax.axis_size("stmt")
    n_p = n_build * n_stmt
    n_q = n_test * n_stmt
    vmem = pl.BlockSpec(memory_space=pltpu.VMEM)
    test_pieces, build_pieces = pl.pallas_call(
        functools.partial(gather_kernel, n_build, n_test, n_stmt),
        out_shape=(
            jax.ShapeDtypeStruct((n_p, *test_rows.shape), test_rows.dtype),
            jax.ShapeDtypeStruct((n_q, *build_rows.shape), build_rows.dtype),
        ),
        in_specs=[vmem, vmem],
        out_specs=(vmem, vmem),
        scratch_shapes=[
            pltpu.VMEM((n_p, *test_rows.shape), test_rows.dtype),
            pltpu.VMEM((n_q, *build_rows.shape), build_rows.dtype),
            pltpu.SemaphoreType.DMA((n_p,)),
            pltpu.SemaphoreType.DMA((n_p,)),
            pltpu.SemaphoreType.DMA((n_q,)),
            pltpu.SemaphoreType.DMA((n_q,)),
        ],
        compiler_params=pltpu.CompilerParams(has_side_effects=True),
    )(test_rows, build_rows)
    return (
        test_pieces.reshape(-1, test_rows.shape[-1]),
        build_pieces.reshape(-1, build_rows.shape[-1]),
    )


def sweep_kernel(g_ref, out_ref):
    n = g_ref.shape[0]
    out_ref[...] = g_ref[...]
    lane = lax.broadcasted_iota(jnp.int32, (1, n), 1)

    def step(k, carry):
        row = out_ref[pl.ds(k, 1), :]
        is_k = lane == k
        pivot = jnp.sum(jnp.where(is_k, row, 0.0), axis=1, keepdims=True)
        inv = 1.0 / pivot
        scaled = jnp.where(is_k, 1.0 - inv, row * inv)
        column = jnp.transpose(jnp.broadcast_to(row, (8, n)))[:, 0:1]
        out_ref[...] = out_ref[...] - column * scaled
        out_ref[pl.ds(k, 1), :] = jnp.where(is_k, -inv, row * inv)
        return carry

    lax.fori_loop(0, n, step, 0)
    out_ref[...] = -out_ref[...]


def spd_inverse(gram):
    vmem = pl.BlockSpec(memory_space=pltpu.VMEM)
    return pl.pallas_call(
        sweep_kernel,
        out_shape=jax.ShapeDtypeStruct(gram.shape, jnp.float32),
        in_specs=[vmem],
        out_specs=vmem,
    )(gram)


def copy_for_each(x, axis):
    copies = jnp.broadcast_to(x, (lax.axis_size(axis), *x.shape))
    return lax.all_to_all(copies, axis, split_axis=0, concat_axis=0, tiled=True)


def over_copies(x, axis):
    everything = copy_for_each(x, axis)
    return jnp.sum(everything, axis=0)


def shards(tile_values, tile_test, tile_stmt, tile_build, tile_count, test_factor, build_factor):
    test_slab, build_slab = gather_factors(test_factor[0], build_factor[0])
    slot_values = tile_values[0, 0, 0]
    slot_tests = tile_test[0, 0, 0]
    slot_stmts = tile_stmt[0, 0, 0]
    slot_builds = tile_build[0, 0, 0]
    live_count = tile_count[0, 0, 0]
    tile_width = slot_values.shape[-1]
    rank_width = test_slab.shape[1]
    running_sum = jnp.zeros((SB * TILE, rank_width), jnp.float32)
    for slot_index in range(slot_values.shape[0]):
        test_block = lax.dynamic_slice_in_dim(
            test_slab, slot_tests[slot_index] * tile_width, tile_width, 0
        ).astype(jnp.float32)
        build_block = lax.dynamic_slice_in_dim(
            build_slab, slot_builds[slot_index] * tile_width, tile_width, 0
        ).astype(jnp.float32)
        khatri_rao = (test_block[:, None, :] * build_block[None, :, :]).astype(jnp.bfloat16)
        term = jnp.einsum(
            "ijk,ikr->jr", slot_values[slot_index], khatri_rao, preferred_element_type=jnp.float32
        )
        live_weight = (slot_index < live_count).astype(jnp.float32)
        accumulate_term = term * live_weight
        start_row = slot_stmts[slot_index] * tile_width
        current = lax.dynamic_slice_in_dim(running_sum, start_row, tile_width, 0)
        running_sum = lax.dynamic_update_slice_in_dim(
            running_sum, current + accumulate_term, start_row, 0
        )
    owned_sums = lax.psum_scatter(running_sum, ("build", "test"), scatter_dimension=0, tiled=True)
    slab_test_gram = jnp.dot(test_slab.T, test_slab, preferred_element_type=jnp.float32)
    slab_build_gram = jnp.dot(build_slab.T, build_slab, preferred_element_type=jnp.float32)
    gram_test = over_copies(slab_test_gram, "test")
    gram_build = over_copies(slab_build_gram, "build")
    gram = gram_test * gram_build
    inverse = spd_inverse(gram)
    solved = jnp.dot(owned_sums, inverse, precision=lax.Precision.HIGHEST, preferred_element_type=jnp.float32)
    return solved[None]


def solution(mesh):
    return jax.shard_map(
        shards,
        mesh=mesh,
        in_specs=(
            P("build", "test", "stmt", None, None, None, None),
            P("build", "test", "stmt", None),
            P("build", "test", "stmt", None),
            P("build", "test", "stmt", None),
            P("build", "test", "stmt"),
            P("test", ("build", "stmt"), None),
            P("build", ("test", "stmt"), None),
        ),
        out_specs=P("stmt", ("build", "test"), None),
        check_vma=False,
    )
```

```python
import functools

import jax
import jax.numpy as jnp
from jax import lax
from jax.experimental import pallas as pl
from jax.experimental.pallas import tpu as pltpu
from jax.sharding import PartitionSpec as P

TILE = 128
SB = 2
MESH = pl.DeviceIdType.MESH
CHUNK = 32


def gather_kernel(n_build, n_test, n_stmt, test_in, build_in, test_out, build_out,
                  test_scr, build_scr, test_send, test_recv, build_send, build_recv):
    b = lax.axis_index("build")
    t = lax.axis_index("test")
    s = lax.axis_index("stmt")
    my_p = b * n_stmt + s
    my_q = t * n_stmt + s

    def test_out_copy(p):
        return pltpu.make_async_remote_copy(
            src_ref=test_in, dst_ref=test_scr.at[my_p], send_sem=test_send.at[p],
            recv_sem=test_recv.at[my_p], device_id=(p // n_stmt, t, p % n_stmt),
            device_id_type=MESH)

    def test_in_copy(p):
        return pltpu.make_async_remote_copy(
            src_ref=test_in, dst_ref=test_scr.at[p], send_sem=test_send.at[p],
            recv_sem=test_recv.at[p], device_id=(p // n_stmt, t, p % n_stmt),
            device_id_type=MESH)

    def build_out_copy(q):
        return pltpu.make_async_remote_copy(
            src_ref=build_in, dst_ref=build_scr.at[my_q], send_sem=build_send.at[q],
            recv_sem=build_recv.at[my_q], device_id=(b, q // n_stmt, q % n_stmt),
            device_id_type=MESH)

    def build_in_copy(q):
        return pltpu.make_async_remote_copy(
            src_ref=build_in, dst_ref=build_scr.at[q], send_sem=build_send.at[q],
            recv_sem=build_recv.at[q], device_id=(b, q // n_stmt, q % n_stmt),
            device_id_type=MESH)

    def start_test(p, carry):
        @pl.when(p != my_p)
        def _():
            test_out_copy(p).start()
        return carry

    def start_build(q, carry):
        @pl.when(q != my_q)
        def _():
            build_out_copy(q).start()
        return carry

    lax.fori_loop(0, n_build * n_stmt, start_test, 0)
    lax.fori_loop(0, n_test * n_stmt, start_build, 0)
    test_scr[pl.ds(my_p, 1)] = test_in[...][None]
    build_scr[pl.ds(my_q, 1)] = build_in[...][None]

    def wait_test(p, carry):
        @pl.when(p != my_p)
        def _():
            test_out_copy(p).wait_send()
            test_in_copy(p).wait_recv()
        return carry

    def wait_build(q, carry):
        @pl.when(q != my_q)
        def _():
            build_out_copy(q).wait_send()
            build_in_copy(q).wait_recv()
        return carry

    lax.fori_loop(0, n_build * n_stmt, wait_test, 0)
    lax.fori_loop(0, n_test * n_stmt, wait_build, 0)
    test_out[...] = test_scr[...]
    build_out[...] = build_scr[...]


def gather_factors(test_rows, build_rows):
    n_build = lax.axis_size("build")
    n_test = lax.axis_size("test")
    n_stmt = lax.axis_size("stmt")
    n_p = n_build * n_stmt
    n_q = n_test * n_stmt
    vmem = pl.BlockSpec(memory_space=pltpu.VMEM)
    test_pieces, build_pieces = pl.pallas_call(
        functools.partial(gather_kernel, n_build, n_test, n_stmt),
        out_shape=(
            jax.ShapeDtypeStruct((n_p, *test_rows.shape), test_rows.dtype),
            jax.ShapeDtypeStruct((n_q, *build_rows.shape), build_rows.dtype),
        ),
        in_specs=[vmem, vmem],
        out_specs=(vmem, vmem),
        scratch_shapes=[
            pltpu.VMEM((n_p, *test_rows.shape), test_rows.dtype),
            pltpu.VMEM((n_q, *build_rows.shape), build_rows.dtype),
            pltpu.SemaphoreType.DMA((n_p,)),
            pltpu.SemaphoreType.DMA((n_p,)),
            pltpu.SemaphoreType.DMA((n_q,)),
            pltpu.SemaphoreType.DMA((n_q,)),
        ],
        compiler_params=pltpu.CompilerParams(has_side_effects=True),
    )(test_rows, build_rows)
    return (
        test_pieces.reshape(-1, test_rows.shape[-1]),
        build_pieces.reshape(-1, build_rows.shape[-1]),
    )


def sweep_kernel(g_ref, out_ref):
    n = g_ref.shape[0]
    out_ref[...] = g_ref[...]
    lane = lax.broadcasted_iota(jnp.int32, (1, n), 1)

    def step(k, row):
        is_k = lane == k
        pivot = jnp.sum(jnp.where(is_k, row, 0.0), axis=1, keepdims=True)
        inv = 1.0 / pivot
        scaled = jnp.where(is_k, 1.0 - inv, row * inv)
        column = jnp.transpose(jnp.broadcast_to(row, (TILE, n)))
        following = jnp.minimum(k + 1, n - 1)
        next_factor = jnp.sum(jnp.where(lane == following, row, 0.0), axis=1, keepdims=True)
        next_row = out_ref[pl.ds(following, 1), :] - next_factor * scaled
        for h in range(n // TILE):
            lanes = slice(h * TILE, (h + 1) * TILE)
            out_ref[:, lanes] = out_ref[:, lanes] - column * scaled[:, lanes]
        out_ref[pl.ds(k, 1), :] = jnp.where(is_k, -inv, row * inv)
        return next_row

    lax.fori_loop(0, n, step, out_ref[0:1, :], unroll=4)
    out_ref[...] = -out_ref[...]


def spd_inverse(gram):
    vmem = pl.BlockSpec(memory_space=pltpu.VMEM)
    return pl.pallas_call(
        sweep_kernel,
        out_shape=jax.ShapeDtypeStruct(gram.shape, jnp.float32),
        in_specs=[vmem],
        out_specs=vmem,
    )(gram)


def mttkrp_kernel(chunk, slot_info, test_ref, build_ref, tile_ref, out_ref, acc_ref):
    q = pl.program_id(0)
    c = pl.program_id(1)
    n_chunks = pl.num_programs(1)

    @pl.when((q == 0) & (c == 0))
    def _():
        out_ref[...] = jnp.zeros_like(out_ref)

    @pl.when(c == 0)
    def _():
        acc_ref[...] = jnp.zeros_like(acc_ref)

    live = q < slot_info[6]

    @pl.when(live)
    def _():
        build_block = build_ref[...].astype(jnp.float32)
        total = acc_ref[...]
        for i in range(chunk):
            test_row = test_ref[i : i + 1, :].astype(jnp.float32)
            khatri_rao = (test_row * build_block).astype(jnp.bfloat16)
            total = total + jnp.dot(tile_ref[i], khatri_rao, preferred_element_type=jnp.float32)
        acc_ref[...] = total

    @pl.when(live & (c == n_chunks - 1))
    def _():
        rows = pl.ds(pl.multiple_of(slot_info[4 + q] * TILE, TILE), TILE)
        out_ref[rows, :] += acc_ref[...]


def local_mttkrp(slot_values, slot_info, test_slab, build_slab):
    slots, width = slot_values.shape[0], slot_values.shape[1]
    rank = test_slab.shape[1]
    per_block = width // CHUNK
    grid_spec = pltpu.PrefetchScalarGridSpec(
        num_scalar_prefetch=1,
        grid=(slots, per_block),
        in_specs=[
            pl.BlockSpec((CHUNK, rank), lambda q, c, info: (info[q] * per_block + c, 0)),
            pl.BlockSpec((width, rank), lambda q, c, info: (info[2 + q], 0)),
            pl.BlockSpec((None, CHUNK, width, width), lambda q, c, info: (q, c, 0, 0)),
        ],
        out_specs=pl.BlockSpec((SB * width, rank), lambda q, c, info: (0, 0)),
        scratch_shapes=[pltpu.VMEM((width, rank), jnp.float32)],
    )
    return pl.pallas_call(
        functools.partial(mttkrp_kernel, CHUNK),
        out_shape=jax.ShapeDtypeStruct((SB * width, rank), jnp.float32),
        grid_spec=grid_spec,
    )(slot_info, test_slab, build_slab, slot_values)


def copy_for_each(x, axis):
    copies = jnp.broadcast_to(x, (lax.axis_size(axis), *x.shape))
    return lax.all_to_all(copies, axis, split_axis=0, concat_axis=0, tiled=True)


def over_copies(x, axis):
    everything = copy_for_each(x, axis)
    return jnp.sum(everything, axis=0)


def shards(tile_values, tile_test, tile_stmt, tile_build, tile_count, test_factor, build_factor):
    test_slab, build_slab = gather_factors(test_factor[0], build_factor[0])
    slot_values = tile_values[0, 0, 0]
    tile_width = slot_values.shape[-1]
    slot_info = jnp.concatenate([
        jnp.clip(tile_test[0, 0, 0], 0, test_slab.shape[0] // tile_width - 1),
        jnp.clip(tile_build[0, 0, 0], 0, build_slab.shape[0] // tile_width - 1),
        jnp.clip(tile_stmt[0, 0, 0], 0, SB - 1),
        tile_count[0, 0, 0][None],
    ]).astype(jnp.int32)
    running_sum = local_mttkrp(slot_values, slot_info, test_slab, build_slab)
    owned_sums = lax.psum_scatter(running_sum, ("build", "test"), scatter_dimension=0, tiled=True)
    slab_test_gram = jnp.dot(test_slab.T, test_slab, preferred_element_type=jnp.float32)
    slab_build_gram = jnp.dot(build_slab.T, build_slab, preferred_element_type=jnp.float32)
    gram_test = over_copies(slab_test_gram, "test")
    gram_build = over_copies(slab_build_gram, "build")
    gram = gram_test * gram_build
    inverse = spd_inverse(gram)
    solved = jnp.dot(owned_sums, inverse, precision=lax.Precision.HIGHEST, preferred_element_type=jnp.float32)
    return solved[None]


def solution(mesh):
    return jax.shard_map(
        shards,
        mesh=mesh,
        in_specs=(
            P("build", "test", "stmt", None, None, None, None),
            P("build", "test", "stmt", None),
            P("build", "test", "stmt", None),
            P("build", "test", "stmt", None),
            P("build", "test", "stmt"),
            P("test", ("build", "stmt"), None),
            P("build", ("test", "stmt"), None),
        ),
        out_specs=P("stmt", ("build", "test"), None),
        check_vma=False,
    )
```

```python
import functools

import jax
import jax.numpy as jnp
from jax import lax
from jax.experimental import pallas as pl
from jax.experimental.pallas import tpu as pltpu
from jax.sharding import PartitionSpec as P

TILE = 128
SB = 2
MESH = pl.DeviceIdType.MESH
CHUNK = 32


def gather_kernel(n_build, n_test, n_stmt, test_in, build_in, test_out, build_out,
                  test_scr, build_scr, test_send, test_recv, build_send, build_recv):
    b = lax.axis_index("build")
    t = lax.axis_index("test")
    s = lax.axis_index("stmt")
    my_p = b * n_stmt + s
    my_q = t * n_stmt + s

    def test_out_copy(p):
        return pltpu.make_async_remote_copy(
            src_ref=test_in, dst_ref=test_scr.at[my_p], send_sem=test_send.at[p],
            recv_sem=test_recv.at[my_p], device_id=(p // n_stmt, t, p % n_stmt),
            device_id_type=MESH)

    def test_in_copy(p):
        return pltpu.make_async_remote_copy(
            src_ref=test_in, dst_ref=test_scr.at[p], send_sem=test_send.at[p],
            recv_sem=test_recv.at[p], device_id=(p // n_stmt, t, p % n_stmt),
            device_id_type=MESH)

    def build_out_copy(q):
        return pltpu.make_async_remote_copy(
            src_ref=build_in, dst_ref=build_scr.at[my_q], send_sem=build_send.at[q],
            recv_sem=build_recv.at[my_q], device_id=(b, q // n_stmt, q % n_stmt),
            device_id_type=MESH)

    def build_in_copy(q):
        return pltpu.make_async_remote_copy(
            src_ref=build_in, dst_ref=build_scr.at[q], send_sem=build_send.at[q],
            recv_sem=build_recv.at[q], device_id=(b, q // n_stmt, q % n_stmt),
            device_id_type=MESH)

    def start_test(p, carry):
        @pl.when(p != my_p)
        def _():
            test_out_copy(p).start()
        return carry

    def start_build(q, carry):
        @pl.when(q != my_q)
        def _():
            build_out_copy(q).start()
        return carry

    lax.fori_loop(0, n_build * n_stmt, start_test, 0)
    lax.fori_loop(0, n_test * n_stmt, start_build, 0)
    test_scr[pl.ds(my_p, 1)] = test_in[...][None]
    build_scr[pl.ds(my_q, 1)] = build_in[...][None]

    def wait_test(p, carry):
        @pl.when(p != my_p)
        def _():
            test_out_copy(p).wait_send()
            test_in_copy(p).wait_recv()
        return carry

    def wait_build(q, carry):
        @pl.when(q != my_q)
        def _():
            build_out_copy(q).wait_send()
            build_in_copy(q).wait_recv()
        return carry

    lax.fori_loop(0, n_build * n_stmt, wait_test, 0)
    lax.fori_loop(0, n_test * n_stmt, wait_build, 0)
    test_out[...] = test_scr[...]
    build_out[...] = build_scr[...]


def gather_factors(test_rows, build_rows):
    n_build = lax.axis_size("build")
    n_test = lax.axis_size("test")
    n_stmt = lax.axis_size("stmt")
    n_p = n_build * n_stmt
    n_q = n_test * n_stmt
    vmem = pl.BlockSpec(memory_space=pltpu.VMEM)
    test_pieces, build_pieces = pl.pallas_call(
        functools.partial(gather_kernel, n_build, n_test, n_stmt),
        out_shape=(
            jax.ShapeDtypeStruct((n_p, *test_rows.shape), test_rows.dtype),
            jax.ShapeDtypeStruct((n_q, *build_rows.shape), build_rows.dtype),
        ),
        in_specs=[vmem, vmem],
        out_specs=(vmem, vmem),
        scratch_shapes=[
            pltpu.VMEM((n_p, *test_rows.shape), test_rows.dtype),
            pltpu.VMEM((n_q, *build_rows.shape), build_rows.dtype),
            pltpu.SemaphoreType.DMA((n_p,)),
            pltpu.SemaphoreType.DMA((n_p,)),
            pltpu.SemaphoreType.DMA((n_q,)),
            pltpu.SemaphoreType.DMA((n_q,)),
        ],
        compiler_params=pltpu.CompilerParams(has_side_effects=True),
    )(test_rows, build_rows)
    return (
        test_pieces.reshape(-1, test_rows.shape[-1]),
        build_pieces.reshape(-1, build_rows.shape[-1]),
    )


def sweep_in_place(a_ref):
    n = a_ref.shape[0]
    lane = lax.broadcasted_iota(jnp.int32, (1, n), 1)

    def step(k, row):
        is_k = lane == k
        pivot = jnp.sum(jnp.where(is_k, row, 0.0), axis=1, keepdims=True)
        inv = 1.0 / pivot
        scaled = jnp.where(is_k, 1.0 - inv, row * inv)
        column = jnp.transpose(jnp.broadcast_to(row, (TILE, n)))
        following = jnp.minimum(k + 1, n - 1)
        next_factor = jnp.sum(jnp.where(lane == following, row, 0.0), axis=1, keepdims=True)
        next_row = a_ref[pl.ds(following, 1), :] - next_factor * scaled
        for h in range(n // TILE):
            lanes = slice(h * TILE, (h + 1) * TILE)
            a_ref[:, lanes] = a_ref[:, lanes] - column * scaled[:, lanes]
        a_ref[pl.ds(k, 1), :] = jnp.where(is_k, -inv, row * inv)
        return next_row

    lax.fori_loop(0, n, step, a_ref[0:1, :], unroll=4)
    a_ref[...] = -a_ref[...]


def tail_kernel(n_build, n_test, part_ref, test_gram_ref, build_gram_ref, owned_ref, inv_ref,
                rs_buf, test_buf, build_buf, product_buf, gram_buf,
                rs_send, rs_recv, test_send, test_recv, build_send, build_recv,
                gram_send, gram_recv):
    b = lax.axis_index("build")
    t = lax.axis_index("test")
    s = lax.axis_index("stmt")
    n_rs = n_build * n_test
    rs_rows = part_ref.shape[0] // n_rs
    g_rows = test_gram_ref.shape[0] // n_test
    me = b * n_test + t

    def rs_copy(m, dst_slot):
        return pltpu.make_async_remote_copy(
            src_ref=part_ref.at[pl.ds(m * rs_rows, rs_rows)], dst_ref=rs_buf.at[dst_slot],
            send_sem=rs_send.at[m], recv_sem=rs_recv.at[dst_slot],
            device_id=(m // n_test, m % n_test, s), device_id_type=MESH)

    def test_copy(j, dst_slot):
        return pltpu.make_async_remote_copy(
            src_ref=test_gram_ref.at[pl.ds(j * g_rows, g_rows)], dst_ref=test_buf.at[dst_slot],
            send_sem=test_send.at[j], recv_sem=test_recv.at[dst_slot],
            device_id=(b, j, s), device_id_type=MESH)

    def build_copy(j, dst_slot):
        return pltpu.make_async_remote_copy(
            src_ref=build_gram_ref, dst_ref=build_buf.at[dst_slot],
            send_sem=build_send.at[j], recv_sem=build_recv.at[dst_slot],
            device_id=(j, t, s), device_id_type=MESH)

    def gram_copy(j, dst_slot):
        return pltpu.make_async_remote_copy(
            src_ref=product_buf, dst_ref=gram_buf.at[dst_slot],
            send_sem=gram_send.at[j], recv_sem=gram_recv.at[dst_slot],
            device_id=(b, j, s), device_id_type=MESH)

    for j in range(n_build):
        @pl.when(j != b)
        def _():
            build_copy(j, b).start()
    for j in range(n_test):
        @pl.when(j != t)
        def _():
            test_copy(j, t).start()
    for m in range(n_rs):
        @pl.when(m != me)
        def _():
            rs_copy(m, me).start()
    build_buf[pl.ds(b, 1)] = build_gram_ref[...][None]
    test_buf[pl.ds(t, 1)] = test_gram_ref[pl.ds(pl.multiple_of(t * g_rows, g_rows), g_rows), :][None]
    rs_buf[pl.ds(me, 1)] = part_ref[pl.ds(pl.multiple_of(me * rs_rows, rs_rows), rs_rows), :][None]

    for j in range(n_build):
        @pl.when(j != b)
        def _():
            build_copy(j, b).wait_send()
            build_copy(j, j).wait_recv()
    for j in range(n_test):
        @pl.when(j != t)
        def _():
            test_copy(j, t).wait_send()
            test_copy(j, j).wait_recv()

    my_rows = pl.ds(pl.multiple_of(t * g_rows, g_rows), g_rows)
    test_rows = test_buf[0]
    for j in range(1, n_test):
        test_rows = test_rows + test_buf[j]
    build_rows = build_buf[0, my_rows, :]
    for j in range(1, n_build):
        build_rows = build_rows + build_buf[j, my_rows, :]
    product_buf[...] = test_rows * build_rows

    for j in range(n_test):
        @pl.when(j != t)
        def _():
            gram_copy(j, t).start()
    gram_buf[pl.ds(t, 1)] = product_buf[...][None]
    for j in range(n_test):
        @pl.when(j != t)
        def _():
            gram_copy(j, t).wait_send()
            gram_copy(j, j).wait_recv()
    for j in range(n_test):
        inv_ref[j * g_rows:(j + 1) * g_rows, :] = gram_buf[j]

    sweep_in_place(inv_ref)

    for m in range(n_rs):
        @pl.when(m != me)
        def _():
            rs_copy(m, me).wait_send()
            rs_copy(m, m).wait_recv()
    owned = rs_buf[0]
    for m in range(1, n_rs):
        owned = owned + rs_buf[m]
    owned_ref[...] = owned


def exchange_and_invert(partial, test_gram, build_gram):
    n_build = lax.axis_size("build")
    n_test = lax.axis_size("test")
    n_rs = n_build * n_test
    rows, rank = partial.shape
    rs_rows = rows // n_rs
    g_rows = rank // n_test
    vmem = pl.BlockSpec(memory_space=pltpu.VMEM)
    f32 = jnp.float32
    return pl.pallas_call(
        functools.partial(tail_kernel, n_build, n_test),
        out_shape=(
            jax.ShapeDtypeStruct((rs_rows, rank), f32),
            jax.ShapeDtypeStruct((rank, rank), f32),
        ),
        in_specs=[vmem, vmem, vmem],
        out_specs=(vmem, vmem),
        scratch_shapes=[
            pltpu.VMEM((n_rs, rs_rows, rank), f32),
            pltpu.VMEM((n_test, g_rows, rank), f32),
            pltpu.VMEM((n_build, rank, rank), f32),
            pltpu.VMEM((g_rows, rank), f32),
            pltpu.VMEM((n_test, g_rows, rank), f32),
            pltpu.SemaphoreType.DMA((n_rs,)),
            pltpu.SemaphoreType.DMA((n_rs,)),
            pltpu.SemaphoreType.DMA((n_test,)),
            pltpu.SemaphoreType.DMA((n_test,)),
            pltpu.SemaphoreType.DMA((n_build,)),
            pltpu.SemaphoreType.DMA((n_build,)),
            pltpu.SemaphoreType.DMA((n_test,)),
            pltpu.SemaphoreType.DMA((n_test,)),
        ],
        compiler_params=pltpu.CompilerParams(has_side_effects=True),
    )(partial, test_gram, build_gram)


def mttkrp_kernel(chunk, slot_info, test_ref, build_ref, tile_ref, out_ref, acc_ref):
    q = pl.program_id(0)
    c = pl.program_id(1)
    n_chunks = pl.num_programs(1)

    @pl.when((q == 0) & (c == 0))
    def _():
        out_ref[...] = jnp.zeros_like(out_ref)

    @pl.when(c == 0)
    def _():
        acc_ref[...] = jnp.zeros_like(acc_ref)

    live = q < slot_info[6]

    @pl.when(live)
    def _():
        build_block = build_ref[...].astype(jnp.float32)
        total = acc_ref[...]
        for i in range(chunk):
            test_row = test_ref[i : i + 1, :].astype(jnp.float32)
            khatri_rao = (test_row * build_block).astype(jnp.bfloat16)
            total = total + jnp.dot(tile_ref[i], khatri_rao, preferred_element_type=jnp.float32)
        acc_ref[...] = total

    @pl.when(live & (c == n_chunks - 1))
    def _():
        rows = pl.ds(pl.multiple_of(slot_info[4 + q] * TILE, TILE), TILE)
        out_ref[rows, :] += acc_ref[...]


def local_mttkrp(slot_values, slot_info, test_slab, build_slab):
    slots, width = slot_values.shape[0], slot_values.shape[1]
    rank = test_slab.shape[1]
    per_block = width // CHUNK
    grid_spec = pltpu.PrefetchScalarGridSpec(
        num_scalar_prefetch=1,
        grid=(slots, per_block),
        in_specs=[
            pl.BlockSpec((CHUNK, rank), lambda q, c, info: (info[q] * per_block + c, 0)),
            pl.BlockSpec((width, rank), lambda q, c, info: (info[2 + q], 0)),
            pl.BlockSpec((None, CHUNK, width, width), lambda q, c, info: (q, c, 0, 0)),
        ],
        out_specs=pl.BlockSpec((SB * width, rank), lambda q, c, info: (0, 0)),
        scratch_shapes=[pltpu.VMEM((width, rank), jnp.float32)],
    )
    return pl.pallas_call(
        functools.partial(mttkrp_kernel, CHUNK),
        out_shape=jax.ShapeDtypeStruct((SB * width, rank), jnp.float32),
        grid_spec=grid_spec,
    )(slot_info, test_slab, build_slab, slot_values)


def shards(tile_values, tile_test, tile_stmt, tile_build, tile_count, test_factor, build_factor):
    test_slab, build_slab = gather_factors(test_factor[0], build_factor[0])
    slot_values = tile_values[0, 0, 0]
    tile_width = slot_values.shape[-1]
    slot_info = jnp.concatenate([
        jnp.clip(tile_test[0, 0, 0], 0, test_slab.shape[0] // tile_width - 1),
        jnp.clip(tile_build[0, 0, 0], 0, build_slab.shape[0] // tile_width - 1),
        jnp.clip(tile_stmt[0, 0, 0], 0, SB - 1),
        tile_count[0, 0, 0][None],
    ]).astype(jnp.int32)
    running_sum = local_mttkrp(slot_values, slot_info, test_slab, build_slab)
    slab_test_gram = jnp.dot(test_slab.T, test_slab, preferred_element_type=jnp.float32)
    slab_build_gram = jnp.dot(build_slab.T, build_slab, preferred_element_type=jnp.float32)
    owned_sums, inverse = exchange_and_invert(running_sum, slab_test_gram, slab_build_gram)
    solved = jnp.dot(owned_sums, inverse, precision=lax.Precision.HIGHEST, preferred_element_type=jnp.float32)
    return solved[None]


def solution(mesh):
    return jax.shard_map(
        shards,
        mesh=mesh,
        in_specs=(
            P("build", "test", "stmt", None, None, None, None),
            P("build", "test", "stmt", None),
            P("build", "test", "stmt", None),
            P("build", "test", "stmt", None),
            P("build", "test", "stmt"),
            P("test", ("build", "stmt"), None),
            P("build", ("test", "stmt"), None),
        ),
        out_specs=P("stmt", ("build", "test"), None),
        check_vma=False,
    )
```

```python
import functools

import jax
import jax.numpy as jnp
from jax import lax
from jax.experimental import pallas as pl
from jax.experimental.pallas import tpu as pltpu
from jax.sharding import PartitionSpec as P

TILE = 128
SB = 2
MESH = pl.DeviceIdType.MESH
CHUNK = 32


def gather_kernel(n_build, n_test, n_stmt, test_in, build_in, test_out, build_out,
                  test_scr, build_scr, test_send, test_recv, build_send, build_recv):
    b = lax.axis_index("build")
    t = lax.axis_index("test")
    s = lax.axis_index("stmt")
    my_p = b * n_stmt + s
    my_q = t * n_stmt + s

    def test_out_copy(p):
        return pltpu.make_async_remote_copy(
            src_ref=test_in, dst_ref=test_scr.at[my_p], send_sem=test_send.at[p],
            recv_sem=test_recv.at[my_p], device_id=(p // n_stmt, t, p % n_stmt),
            device_id_type=MESH)

    def test_in_copy(p):
        return pltpu.make_async_remote_copy(
            src_ref=test_in, dst_ref=test_scr.at[p], send_sem=test_send.at[p],
            recv_sem=test_recv.at[p], device_id=(p // n_stmt, t, p % n_stmt),
            device_id_type=MESH)

    def build_out_copy(q):
        return pltpu.make_async_remote_copy(
            src_ref=build_in, dst_ref=build_scr.at[my_q], send_sem=build_send.at[q],
            recv_sem=build_recv.at[my_q], device_id=(b, q // n_stmt, q % n_stmt),
            device_id_type=MESH)

    def build_in_copy(q):
        return pltpu.make_async_remote_copy(
            src_ref=build_in, dst_ref=build_scr.at[q], send_sem=build_send.at[q],
            recv_sem=build_recv.at[q], device_id=(b, q // n_stmt, q % n_stmt),
            device_id_type=MESH)

    barrier = pltpu.get_barrier_semaphore()

    def greet_test(p, carry):
        @pl.when(p != my_p)
        def _():
            pl.semaphore_signal(barrier, 1, device_id=(p // n_stmt, t, p % n_stmt), device_id_type=MESH)
        return carry

    def greet_build(q, carry):
        @pl.when(q != my_q)
        def _():
            pl.semaphore_signal(barrier, 1, device_id=(b, q // n_stmt, q % n_stmt), device_id_type=MESH)
        return carry

    lax.fori_loop(0, n_build * n_stmt, greet_test, 0)
    lax.fori_loop(0, n_test * n_stmt, greet_build, 0)
    pl.semaphore_wait(barrier, n_build * n_stmt + n_test * n_stmt - 2)

    def start_test(p, carry):
        @pl.when(p != my_p)
        def _():
            test_out_copy(p).start()
        return carry

    def start_build(q, carry):
        @pl.when(q != my_q)
        def _():
            build_out_copy(q).start()
        return carry

    lax.fori_loop(0, n_build * n_stmt, start_test, 0)
    lax.fori_loop(0, n_test * n_stmt, start_build, 0)
    test_scr[pl.ds(my_p, 1)] = test_in[...][None]
    build_scr[pl.ds(my_q, 1)] = build_in[...][None]

    def wait_test(p, carry):
        @pl.when(p != my_p)
        def _():
            test_out_copy(p).wait_send()
            test_in_copy(p).wait_recv()
        return carry

    def wait_build(q, carry):
        @pl.when(q != my_q)
        def _():
            build_out_copy(q).wait_send()
            build_in_copy(q).wait_recv()
        return carry

    lax.fori_loop(0, n_build * n_stmt, wait_test, 0)
    lax.fori_loop(0, n_test * n_stmt, wait_build, 0)
    test_out[...] = test_scr[...]
    build_out[...] = build_scr[...]


def gather_factors(test_rows, build_rows):
    n_build = lax.axis_size("build")
    n_test = lax.axis_size("test")
    n_stmt = lax.axis_size("stmt")
    n_p = n_build * n_stmt
    n_q = n_test * n_stmt
    vmem = pl.BlockSpec(memory_space=pltpu.VMEM)
    test_pieces, build_pieces = pl.pallas_call(
        functools.partial(gather_kernel, n_build, n_test, n_stmt),
        out_shape=(
            jax.ShapeDtypeStruct((n_p, *test_rows.shape), test_rows.dtype),
            jax.ShapeDtypeStruct((n_q, *build_rows.shape), build_rows.dtype),
        ),
        in_specs=[vmem, vmem],
        out_specs=(vmem, vmem),
        scratch_shapes=[
            pltpu.VMEM((n_p, *test_rows.shape), test_rows.dtype),
            pltpu.VMEM((n_q, *build_rows.shape), build_rows.dtype),
            pltpu.SemaphoreType.DMA((n_p,)),
            pltpu.SemaphoreType.DMA((n_p,)),
            pltpu.SemaphoreType.DMA((n_q,)),
            pltpu.SemaphoreType.DMA((n_q,)),
        ],
        compiler_params=pltpu.CompilerParams(has_side_effects=True, collective_id=0),
    )(test_rows, build_rows)
    return (
        test_pieces.reshape(-1, test_rows.shape[-1]),
        build_pieces.reshape(-1, build_rows.shape[-1]),
    )


def sweep_in_place(a_ref):
    n = a_ref.shape[0]
    lane = lax.broadcasted_iota(jnp.int32, (1, n), 1)

    def step(k, row):
        is_k = lane == k
        pivot = jnp.sum(jnp.where(is_k, row, 0.0), axis=1, keepdims=True)
        inv = 1.0 / pivot
        scaled = jnp.where(is_k, 1.0 - inv, row * inv)
        column = jnp.transpose(jnp.broadcast_to(row, (TILE, n)))
        following = jnp.minimum(k + 1, n - 1)
        next_factor = jnp.sum(jnp.where(lane == following, row, 0.0), axis=1, keepdims=True)
        next_row = a_ref[pl.ds(following, 1), :] - next_factor * scaled
        for h in range(n // TILE):
            lanes = slice(h * TILE, (h + 1) * TILE)
            a_ref[:, lanes] = a_ref[:, lanes] - column * scaled[:, lanes]
        a_ref[pl.ds(k, 1), :] = jnp.where(is_k, -inv, row * inv)
        return next_row

    lax.fori_loop(0, n, step, a_ref[0:1, :], unroll=4)
    a_ref[...] = -a_ref[...]


def tail_kernel(n_build, n_test, part_ref, test_gram_ref, build_gram_ref, owned_ref, inv_ref,
                rs_buf, test_buf, build_buf, product_buf, gram_buf,
                rs_send, rs_recv, test_send, test_recv, build_send, build_recv,
                gram_send, gram_recv):
    b = lax.axis_index("build")
    t = lax.axis_index("test")
    s = lax.axis_index("stmt")
    n_rs = n_build * n_test
    rs_rows = part_ref.shape[0] // n_rs
    g_rows = test_gram_ref.shape[0] // n_test
    me = b * n_test + t

    def rs_copy(m, dst_slot):
        return pltpu.make_async_remote_copy(
            src_ref=part_ref.at[pl.ds(m * rs_rows, rs_rows)], dst_ref=rs_buf.at[dst_slot],
            send_sem=rs_send.at[m], recv_sem=rs_recv.at[dst_slot],
            device_id=(m // n_test, m % n_test, s), device_id_type=MESH)

    def test_copy(j, dst_slot):
        return pltpu.make_async_remote_copy(
            src_ref=test_gram_ref.at[pl.ds(j * g_rows, g_rows)], dst_ref=test_buf.at[dst_slot],
            send_sem=test_send.at[j], recv_sem=test_recv.at[dst_slot],
            device_id=(b, j, s), device_id_type=MESH)

    def build_copy(j, dst_slot):
        return pltpu.make_async_remote_copy(
            src_ref=build_gram_ref, dst_ref=build_buf.at[dst_slot],
            send_sem=build_send.at[j], recv_sem=build_recv.at[dst_slot],
            device_id=(j, t, s), device_id_type=MESH)

    def gram_copy(j, dst_slot):
        return pltpu.make_async_remote_copy(
            src_ref=product_buf, dst_ref=gram_buf.at[dst_slot],
            send_sem=gram_send.at[j], recv_sem=gram_recv.at[dst_slot],
            device_id=(b, j, s), device_id_type=MESH)

    barrier = pltpu.get_barrier_semaphore()
    for m in range(n_rs):
        @pl.when(m != me)
        def _():
            pl.semaphore_signal(barrier, 1, device_id=(m // n_test, m % n_test, s), device_id_type=MESH)
    pl.semaphore_wait(barrier, n_rs - 1)

    for j in range(n_build):
        @pl.when(j != b)
        def _():
            build_copy(j, b).start()
    for j in range(n_test):
        @pl.when(j != t)
        def _():
            test_copy(j, t).start()
    for m in range(n_rs):
        @pl.when(m != me)
        def _():
            rs_copy(m, me).start()
    build_buf[pl.ds(b, 1)] = build_gram_ref[...][None]
    test_buf[pl.ds(t, 1)] = test_gram_ref[pl.ds(pl.multiple_of(t * g_rows, g_rows), g_rows), :][None]
    rs_buf[pl.ds(me, 1)] = part_ref[pl.ds(pl.multiple_of(me * rs_rows, rs_rows), rs_rows), :][None]

    for j in range(n_build):
        @pl.when(j != b)
        def _():
            build_copy(j, b).wait_send()
            build_copy(j, j).wait_recv()
    for j in range(n_test):
        @pl.when(j != t)
        def _():
            test_copy(j, t).wait_send()
            test_copy(j, j).wait_recv()

    my_rows = pl.ds(pl.multiple_of(t * g_rows, g_rows), g_rows)
    test_rows = test_buf[0]
    for j in range(1, n_test):
        test_rows = test_rows + test_buf[j]
    build_rows = build_buf[0, my_rows, :]
    for j in range(1, n_build):
        build_rows = build_rows + build_buf[j, my_rows, :]
    product_buf[...] = test_rows * build_rows

    for j in range(n_test):
        @pl.when(j != t)
        def _():
            gram_copy(j, t).start()
    gram_buf[pl.ds(t, 1)] = product_buf[...][None]
    for j in range(n_test):
        @pl.when(j != t)
        def _():
            gram_copy(j, t).wait_send()
            gram_copy(j, j).wait_recv()
    for j in range(n_test):
        inv_ref[j * g_rows:(j + 1) * g_rows, :] = gram_buf[j]

    sweep_in_place(inv_ref)

    for m in range(n_rs):
        @pl.when(m != me)
        def _():
            rs_copy(m, me).wait_send()
            rs_copy(m, m).wait_recv()
    owned = rs_buf[0]
    for m in range(1, n_rs):
        owned = owned + rs_buf[m]
    owned_ref[...] = owned


def exchange_and_invert(partial, test_gram, build_gram):
    n_build = lax.axis_size("build")
    n_test = lax.axis_size("test")
    n_rs = n_build * n_test
    rows, rank = partial.shape
    rs_rows = rows // n_rs
    g_rows = rank // n_test
    vmem = pl.BlockSpec(memory_space=pltpu.VMEM)
    f32 = jnp.float32
    return pl.pallas_call(
        functools.partial(tail_kernel, n_build, n_test),
        out_shape=(
            jax.ShapeDtypeStruct((rs_rows, rank), f32),
            jax.ShapeDtypeStruct((rank, rank), f32),
        ),
        in_specs=[vmem, vmem, vmem],
        out_specs=(vmem, vmem),
        scratch_shapes=[
            pltpu.VMEM((n_rs, rs_rows, rank), f32),
            pltpu.VMEM((n_test, g_rows, rank), f32),
            pltpu.VMEM((n_build, rank, rank), f32),
            pltpu.VMEM((g_rows, rank), f32),
            pltpu.VMEM((n_test, g_rows, rank), f32),
            pltpu.SemaphoreType.DMA((n_rs,)),
            pltpu.SemaphoreType.DMA((n_rs,)),
            pltpu.SemaphoreType.DMA((n_test,)),
            pltpu.SemaphoreType.DMA((n_test,)),
            pltpu.SemaphoreType.DMA((n_build,)),
            pltpu.SemaphoreType.DMA((n_build,)),
            pltpu.SemaphoreType.DMA((n_test,)),
            pltpu.SemaphoreType.DMA((n_test,)),
        ],
        compiler_params=pltpu.CompilerParams(has_side_effects=True, collective_id=1),
    )(partial, test_gram, build_gram)


def mttkrp_kernel(chunk, slot_info, test_ref, build_ref, tile_ref, out_ref, acc_ref):
    q = pl.program_id(0)
    c = pl.program_id(1)
    n_chunks = pl.num_programs(1)

    @pl.when((q == 0) & (c == 0))
    def _():
        out_ref[...] = jnp.zeros_like(out_ref)

    @pl.when(c == 0)
    def _():
        acc_ref[...] = jnp.zeros_like(acc_ref)

    live = q < slot_info[6]

    @pl.when(live)
    def _():
        build_block = build_ref[...].astype(jnp.float32)
        total = acc_ref[...]
        for i in range(chunk):
            test_row = test_ref[i : i + 1, :].astype(jnp.float32)
            khatri_rao = (test_row * build_block).astype(jnp.bfloat16)
            total = total + jnp.dot(tile_ref[i], khatri_rao, preferred_element_type=jnp.float32)
        acc_ref[...] = total

    @pl.when(live & (c == n_chunks - 1))
    def _():
        rows = pl.ds(pl.multiple_of(slot_info[4 + q] * TILE, TILE), TILE)
        out_ref[rows, :] += acc_ref[...]


def local_mttkrp(slot_values, slot_info, test_slab, build_slab):
    slots, width = slot_values.shape[0], slot_values.shape[1]
    rank = test_slab.shape[1]
    per_block = width // CHUNK
    grid_spec = pltpu.PrefetchScalarGridSpec(
        num_scalar_prefetch=1,
        grid=(slots, per_block),
        in_specs=[
            pl.BlockSpec((CHUNK, rank), lambda q, c, info: (info[q] * per_block + c, 0)),
            pl.BlockSpec((width, rank), lambda q, c, info: (info[2 + q], 0)),
            pl.BlockSpec((None, CHUNK, width, width), lambda q, c, info: (q, c, 0, 0)),
        ],
        out_specs=pl.BlockSpec((SB * width, rank), lambda q, c, info: (0, 0)),
        scratch_shapes=[pltpu.VMEM((width, rank), jnp.float32)],
    )
    return pl.pallas_call(
        functools.partial(mttkrp_kernel, CHUNK),
        out_shape=jax.ShapeDtypeStruct((SB * width, rank), jnp.float32),
        grid_spec=grid_spec,
    )(slot_info, test_slab, build_slab, slot_values)


def shards(tile_values, tile_test, tile_stmt, tile_build, tile_count, test_factor, build_factor):
    test_slab, build_slab = gather_factors(test_factor[0], build_factor[0])
    slot_values = tile_values[0, 0, 0]
    tile_width = slot_values.shape[-1]
    slot_info = jnp.concatenate([
        jnp.clip(tile_test[0, 0, 0], 0, test_slab.shape[0] // tile_width - 1),
        jnp.clip(tile_build[0, 0, 0], 0, build_slab.shape[0] // tile_width - 1),
        jnp.clip(tile_stmt[0, 0, 0], 0, SB - 1),
        tile_count[0, 0, 0][None],
    ]).astype(jnp.int32)
    running_sum = local_mttkrp(slot_values, slot_info, test_slab, build_slab)
    slab_test_gram = jnp.dot(test_slab.T, test_slab, preferred_element_type=jnp.float32)
    slab_build_gram = jnp.dot(build_slab.T, build_slab, preferred_element_type=jnp.float32)
    owned_sums, inverse = exchange_and_invert(running_sum, slab_test_gram, slab_build_gram)
    solved = jnp.dot(owned_sums, inverse, precision=lax.Precision.HIGHEST, preferred_element_type=jnp.float32)
    return solved[None]


def solution(mesh):
    return jax.shard_map(
        shards,
        mesh=mesh,
        in_specs=(
            P("build", "test", "stmt", None, None, None, None),
            P("build", "test", "stmt", None),
            P("build", "test", "stmt", None),
            P("build", "test", "stmt", None),
            P("build", "test", "stmt"),
            P("test", ("build", "stmt"), None),
            P("build", ("test", "stmt"), None),
        ),
        out_specs=P("stmt", ("build", "test"), None),
        check_vma=False,
    )
```

```python
import functools

import jax
import jax.numpy as jnp
from jax import lax
from jax.experimental import pallas as pl
from jax.experimental.pallas import tpu as pltpu
from jax.sharding import PartitionSpec as P

TILE = 128
SB = 2
MESH = pl.DeviceIdType.MESH
CHUNK = 32


def gather_kernel(n_build, n_test, n_stmt, test_in, build_in, test_out, build_out,
                  test_scr, build_scr, local_sem, t1_send, t1_recv, b1_send, b1_recv,
                  t2_send, t2_recv, b2_send, b2_recv):
    b = lax.axis_index("build")
    t = lax.axis_index("test")
    s = lax.axis_index("stmt")

    barrier = pltpu.get_barrier_semaphore()
    for j in range(n_stmt):
        @pl.when(j != s)
        def _():
            pl.semaphore_signal(barrier, 1, device_id=(b, t, j), device_id_type=MESH)
    for j in range(n_build):
        @pl.when(j != b)
        def _():
            pl.semaphore_signal(barrier, 1, device_id=(j, t, s), device_id_type=MESH)
    for j in range(n_test):
        @pl.when(j != t)
        def _():
            pl.semaphore_signal(barrier, 1, device_id=(b, j, s), device_id_type=MESH)
    pl.semaphore_wait(barrier, n_stmt + n_build + n_test - 3)

    def t1(j, slot):
        return pltpu.make_async_remote_copy(
            src_ref=test_in, dst_ref=test_scr.at[b, slot], send_sem=t1_send.at[j],
            recv_sem=t1_recv.at[slot], device_id=(b, t, j), device_id_type=MESH)

    def b1(j, slot):
        return pltpu.make_async_remote_copy(
            src_ref=build_in, dst_ref=build_scr.at[t, slot], send_sem=b1_send.at[j],
            recv_sem=b1_recv.at[slot], device_id=(b, t, j), device_id_type=MESH)

    def t2(j, slot):
        return pltpu.make_async_remote_copy(
            src_ref=test_scr.at[b], dst_ref=test_scr.at[slot], send_sem=t2_send.at[j],
            recv_sem=t2_recv.at[slot], device_id=(j, t, s), device_id_type=MESH)

    def b2(j, slot):
        return pltpu.make_async_remote_copy(
            src_ref=build_scr.at[t], dst_ref=build_scr.at[slot], send_sem=b2_send.at[j],
            recv_sem=b2_recv.at[slot], device_id=(b, j, s), device_id_type=MESH)

    for j in range(n_stmt):
        @pl.when(j != s)
        def _():
            t1(j, s).start()
            b1(j, s).start()
    own_test = pltpu.make_async_copy(test_in, test_scr.at[b, s], local_sem.at[0])
    own_build = pltpu.make_async_copy(build_in, build_scr.at[t, s], local_sem.at[1])
    own_test.start()
    own_build.start()
    own_test.wait()
    own_build.wait()
    for j in range(n_stmt):
        @pl.when(j != s)
        def _():
            t1(j, s).wait_send()
            b1(j, s).wait_send()
            t1(j, j).wait_recv()
            b1(j, j).wait_recv()

    for j in range(n_build):
        @pl.when(j != b)
        def _():
            t2(j, b).start()
    for j in range(n_test):
        @pl.when(j != t)
        def _():
            b2(j, t).start()
    for j in range(n_build):
        @pl.when(j != b)
        def _():
            t2(j, b).wait_send()
            t2(j, j).wait_recv()
    for j in range(n_test):
        @pl.when(j != t)
        def _():
            b2(j, t).wait_send()
            b2(j, j).wait_recv()
    test_out[...] = test_scr[...]
    build_out[...] = build_scr[...]


def gather_factors(test_rows, build_rows):
    n_build = lax.axis_size("build")
    n_test = lax.axis_size("test")
    n_stmt = lax.axis_size("stmt")
    vmem = pl.BlockSpec(memory_space=pltpu.VMEM)
    test_shape = (n_build, n_stmt, *test_rows.shape)
    build_shape = (n_test, n_stmt, *build_rows.shape)
    dma = pltpu.SemaphoreType.DMA
    test_pieces, build_pieces = pl.pallas_call(
        functools.partial(gather_kernel, n_build, n_test, n_stmt),
        out_shape=(
            jax.ShapeDtypeStruct(test_shape, test_rows.dtype),
            jax.ShapeDtypeStruct(build_shape, build_rows.dtype),
        ),
        in_specs=[vmem, vmem],
        out_specs=(vmem, vmem),
        scratch_shapes=[
            pltpu.VMEM(test_shape, test_rows.dtype),
            pltpu.VMEM(build_shape, build_rows.dtype),
            dma((2,)),
            dma((n_stmt,)), dma((n_stmt,)), dma((n_stmt,)), dma((n_stmt,)),
            dma((n_build,)), dma((n_build,)), dma((n_test,)), dma((n_test,)),
        ],
        compiler_params=pltpu.CompilerParams(has_side_effects=True, collective_id=0),
    )(test_rows, build_rows)
    return (
        test_pieces.reshape(-1, test_rows.shape[-1]),
        build_pieces.reshape(-1, build_rows.shape[-1]),
    )


def sweep_in_place(a_ref):
    n = a_ref.shape[0]
    lane = lax.broadcasted_iota(jnp.int32, (1, n), 1)

    def step(k, row):
        is_k = lane == k
        pivot = jnp.sum(jnp.where(is_k, row, 0.0), axis=1, keepdims=True)
        inv = 1.0 / pivot
        scaled = jnp.where(is_k, 1.0 - inv, row * inv)
        column = jnp.transpose(jnp.broadcast_to(row, (TILE, n)))
        following = jnp.minimum(k + 1, n - 1)
        next_factor = jnp.sum(jnp.where(lane == following, row, 0.0), axis=1, keepdims=True)
        next_row = a_ref[pl.ds(following, 1), :] - next_factor * scaled
        for h in range(n // TILE):
            lanes = slice(h * TILE, (h + 1) * TILE)
            a_ref[:, lanes] = a_ref[:, lanes] - column * scaled[:, lanes]
        a_ref[pl.ds(k, 1), :] = jnp.where(is_k, -inv, row * inv)
        return next_row

    lax.fori_loop(0, n, step, a_ref[0:1, :], unroll=4)
    a_ref[...] = -a_ref[...]


def tail_kernel(n_build, n_test, part_ref, test_gram_ref, build_gram_ref, owned_ref, inv_ref,
                rs_buf, test_buf, build_buf, product_buf, gram_buf,
                rs_send, rs_recv, test_send, test_recv, build_send, build_recv,
                gram_send, gram_recv):
    b = lax.axis_index("build")
    t = lax.axis_index("test")
    s = lax.axis_index("stmt")
    n_rs = n_build * n_test
    rs_rows = part_ref.shape[0] // n_rs
    g_rows = test_gram_ref.shape[0] // n_test
    me = b * n_test + t

    def rs_copy(m, dst_slot):
        return pltpu.make_async_remote_copy(
            src_ref=part_ref.at[pl.ds(m * rs_rows, rs_rows)], dst_ref=rs_buf.at[dst_slot],
            send_sem=rs_send.at[m], recv_sem=rs_recv.at[dst_slot],
            device_id=(m // n_test, m % n_test, s), device_id_type=MESH)

    def test_copy(j, dst_slot):
        return pltpu.make_async_remote_copy(
            src_ref=test_gram_ref.at[pl.ds(j * g_rows, g_rows)], dst_ref=test_buf.at[dst_slot],
            send_sem=test_send.at[j], recv_sem=test_recv.at[dst_slot],
            device_id=(b, j, s), device_id_type=MESH)

    def build_copy(j, dst_slot):
        return pltpu.make_async_remote_copy(
            src_ref=build_gram_ref, dst_ref=build_buf.at[dst_slot],
            send_sem=build_send.at[j], recv_sem=build_recv.at[dst_slot],
            device_id=(j, t, s), device_id_type=MESH)

    def gram_copy(j, dst_slot):
        return pltpu.make_async_remote_copy(
            src_ref=product_buf, dst_ref=gram_buf.at[dst_slot],
            send_sem=gram_send.at[j], recv_sem=gram_recv.at[dst_slot],
            device_id=(b, j, s), device_id_type=MESH)

    barrier = pltpu.get_barrier_semaphore()
    for m in range(n_rs):
        @pl.when(m != me)
        def _():
            pl.semaphore_signal(barrier, 1, device_id=(m // n_test, m % n_test, s), device_id_type=MESH)
    pl.semaphore_wait(barrier, n_rs - 1)

    for j in range(n_build):
        @pl.when(j != b)
        def _():
            build_copy(j, b).start()
    for j in range(n_test):
        @pl.when(j != t)
        def _():
            test_copy(j, t).start()
    for m in range(n_rs):
        @pl.when(m != me)
        def _():
            rs_copy(m, me).start()
    build_buf[pl.ds(b, 1)] = build_gram_ref[...][None]
    test_buf[pl.ds(t, 1)] = test_gram_ref[pl.ds(pl.multiple_of(t * g_rows, g_rows), g_rows), :][None]
    rs_buf[pl.ds(me, 1)] = part_ref[pl.ds(pl.multiple_of(me * rs_rows, rs_rows), rs_rows), :][None]

    for j in range(n_build):
        @pl.when(j != b)
        def _():
            build_copy(j, b).wait_send()
            build_copy(j, j).wait_recv()
    for j in range(n_test):
        @pl.when(j != t)
        def _():
            test_copy(j, t).wait_send()
            test_copy(j, j).wait_recv()

    my_rows = pl.ds(pl.multiple_of(t * g_rows, g_rows), g_rows)
    test_rows = test_buf[0]
    for j in range(1, n_test):
        test_rows = test_rows + test_buf[j]
    build_rows = build_buf[0, my_rows, :]
    for j in range(1, n_build):
        build_rows = build_rows + build_buf[j, my_rows, :]
    product_buf[...] = test_rows * build_rows

    for j in range(n_test):
        @pl.when(j != t)
        def _():
            gram_copy(j, t).start()
    gram_buf[pl.ds(t, 1)] = product_buf[...][None]
    for j in range(n_test):
        @pl.when(j != t)
        def _():
            gram_copy(j, t).wait_send()
            gram_copy(j, j).wait_recv()
    for j in range(n_test):
        inv_ref[j * g_rows:(j + 1) * g_rows, :] = gram_buf[j]

    sweep_in_place(inv_ref)

    for m in range(n_rs):
        @pl.when(m != me)
        def _():
            rs_copy(m, me).wait_send()
            rs_copy(m, m).wait_recv()
    owned = rs_buf[0]
    for m in range(1, n_rs):
        owned = owned + rs_buf[m]
    owned_ref[...] = owned


def exchange_and_invert(partial, test_gram, build_gram):
    n_build = lax.axis_size("build")
    n_test = lax.axis_size("test")
    n_rs = n_build * n_test
    rows, rank = partial.shape
    rs_rows = rows // n_rs
    g_rows = rank // n_test
    vmem = pl.BlockSpec(memory_space=pltpu.VMEM)
    f32 = jnp.float32
    return pl.pallas_call(
        functools.partial(tail_kernel, n_build, n_test),
        out_shape=(
            jax.ShapeDtypeStruct((rs_rows, rank), f32),
            jax.ShapeDtypeStruct((rank, rank), f32),
        ),
        in_specs=[vmem, vmem, vmem],
        out_specs=(vmem, vmem),
        scratch_shapes=[
            pltpu.VMEM((n_rs, rs_rows, rank), f32),
            pltpu.VMEM((n_test, g_rows, rank), f32),
            pltpu.VMEM((n_build, rank, rank), f32),
            pltpu.VMEM((g_rows, rank), f32),
            pltpu.VMEM((n_test, g_rows, rank), f32),
            pltpu.SemaphoreType.DMA((n_rs,)),
            pltpu.SemaphoreType.DMA((n_rs,)),
            pltpu.SemaphoreType.DMA((n_test,)),
            pltpu.SemaphoreType.DMA((n_test,)),
            pltpu.SemaphoreType.DMA((n_build,)),
            pltpu.SemaphoreType.DMA((n_build,)),
            pltpu.SemaphoreType.DMA((n_test,)),
            pltpu.SemaphoreType.DMA((n_test,)),
        ],
        compiler_params=pltpu.CompilerParams(has_side_effects=True, collective_id=1),
    )(partial, test_gram, build_gram)


def mttkrp_kernel(chunk, slot_info, test_ref, build_ref, tile_ref, out_ref, acc_ref):
    q = pl.program_id(0)
    c = pl.program_id(1)
    n_chunks = pl.num_programs(1)

    @pl.when((q == 0) & (c == 0))
    def _():
        out_ref[...] = jnp.zeros_like(out_ref)

    @pl.when(c == 0)
    def _():
        acc_ref[...] = jnp.zeros_like(acc_ref)

    live = q < slot_info[6]

    @pl.when(live)
    def _():
        build_block = build_ref[...].astype(jnp.float32)
        total = acc_ref[...]
        for i in range(chunk):
            test_row = test_ref[i : i + 1, :].astype(jnp.float32)
            khatri_rao = (test_row * build_block).astype(jnp.bfloat16)
            total = total + jnp.dot(tile_ref[i], khatri_rao, preferred_element_type=jnp.float32)
        acc_ref[...] = total

    @pl.when(live & (c == n_chunks - 1))
    def _():
        rows = pl.ds(pl.multiple_of(slot_info[4 + q] * TILE, TILE), TILE)
        out_ref[rows, :] += acc_ref[...]


def local_mttkrp(slot_values, slot_info, test_slab, build_slab):
    slots, width = slot_values.shape[0], slot_values.shape[1]
    rank = test_slab.shape[1]
    per_block = width // CHUNK
    grid_spec = pltpu.PrefetchScalarGridSpec(
        num_scalar_prefetch=1,
        grid=(slots, per_block),
        in_specs=[
            pl.BlockSpec((CHUNK, rank), lambda q, c, info: (info[q] * per_block + c, 0)),
            pl.BlockSpec((width, rank), lambda q, c, info: (info[2 + q], 0)),
            pl.BlockSpec((None, CHUNK, width, width), lambda q, c, info: (q, c, 0, 0)),
        ],
        out_specs=pl.BlockSpec((SB * width, rank), lambda q, c, info: (0, 0)),
        scratch_shapes=[pltpu.VMEM((width, rank), jnp.float32)],
    )
    return pl.pallas_call(
        functools.partial(mttkrp_kernel, CHUNK),
        out_shape=jax.ShapeDtypeStruct((SB * width, rank), jnp.float32),
        grid_spec=grid_spec,
    )(slot_info, test_slab, build_slab, slot_values)


def shards(tile_values, tile_test, tile_stmt, tile_build, tile_count, test_factor, build_factor):
    test_slab, build_slab = gather_factors(test_factor[0], build_factor[0])
    slot_values = tile_values[0, 0, 0]
    tile_width = slot_values.shape[-1]
    slot_info = jnp.concatenate([
        jnp.clip(tile_test[0, 0, 0], 0, test_slab.shape[0] // tile_width - 1),
        jnp.clip(tile_build[0, 0, 0], 0, build_slab.shape[0] // tile_width - 1),
        jnp.clip(tile_stmt[0, 0, 0], 0, SB - 1),
        tile_count[0, 0, 0][None],
    ]).astype(jnp.int32)
    running_sum = local_mttkrp(slot_values, slot_info, test_slab, build_slab)
    slab_test_gram = jnp.dot(test_slab.T, test_slab, preferred_element_type=jnp.float32)
    slab_build_gram = jnp.dot(build_slab.T, build_slab, preferred_element_type=jnp.float32)
    owned_sums, inverse = exchange_and_invert(running_sum, slab_test_gram, slab_build_gram)
    solved = jnp.dot(owned_sums, inverse, precision=lax.Precision.HIGHEST, preferred_element_type=jnp.float32)
    return solved[None]


def solution(mesh):
    return jax.shard_map(
        shards,
        mesh=mesh,
        in_specs=(
            P("build", "test", "stmt", None, None, None, None),
            P("build", "test", "stmt", None),
            P("build", "test", "stmt", None),
            P("build", "test", "stmt", None),
            P("build", "test", "stmt"),
            P("test", ("build", "stmt"), None),
            P("build", ("test", "stmt"), None),
        ),
        out_specs=P("stmt", ("build", "test"), None),
        check_vma=False,
    )
```

```python
import functools

import jax
import jax.numpy as jnp
from jax import lax
from jax.experimental import pallas as pl
from jax.experimental.pallas import tpu as pltpu
from jax.sharding import PartitionSpec as P

TILE = 128
SB = 2
MESH = pl.DeviceIdType.MESH
CHUNK = 32


def gather_kernel(n_build, n_test, n_stmt, test_in, build_in, test_out, build_out,
                  test_scr, build_scr, local_sem, t1_send, t1_recv, b1_send, b1_recv,
                  t2_send, t2_recv, b2_send, b2_recv):
    b = lax.axis_index("build")
    t = lax.axis_index("test")
    s = lax.axis_index("stmt")

    barrier = pltpu.get_barrier_semaphore()
    for j in range(n_stmt):
        @pl.when(j != s)
        def _():
            pl.semaphore_signal(barrier, 1, device_id=(b, t, j), device_id_type=MESH)
    for j in range(n_build):
        @pl.when(j != b)
        def _():
            pl.semaphore_signal(barrier, 1, device_id=(j, t, s), device_id_type=MESH)
    for j in range(n_test):
        @pl.when(j != t)
        def _():
            pl.semaphore_signal(barrier, 1, device_id=(b, j, s), device_id_type=MESH)
    pl.semaphore_wait(barrier, n_stmt + n_build + n_test - 3)

    def t1(j, slot):
        return pltpu.make_async_remote_copy(
            src_ref=test_in, dst_ref=test_scr.at[b, slot], send_sem=t1_send.at[j],
            recv_sem=t1_recv.at[slot], device_id=(b, t, j), device_id_type=MESH)

    def b1(j, slot):
        return pltpu.make_async_remote_copy(
            src_ref=build_in, dst_ref=build_scr.at[t, slot], send_sem=b1_send.at[j],
            recv_sem=b1_recv.at[slot], device_id=(b, t, j), device_id_type=MESH)

    def t2(j, slot):
        return pltpu.make_async_remote_copy(
            src_ref=test_scr.at[b], dst_ref=test_scr.at[slot], send_sem=t2_send.at[j],
            recv_sem=t2_recv.at[slot], device_id=(j, t, s), device_id_type=MESH)

    def b2(j, slot):
        return pltpu.make_async_remote_copy(
            src_ref=build_scr.at[t], dst_ref=build_scr.at[slot], send_sem=b2_send.at[j],
            recv_sem=b2_recv.at[slot], device_id=(b, j, s), device_id_type=MESH)

    for j in range(n_stmt):
        @pl.when(j != s)
        def _():
            t1(j, s).start()
            b1(j, s).start()
    own_test = pltpu.make_async_copy(test_in, test_scr.at[b, s], local_sem.at[0])
    own_build = pltpu.make_async_copy(build_in, build_scr.at[t, s], local_sem.at[1])
    own_test.start()
    own_build.start()
    own_test.wait()
    own_build.wait()
    for j in range(n_stmt):
        @pl.when(j != s)
        def _():
            t1(j, s).wait_send()
            b1(j, s).wait_send()
            t1(j, j).wait_recv()
            b1(j, j).wait_recv()

    for j in range(n_build):
        @pl.when(j != b)
        def _():
            t2(j, b).start()
    for j in range(n_test):
        @pl.when(j != t)
        def _():
            b2(j, t).start()
    for j in range(n_build):
        @pl.when(j != b)
        def _():
            t2(j, b).wait_send()
            t2(j, j).wait_recv()
    for j in range(n_test):
        @pl.when(j != t)
        def _():
            b2(j, t).wait_send()
            b2(j, j).wait_recv()
    test_out[...] = test_scr[...]
    build_out[...] = build_scr[...]


def gather_factors(test_rows, build_rows):
    n_build = lax.axis_size("build")
    n_test = lax.axis_size("test")
    n_stmt = lax.axis_size("stmt")
    vmem = pl.BlockSpec(memory_space=pltpu.VMEM)
    test_shape = (n_build, n_stmt, *test_rows.shape)
    build_shape = (n_test, n_stmt, *build_rows.shape)
    dma = pltpu.SemaphoreType.DMA
    test_pieces, build_pieces = pl.pallas_call(
        functools.partial(gather_kernel, n_build, n_test, n_stmt),
        out_shape=(
            jax.ShapeDtypeStruct(test_shape, test_rows.dtype),
            jax.ShapeDtypeStruct(build_shape, build_rows.dtype),
        ),
        in_specs=[vmem, vmem],
        out_specs=(vmem, vmem),
        scratch_shapes=[
            pltpu.VMEM(test_shape, test_rows.dtype),
            pltpu.VMEM(build_shape, build_rows.dtype),
            dma((2,)),
            dma((n_stmt,)), dma((n_stmt,)), dma((n_stmt,)), dma((n_stmt,)),
            dma((n_build,)), dma((n_build,)), dma((n_test,)), dma((n_test,)),
        ],
        compiler_params=pltpu.CompilerParams(has_side_effects=True, collective_id=0),
    )(test_rows, build_rows)
    return (
        test_pieces.reshape(-1, test_rows.shape[-1]),
        build_pieces.reshape(-1, build_rows.shape[-1]),
    )


def sweep_in_place(a_ref):
    n = a_ref.shape[0]
    lane = lax.broadcasted_iota(jnp.int32, (1, n), 1)

    def step(k, row):
        is_k = lane == k
        pivot = jnp.sum(jnp.where(is_k, row, 0.0), axis=1, keepdims=True)
        inv = 1.0 / pivot
        scaled = jnp.where(is_k, 1.0 - inv, row * inv)
        column = jnp.transpose(jnp.broadcast_to(row, (TILE, n)))
        following = jnp.minimum(k + 1, n - 1)
        next_factor = jnp.sum(jnp.where(lane == following, row, 0.0), axis=1, keepdims=True)
        next_row = a_ref[pl.ds(following, 1), :] - next_factor * scaled
        for h in range(n // TILE):
            lanes = slice(h * TILE, (h + 1) * TILE)
            a_ref[:, lanes] = a_ref[:, lanes] - column * scaled[:, lanes]
        a_ref[pl.ds(k, 1), :] = jnp.where(is_k, -inv, row * inv)
        return next_row

    lax.fori_loop(0, n, step, a_ref[0:1, :], unroll=4)
    a_ref[...] = -a_ref[...]


def tail_kernel(n_build, n_test, part_ref, test_gram_ref, build_gram_ref, owned_ref, inv_ref,
                rs_buf, test_buf, build_buf, product_buf, gram_buf,
                rs_send, rs_recv, test_send, test_recv, build_send, build_recv,
                gram_send, gram_recv):
    b = lax.axis_index("build")
    t = lax.axis_index("test")
    s = lax.axis_index("stmt")
    n_rs = n_build * n_test
    rs_rows = part_ref.shape[0] // n_rs
    g_rows = test_gram_ref.shape[0] // n_test
    me = b * n_test + t

    def rs_copy(m, dst_slot):
        return pltpu.make_async_remote_copy(
            src_ref=part_ref.at[pl.ds(m * rs_rows, rs_rows)], dst_ref=rs_buf.at[dst_slot],
            send_sem=rs_send.at[m], recv_sem=rs_recv.at[dst_slot],
            device_id=(m // n_test, m % n_test, s), device_id_type=MESH)

    def test_copy(j, dst_slot):
        return pltpu.make_async_remote_copy(
            src_ref=test_gram_ref.at[pl.ds(j * g_rows, g_rows)], dst_ref=test_buf.at[dst_slot],
            send_sem=test_send.at[j], recv_sem=test_recv.at[dst_slot],
            device_id=(b, j, s), device_id_type=MESH)

    def build_copy(j, dst_slot):
        return pltpu.make_async_remote_copy(
            src_ref=build_gram_ref.at[pl.ds(t * g_rows, g_rows)], dst_ref=build_buf.at[dst_slot],
            send_sem=build_send.at[j], recv_sem=build_recv.at[dst_slot],
            device_id=(j, t, s), device_id_type=MESH)

    def gram_copy(j, dst_slot):
        return pltpu.make_async_remote_copy(
            src_ref=product_buf, dst_ref=gram_buf.at[dst_slot],
            send_sem=gram_send.at[j], recv_sem=gram_recv.at[dst_slot],
            device_id=(b, j, s), device_id_type=MESH)

    barrier = pltpu.get_barrier_semaphore()
    for m in range(n_rs):
        @pl.when(m != me)
        def _():
            pl.semaphore_signal(barrier, 1, device_id=(m // n_test, m % n_test, s), device_id_type=MESH)
    pl.semaphore_wait(barrier, n_rs - 1)

    for j in range(n_build):
        @pl.when(j != b)
        def _():
            build_copy(j, b).start()
    for j in range(n_test):
        @pl.when(j != t)
        def _():
            test_copy(j, t).start()
    build_buf[pl.ds(b, 1)] = build_gram_ref[pl.ds(pl.multiple_of(t * g_rows, g_rows), g_rows), :][None]
    test_buf[pl.ds(t, 1)] = test_gram_ref[pl.ds(pl.multiple_of(t * g_rows, g_rows), g_rows), :][None]

    for j in range(n_build):
        @pl.when(j != b)
        def _():
            build_copy(j, b).wait_send()
            build_copy(j, j).wait_recv()
    for j in range(n_test):
        @pl.when(j != t)
        def _():
            test_copy(j, t).wait_send()
            test_copy(j, j).wait_recv()

    test_rows = test_buf[0]
    for j in range(1, n_test):
        test_rows = test_rows + test_buf[j]
    build_rows = build_buf[0]
    for j in range(1, n_build):
        build_rows = build_rows + build_buf[j]
    product_buf[...] = test_rows * build_rows

    for j in range(n_test):
        @pl.when(j != t)
        def _():
            gram_copy(j, t).start()
    gram_buf[pl.ds(t, 1)] = product_buf[...][None]
    for j in range(n_test):
        @pl.when(j != t)
        def _():
            gram_copy(j, t).wait_send()
            gram_copy(j, j).wait_recv()
    for j in range(n_test):
        inv_ref[j * g_rows:(j + 1) * g_rows, :] = gram_buf[j]

    for m in range(n_rs):
        @pl.when(m != me)
        def _():
            rs_copy(m, me).start()
    rs_buf[pl.ds(me, 1)] = part_ref[pl.ds(pl.multiple_of(me * rs_rows, rs_rows), rs_rows), :][None]

    sweep_in_place(inv_ref)

    for m in range(n_rs):
        @pl.when(m != me)
        def _():
            rs_copy(m, me).wait_send()
            rs_copy(m, m).wait_recv()
    owned = rs_buf[0]
    for m in range(1, n_rs):
        owned = owned + rs_buf[m]
    owned_ref[...] = owned


def exchange_and_invert(partial, test_gram, build_gram):
    n_build = lax.axis_size("build")
    n_test = lax.axis_size("test")
    n_rs = n_build * n_test
    rows, rank = partial.shape
    rs_rows = rows // n_rs
    g_rows = rank // n_test
    vmem = pl.BlockSpec(memory_space=pltpu.VMEM)
    f32 = jnp.float32
    return pl.pallas_call(
        functools.partial(tail_kernel, n_build, n_test),
        out_shape=(
            jax.ShapeDtypeStruct((rs_rows, rank), f32),
            jax.ShapeDtypeStruct((rank, rank), f32),
        ),
        in_specs=[vmem, vmem, vmem],
        out_specs=(vmem, vmem),
        scratch_shapes=[
            pltpu.VMEM((n_rs, rs_rows, rank), f32),
            pltpu.VMEM((n_test, g_rows, rank), f32),
            pltpu.VMEM((n_build, g_rows, rank), f32),
            pltpu.VMEM((g_rows, rank), f32),
            pltpu.VMEM((n_test, g_rows, rank), f32),
            pltpu.SemaphoreType.DMA((n_rs,)),
            pltpu.SemaphoreType.DMA((n_rs,)),
            pltpu.SemaphoreType.DMA((n_test,)),
            pltpu.SemaphoreType.DMA((n_test,)),
            pltpu.SemaphoreType.DMA((n_build,)),
            pltpu.SemaphoreType.DMA((n_build,)),
            pltpu.SemaphoreType.DMA((n_test,)),
            pltpu.SemaphoreType.DMA((n_test,)),
        ],
        compiler_params=pltpu.CompilerParams(has_side_effects=True, collective_id=1),
    )(partial, test_gram, build_gram)


def mttkrp_kernel(chunk, slot_info, test_ref, build_ref, tile_ref, out_ref, acc_ref):
    q = pl.program_id(0)
    c = pl.program_id(1)
    n_chunks = pl.num_programs(1)

    @pl.when((q == 0) & (c == 0))
    def _():
        out_ref[...] = jnp.zeros_like(out_ref)

    @pl.when(c == 0)
    def _():
        acc_ref[...] = jnp.zeros_like(acc_ref)

    live = q < slot_info[6]

    @pl.when(live)
    def _():
        build_block = build_ref[...].astype(jnp.float32)
        total = acc_ref[...]
        for i in range(chunk):
            test_row = test_ref[i : i + 1, :].astype(jnp.float32)
            khatri_rao = (test_row * build_block).astype(jnp.bfloat16)
            total = total + jnp.dot(tile_ref[i], khatri_rao, preferred_element_type=jnp.float32)
        acc_ref[...] = total

    @pl.when(live & (c == n_chunks - 1))
    def _():
        rows = pl.ds(pl.multiple_of(slot_info[4 + q] * TILE, TILE), TILE)
        out_ref[rows, :] += acc_ref[...]


def local_mttkrp(slot_values, slot_info, test_slab, build_slab):
    slots, width = slot_values.shape[0], slot_values.shape[1]
    rank = test_slab.shape[1]
    per_block = width // CHUNK
    grid_spec = pltpu.PrefetchScalarGridSpec(
        num_scalar_prefetch=1,
        grid=(slots, per_block),
        in_specs=[
            pl.BlockSpec((CHUNK, rank), lambda q, c, info: (info[q] * per_block + c, 0)),
            pl.BlockSpec((width, rank), lambda q, c, info: (info[2 + q], 0)),
            pl.BlockSpec((None, CHUNK, width, width), lambda q, c, info: (q, c, 0, 0)),
        ],
        out_specs=pl.BlockSpec((SB * width, rank), lambda q, c, info: (0, 0)),
        scratch_shapes=[pltpu.VMEM((width, rank), jnp.float32)],
    )
    return pl.pallas_call(
        functools.partial(mttkrp_kernel, CHUNK),
        out_shape=jax.ShapeDtypeStruct((SB * width, rank), jnp.float32),
        grid_spec=grid_spec,
    )(slot_info, test_slab, build_slab, slot_values)


def shards(tile_values, tile_test, tile_stmt, tile_build, tile_count, test_factor, build_factor):
    test_slab, build_slab = gather_factors(test_factor[0], build_factor[0])
    slot_values = tile_values[0, 0, 0]
    tile_width = slot_values.shape[-1]
    slot_info = jnp.concatenate([
        jnp.clip(tile_test[0, 0, 0], 0, test_slab.shape[0] // tile_width - 1),
        jnp.clip(tile_build[0, 0, 0], 0, build_slab.shape[0] // tile_width - 1),
        jnp.clip(tile_stmt[0, 0, 0], 0, SB - 1),
        tile_count[0, 0, 0][None],
    ]).astype(jnp.int32)
    running_sum = local_mttkrp(slot_values, slot_info, test_slab, build_slab)
    slab_test_gram = jnp.dot(test_slab.T, test_slab, preferred_element_type=jnp.float32)
    slab_build_gram = jnp.dot(build_slab.T, build_slab, preferred_element_type=jnp.float32)
    owned_sums, inverse = exchange_and_invert(running_sum, slab_test_gram, slab_build_gram)
    solved = jnp.dot(owned_sums, inverse, precision=lax.Precision.HIGHEST, preferred_element_type=jnp.float32)
    return solved[None]


def solution(mesh):
    return jax.shard_map(
        shards,
        mesh=mesh,
        in_specs=(
            P("build", "test", "stmt", None, None, None, None),
            P("build", "test", "stmt", None),
            P("build", "test", "stmt", None),
            P("build", "test", "stmt", None),
            P("build", "test", "stmt"),
            P("test", ("build", "stmt"), None),
            P("build", ("test", "stmt"), None),
        ),
        out_specs=P("stmt", ("build", "test"), None),
        check_vma=False,
    )
```

```python
import functools

import jax
import jax.numpy as jnp
from jax import lax
from jax.experimental import pallas as pl
from jax.experimental.pallas import tpu as pltpu
from jax.sharding import PartitionSpec as P

TILE = 128
SB = 2
MESH = pl.DeviceIdType.MESH
CHUNK = 32


def gather_kernel(n_build, n_test, n_stmt, test_in, build_in, test_out, build_out,
                  test_scr, build_scr, local_sem, t1_send, t1_recv, b1_send, b1_recv,
                  t2_send, t2_recv, b2_send, b2_recv):
    b = lax.axis_index("build")
    t = lax.axis_index("test")
    s = lax.axis_index("stmt")

    barrier = pltpu.get_barrier_semaphore()
    for j in range(n_stmt):
        @pl.when(j != s)
        def _():
            pl.semaphore_signal(barrier, 1, device_id=(b, t, j), device_id_type=MESH)
    for j in range(n_build):
        @pl.when(j != b)
        def _():
            pl.semaphore_signal(barrier, 1, device_id=(j, t, s), device_id_type=MESH)
    for j in range(n_test):
        @pl.when(j != t)
        def _():
            pl.semaphore_signal(barrier, 1, device_id=(b, j, s), device_id_type=MESH)
    pl.semaphore_wait(barrier, n_stmt + n_build + n_test - 3)

    def t1(j, slot):
        return pltpu.make_async_remote_copy(
            src_ref=test_in, dst_ref=test_scr.at[b, slot], send_sem=t1_send.at[j],
            recv_sem=t1_recv.at[slot], device_id=(b, t, j), device_id_type=MESH)

    def b1(j, slot):
        return pltpu.make_async_remote_copy(
            src_ref=build_in, dst_ref=build_scr.at[t, slot], send_sem=b1_send.at[j],
            recv_sem=b1_recv.at[slot], device_id=(b, t, j), device_id_type=MESH)

    def t2(j, slot):
        return pltpu.make_async_remote_copy(
            src_ref=test_scr.at[b], dst_ref=test_scr.at[slot], send_sem=t2_send.at[j],
            recv_sem=t2_recv.at[slot], device_id=(j, t, s), device_id_type=MESH)

    def b2(j, slot):
        return pltpu.make_async_remote_copy(
            src_ref=build_scr.at[t], dst_ref=build_scr.at[slot], send_sem=b2_send.at[j],
            recv_sem=b2_recv.at[slot], device_id=(b, j, s), device_id_type=MESH)

    for j in range(n_stmt):
        @pl.when(j != s)
        def _():
            t1(j, s).start()
            b1(j, s).start()
    own_test = pltpu.make_async_copy(test_in, test_scr.at[b, s], local_sem.at[0])
    own_build = pltpu.make_async_copy(build_in, build_scr.at[t, s], local_sem.at[1])
    own_test.start()
    own_build.start()
    own_test.wait()
    own_build.wait()
    for j in range(n_stmt):
        @pl.when(j != s)
        def _():
            t1(j, s).wait_send()
            b1(j, s).wait_send()
            t1(j, j).wait_recv()
            b1(j, j).wait_recv()

    for j in range(n_build):
        @pl.when(j != b)
        def _():
            t2(j, b).start()
    for j in range(n_test):
        @pl.when(j != t)
        def _():
            b2(j, t).start()
    for j in range(n_build):
        @pl.when(j != b)
        def _():
            t2(j, b).wait_send()
            t2(j, j).wait_recv()
    for j in range(n_test):
        @pl.when(j != t)
        def _():
            b2(j, t).wait_send()
            b2(j, j).wait_recv()
    test_out[...] = test_scr[...]
    build_out[...] = build_scr[...]


def gather_factors(test_rows, build_rows):
    n_build = lax.axis_size("build")
    n_test = lax.axis_size("test")
    n_stmt = lax.axis_size("stmt")
    vmem = pl.BlockSpec(memory_space=pltpu.VMEM)
    test_shape = (n_build, n_stmt, *test_rows.shape)
    build_shape = (n_test, n_stmt, *build_rows.shape)
    dma = pltpu.SemaphoreType.DMA
    test_pieces, build_pieces = pl.pallas_call(
        functools.partial(gather_kernel, n_build, n_test, n_stmt),
        out_shape=(
            jax.ShapeDtypeStruct(test_shape, test_rows.dtype),
            jax.ShapeDtypeStruct(build_shape, build_rows.dtype),
        ),
        in_specs=[vmem, vmem],
        out_specs=(vmem, vmem),
        scratch_shapes=[
            pltpu.VMEM(test_shape, test_rows.dtype),
            pltpu.VMEM(build_shape, build_rows.dtype),
            dma((2,)),
            dma((n_stmt,)), dma((n_stmt,)), dma((n_stmt,)), dma((n_stmt,)),
            dma((n_build,)), dma((n_build,)), dma((n_test,)), dma((n_test,)),
        ],
        compiler_params=pltpu.CompilerParams(has_side_effects=True, collective_id=0),
    )(test_rows, build_rows)
    return (
        test_pieces.reshape(-1, test_rows.shape[-1]),
        build_pieces.reshape(-1, build_rows.shape[-1]),
    )


def sweep_in_place(a_ref):
    n = a_ref.shape[0]
    lane = lax.broadcasted_iota(jnp.int32, (1, n), 1)

    def step(k, row):
        is_k = lane == k
        pivot = jnp.sum(jnp.where(is_k, row, 0.0), axis=1, keepdims=True)
        inv = 1.0 / pivot
        scaled = jnp.where(is_k, 1.0 - inv, row * inv)
        column = jnp.transpose(jnp.broadcast_to(row, (TILE, n)))
        following = jnp.minimum(k + 1, n - 1)
        next_factor = jnp.sum(jnp.where(lane == following, row, 0.0), axis=1, keepdims=True)
        next_row = a_ref[pl.ds(following, 1), :] - next_factor * scaled
        for h in range(n // TILE):
            lanes = slice(h * TILE, (h + 1) * TILE)
            a_ref[:, lanes] = a_ref[:, lanes] - column * scaled[:, lanes]
        a_ref[pl.ds(k, 1), :] = jnp.where(is_k, -inv, row * inv)
        return next_row

    lax.fori_loop(0, n, step, a_ref[0:1, :], unroll=8)
    a_ref[...] = -a_ref[...]


def tail_kernel(n_build, n_test, part_ref, test_gram_ref, build_gram_ref, owned_ref, inv_ref,
                rs_buf, test_buf, build_buf, product_buf, gram_buf,
                rs_send, rs_recv, test_send, test_recv, build_send, build_recv,
                gram_send, gram_recv):
    b = lax.axis_index("build")
    t = lax.axis_index("test")
    s = lax.axis_index("stmt")
    n_rs = n_build * n_test
    rs_rows = part_ref.shape[0] // n_rs
    g_rows = test_gram_ref.shape[0] // n_test
    me = b * n_test + t

    def rs_copy(m, dst_slot):
        return pltpu.make_async_remote_copy(
            src_ref=part_ref.at[pl.ds(m * rs_rows, rs_rows)], dst_ref=rs_buf.at[dst_slot],
            send_sem=rs_send.at[m], recv_sem=rs_recv.at[dst_slot],
            device_id=(m // n_test, m % n_test, s), device_id_type=MESH)

    def test_copy(j, dst_slot):
        return pltpu.make_async_remote_copy(
            src_ref=test_gram_ref.at[pl.ds(j * g_rows, g_rows)], dst_ref=test_buf.at[dst_slot],
            send_sem=test_send.at[j], recv_sem=test_recv.at[dst_slot],
            device_id=(b, j, s), device_id_type=MESH)

    def build_copy(j, dst_slot):
        return pltpu.make_async_remote_copy(
            src_ref=build_gram_ref.at[pl.ds(t * g_rows, g_rows)], dst_ref=build_buf.at[dst_slot],
            send_sem=build_send.at[j], recv_sem=build_recv.at[dst_slot],
            device_id=(j, t, s), device_id_type=MESH)

    def gram_copy(j, dst_slot):
        return pltpu.make_async_remote_copy(
            src_ref=product_buf, dst_ref=gram_buf.at[dst_slot],
            send_sem=gram_send.at[j], recv_sem=gram_recv.at[dst_slot],
            device_id=(b, j, s), device_id_type=MESH)

    barrier = pltpu.get_barrier_semaphore()
    for m in range(n_rs):
        @pl.when(m != me)
        def _():
            pl.semaphore_signal(barrier, 1, device_id=(m // n_test, m % n_test, s), device_id_type=MESH)
    pl.semaphore_wait(barrier, n_rs - 1)

    for j in range(n_build):
        @pl.when(j != b)
        def _():
            build_copy(j, b).start()
    for j in range(n_test):
        @pl.when(j != t)
        def _():
            test_copy(j, t).start()
    build_buf[pl.ds(b, 1)] = build_gram_ref[pl.ds(pl.multiple_of(t * g_rows, g_rows), g_rows), :][None]
    test_buf[pl.ds(t, 1)] = test_gram_ref[pl.ds(pl.multiple_of(t * g_rows, g_rows), g_rows), :][None]

    for j in range(n_build):
        @pl.when(j != b)
        def _():
            build_copy(j, b).wait_send()
            build_copy(j, j).wait_recv()
    for j in range(n_test):
        @pl.when(j != t)
        def _():
            test_copy(j, t).wait_send()
            test_copy(j, j).wait_recv()

    test_rows = test_buf[0]
    for j in range(1, n_test):
        test_rows = test_rows + test_buf[j]
    build_rows = build_buf[0]
    for j in range(1, n_build):
        build_rows = build_rows + build_buf[j]
    product_buf[...] = test_rows * build_rows

    for j in range(n_test):
        @pl.when(j != t)
        def _():
            gram_copy(j, t).start()
    gram_buf[pl.ds(t, 1)] = product_buf[...][None]
    for j in range(n_test):
        @pl.when(j != t)
        def _():
            gram_copy(j, t).wait_send()
            gram_copy(j, j).wait_recv()
    for j in range(n_test):
        inv_ref[j * g_rows:(j + 1) * g_rows, :] = gram_buf[j]

    for m in range(n_rs):
        @pl.when(m != me)
        def _():
            rs_copy(m, me).start()
    rs_buf[pl.ds(me, 1)] = part_ref[pl.ds(pl.multiple_of(me * rs_rows, rs_rows), rs_rows), :][None]

    sweep_in_place(inv_ref)

    for m in range(n_rs):
        @pl.when(m != me)
        def _():
            rs_copy(m, me).wait_send()
            rs_copy(m, m).wait_recv()
    owned = rs_buf[0]
    for m in range(1, n_rs):
        owned = owned + rs_buf[m]
    owned_ref[...] = owned


def exchange_and_invert(partial, test_gram, build_gram):
    n_build = lax.axis_size("build")
    n_test = lax.axis_size("test")
    n_rs = n_build * n_test
    rows, rank = partial.shape
    rs_rows = rows // n_rs
    g_rows = rank // n_test
    vmem = pl.BlockSpec(memory_space=pltpu.VMEM)
    f32 = jnp.float32
    return pl.pallas_call(
        functools.partial(tail_kernel, n_build, n_test),
        out_shape=(
            jax.ShapeDtypeStruct((rs_rows, rank), f32),
            jax.ShapeDtypeStruct((rank, rank), f32),
        ),
        in_specs=[vmem, vmem, vmem],
        out_specs=(vmem, vmem),
        scratch_shapes=[
            pltpu.VMEM((n_rs, rs_rows, rank), f32),
            pltpu.VMEM((n_test, g_rows, rank), f32),
            pltpu.VMEM((n_build, g_rows, rank), f32),
            pltpu.VMEM((g_rows, rank), f32),
            pltpu.VMEM((n_test, g_rows, rank), f32),
            pltpu.SemaphoreType.DMA((n_rs,)),
            pltpu.SemaphoreType.DMA((n_rs,)),
            pltpu.SemaphoreType.DMA((n_test,)),
            pltpu.SemaphoreType.DMA((n_test,)),
            pltpu.SemaphoreType.DMA((n_build,)),
            pltpu.SemaphoreType.DMA((n_build,)),
            pltpu.SemaphoreType.DMA((n_test,)),
            pltpu.SemaphoreType.DMA((n_test,)),
        ],
        compiler_params=pltpu.CompilerParams(has_side_effects=True, collective_id=1),
    )(partial, test_gram, build_gram)


def mttkrp_kernel(chunk, slot_info, test_ref, build_ref, tile_ref, out_ref, acc_ref):
    q = pl.program_id(0)
    c = pl.program_id(1)
    n_chunks = pl.num_programs(1)

    @pl.when((q == 0) & (c == 0))
    def _():
        out_ref[...] = jnp.zeros_like(out_ref)

    @pl.when(c == 0)
    def _():
        acc_ref[...] = jnp.zeros_like(acc_ref)

    live = q < slot_info[6]

    @pl.when(live)
    def _():
        build_block = build_ref[...].astype(jnp.float32)
        total = acc_ref[...]
        for i in range(chunk):
            test_row = test_ref[i : i + 1, :].astype(jnp.float32)
            khatri_rao = (test_row * build_block).astype(jnp.bfloat16)
            total = total + jnp.dot(tile_ref[i], khatri_rao, preferred_element_type=jnp.float32)
        acc_ref[...] = total

    @pl.when(live & (c == n_chunks - 1))
    def _():
        rows = pl.ds(pl.multiple_of(slot_info[4 + q] * TILE, TILE), TILE)
        out_ref[rows, :] += acc_ref[...]


def local_mttkrp(slot_values, slot_info, test_slab, build_slab):
    slots, width = slot_values.shape[0], slot_values.shape[1]
    rank = test_slab.shape[1]
    per_block = width // CHUNK
    grid_spec = pltpu.PrefetchScalarGridSpec(
        num_scalar_prefetch=1,
        grid=(slots, per_block),
        in_specs=[
            pl.BlockSpec((CHUNK, rank), lambda q, c, info: (info[q] * per_block + c, 0)),
            pl.BlockSpec((width, rank), lambda q, c, info: (info[2 + q], 0)),
            pl.BlockSpec((None, CHUNK, width, width), lambda q, c, info: (q, c, 0, 0)),
        ],
        out_specs=pl.BlockSpec((SB * width, rank), lambda q, c, info: (0, 0)),
        scratch_shapes=[pltpu.VMEM((width, rank), jnp.float32)],
    )
    return pl.pallas_call(
        functools.partial(mttkrp_kernel, CHUNK),
        out_shape=jax.ShapeDtypeStruct((SB * width, rank), jnp.float32),
        grid_spec=grid_spec,
    )(slot_info, test_slab, build_slab, slot_values)


def shards(tile_values, tile_test, tile_stmt, tile_build, tile_count, test_factor, build_factor):
    test_slab, build_slab = gather_factors(test_factor[0], build_factor[0])
    slot_values = tile_values[0, 0, 0]
    tile_width = slot_values.shape[-1]
    slot_info = jnp.concatenate([
        jnp.clip(tile_test[0, 0, 0], 0, test_slab.shape[0] // tile_width - 1),
        jnp.clip(tile_build[0, 0, 0], 0, build_slab.shape[0] // tile_width - 1),
        jnp.clip(tile_stmt[0, 0, 0], 0, SB - 1),
        tile_count[0, 0, 0][None],
    ]).astype(jnp.int32)
    running_sum = local_mttkrp(slot_values, slot_info, test_slab, build_slab)
    slab_test_gram = jnp.dot(test_slab.T, test_slab, preferred_element_type=jnp.float32)
    slab_build_gram = jnp.dot(build_slab.T, build_slab, preferred_element_type=jnp.float32)
    owned_sums, inverse = exchange_and_invert(running_sum, slab_test_gram, slab_build_gram)
    solved = jnp.dot(owned_sums, inverse, precision=lax.Precision.HIGHEST, preferred_element_type=jnp.float32)
    return solved[None]


def solution(mesh):
    return jax.shard_map(
        shards,
        mesh=mesh,
        in_specs=(
            P("build", "test", "stmt", None, None, None, None),
            P("build", "test", "stmt", None),
            P("build", "test", "stmt", None),
            P("build", "test", "stmt", None),
            P("build", "test", "stmt"),
            P("test", ("build", "stmt"), None),
            P("build", ("test", "stmt"), None),
        ),
        out_specs=P("stmt", ("build", "test"), None),
        check_vma=False,
    )
```

```python
import functools

import jax
import jax.numpy as jnp
from jax import lax
from jax.experimental import pallas as pl
from jax.experimental.pallas import tpu as pltpu
from jax.sharding import PartitionSpec as P

TILE = 128
SB = 2
MESH = pl.DeviceIdType.MESH
CHUNK = 32


def gather_kernel(n_build, n_test, n_stmt, test_in, build_in, test_out, build_out,
                  test_scr, build_scr, local_sem, t1_send, t1_recv, b1_send, b1_recv,
                  t2_send, t2_recv, b2_send, b2_recv):
    b = lax.axis_index("build")
    t = lax.axis_index("test")
    s = lax.axis_index("stmt")

    barrier = pltpu.get_barrier_semaphore()
    for j in range(n_stmt):
        @pl.when(j != s)
        def _():
            pl.semaphore_signal(barrier, 1, device_id=(b, t, j), device_id_type=MESH)
    for j in range(n_build):
        @pl.when(j != b)
        def _():
            pl.semaphore_signal(barrier, 1, device_id=(j, t, s), device_id_type=MESH)
    for j in range(n_test):
        @pl.when(j != t)
        def _():
            pl.semaphore_signal(barrier, 1, device_id=(b, j, s), device_id_type=MESH)
    pl.semaphore_wait(barrier, n_stmt + n_build + n_test - 3)

    def t1(j, slot):
        return pltpu.make_async_remote_copy(
            src_ref=test_in, dst_ref=test_scr.at[b, slot], send_sem=t1_send.at[j],
            recv_sem=t1_recv.at[slot], device_id=(b, t, j), device_id_type=MESH)

    def b1(j, slot):
        return pltpu.make_async_remote_copy(
            src_ref=build_in, dst_ref=build_scr.at[t, slot], send_sem=b1_send.at[j],
            recv_sem=b1_recv.at[slot], device_id=(b, t, j), device_id_type=MESH)

    def t2(j, slot):
        return pltpu.make_async_remote_copy(
            src_ref=test_scr.at[b], dst_ref=test_scr.at[slot], send_sem=t2_send.at[j],
            recv_sem=t2_recv.at[slot], device_id=(j, t, s), device_id_type=MESH)

    def b2(j, slot):
        return pltpu.make_async_remote_copy(
            src_ref=build_scr.at[t], dst_ref=build_scr.at[slot], send_sem=b2_send.at[j],
            recv_sem=b2_recv.at[slot], device_id=(b, j, s), device_id_type=MESH)

    for j in range(n_stmt):
        @pl.when(j != s)
        def _():
            t1(j, s).start()
            b1(j, s).start()
    own_test = pltpu.make_async_copy(test_in, test_scr.at[b, s], local_sem.at[0])
    own_build = pltpu.make_async_copy(build_in, build_scr.at[t, s], local_sem.at[1])
    own_test.start()
    own_build.start()
    own_test.wait()
    own_build.wait()
    for j in range(n_stmt):
        @pl.when(j != s)
        def _():
            t1(j, s).wait_send()
            b1(j, s).wait_send()
            t1(j, j).wait_recv()
            b1(j, j).wait_recv()

    for j in range(n_build):
        @pl.when(j != b)
        def _():
            t2(j, b).start()
    for j in range(n_test):
        @pl.when(j != t)
        def _():
            b2(j, t).start()
    for j in range(n_build):
        @pl.when(j != b)
        def _():
            t2(j, b).wait_send()
            t2(j, j).wait_recv()
    for j in range(n_test):
        @pl.when(j != t)
        def _():
            b2(j, t).wait_send()
            b2(j, j).wait_recv()
    test_out[...] = test_scr[...]
    build_out[...] = build_scr[...]


def gather_factors(test_rows, build_rows):
    n_build = lax.axis_size("build")
    n_test = lax.axis_size("test")
    n_stmt = lax.axis_size("stmt")
    vmem = pl.BlockSpec(memory_space=pltpu.VMEM)
    test_shape = (n_build, n_stmt, *test_rows.shape)
    build_shape = (n_test, n_stmt, *build_rows.shape)
    dma = pltpu.SemaphoreType.DMA
    test_pieces, build_pieces = pl.pallas_call(
        functools.partial(gather_kernel, n_build, n_test, n_stmt),
        out_shape=(
            jax.ShapeDtypeStruct(test_shape, test_rows.dtype),
            jax.ShapeDtypeStruct(build_shape, build_rows.dtype),
        ),
        in_specs=[vmem, vmem],
        out_specs=(vmem, vmem),
        scratch_shapes=[
            pltpu.VMEM(test_shape, test_rows.dtype),
            pltpu.VMEM(build_shape, build_rows.dtype),
            dma((2,)),
            dma((n_stmt,)), dma((n_stmt,)), dma((n_stmt,)), dma((n_stmt,)),
            dma((n_build,)), dma((n_build,)), dma((n_test,)), dma((n_test,)),
        ],
        compiler_params=pltpu.CompilerParams(has_side_effects=True, collective_id=0),
    )(test_rows, build_rows)
    return (
        test_pieces.reshape(-1, test_rows.shape[-1]),
        build_pieces.reshape(-1, build_rows.shape[-1]),
    )


def sweep_in_place(a_ref):
    n = a_ref.shape[0]
    lane = lax.broadcasted_iota(jnp.int32, (1, n), 1)

    def step(k, row):
        is_k = lane == k
        pivot = jnp.sum(jnp.where(is_k, row, 0.0), axis=1, keepdims=True)
        inv = 1.0 / pivot
        scaled = jnp.where(is_k, 1.0 - inv, row * inv)
        column = jnp.transpose(jnp.broadcast_to(row, (TILE, n)))
        following = jnp.minimum(k + 1, n - 1)
        next_factor = jnp.sum(jnp.where(lane == following, row, 0.0), axis=1, keepdims=True)
        next_row = a_ref[pl.ds(following, 1), :] - next_factor * scaled
        for h in range(n // TILE):
            lanes = slice(h * TILE, (h + 1) * TILE)
            a_ref[:, lanes] = a_ref[:, lanes] - column * scaled[:, lanes]
        a_ref[pl.ds(k, 1), :] = jnp.where(is_k, -inv, row * inv)
        return next_row

    lax.fori_loop(0, n, step, a_ref[0:1, :], unroll=8)
    a_ref[...] = -a_ref[...]


def tail_kernel(n_build, n_test, part_ref, test_gram_ref, build_gram_ref, owned_ref, inv_ref,
                rs_buf, test_buf, build_buf, product_buf, gram_buf,
                rs_send, rs_recv, test_send, test_recv, build_send, build_recv,
                gram_send, gram_recv):
    b = lax.axis_index("build")
    t = lax.axis_index("test")
    s = lax.axis_index("stmt")
    n_rs = n_build * n_test
    rs_rows = part_ref.shape[0] // n_rs
    g_rows = test_gram_ref.shape[0] // n_test
    me = b * n_test + t

    def rs_copy(m, dst_slot):
        return pltpu.make_async_remote_copy(
            src_ref=part_ref.at[pl.ds(m * rs_rows, rs_rows)], dst_ref=rs_buf.at[dst_slot],
            send_sem=rs_send.at[m], recv_sem=rs_recv.at[dst_slot],
            device_id=(m // n_test, m % n_test, s), device_id_type=MESH)

    def test_copy(j, dst_slot):
        return pltpu.make_async_remote_copy(
            src_ref=test_gram_ref.at[pl.ds(j * g_rows, g_rows)], dst_ref=test_buf.at[dst_slot],
            send_sem=test_send.at[j], recv_sem=test_recv.at[dst_slot],
            device_id=(b, j, s), device_id_type=MESH)

    def build_copy(j, dst_slot):
        return pltpu.make_async_remote_copy(
            src_ref=build_gram_ref.at[pl.ds(t * g_rows, g_rows)], dst_ref=build_buf.at[dst_slot],
            send_sem=build_send.at[j], recv_sem=build_recv.at[dst_slot],
            device_id=(j, t, s), device_id_type=MESH)

    def gram_copy(j, dst_slot):
        return pltpu.make_async_remote_copy(
            src_ref=product_buf, dst_ref=gram_buf.at[dst_slot],
            send_sem=gram_send.at[j], recv_sem=gram_recv.at[dst_slot],
            device_id=(b, j, s), device_id_type=MESH)

    barrier = pltpu.get_barrier_semaphore()
    for m in range(n_rs):
        @pl.when(m != me)
        def _():
            pl.semaphore_signal(barrier, 1, device_id=(m // n_test, m % n_test, s), device_id_type=MESH)
    pl.semaphore_wait(barrier, n_rs - 1)

    for j in range(n_build):
        @pl.when(j != b)
        def _():
            build_copy(j, b).start()
    for j in range(n_test):
        @pl.when(j != t)
        def _():
            test_copy(j, t).start()
    build_buf[pl.ds(b, 1)] = build_gram_ref[pl.ds(pl.multiple_of(t * g_rows, g_rows), g_rows), :][None]
    test_buf[pl.ds(t, 1)] = test_gram_ref[pl.ds(pl.multiple_of(t * g_rows, g_rows), g_rows), :][None]

    for j in range(n_build):
        @pl.when(j != b)
        def _():
            build_copy(j, b).wait_send()
            build_copy(j, j).wait_recv()
    for j in range(n_test):
        @pl.when(j != t)
        def _():
            test_copy(j, t).wait_send()
            test_copy(j, j).wait_recv()

    test_rows = test_buf[0]
    for j in range(1, n_test):
        test_rows = test_rows + test_buf[j]
    build_rows = build_buf[0]
    for j in range(1, n_build):
        build_rows = build_rows + build_buf[j]
    product_buf[...] = test_rows * build_rows

    for j in range(n_test):
        @pl.when(j != t)
        def _():
            gram_copy(j, t).start()
    gram_buf[pl.ds(t, 1)] = product_buf[...][None]
    for j in range(n_test):
        @pl.when(j != t)
        def _():
            gram_copy(j, t).wait_send()
            gram_copy(j, j).wait_recv()
    for j in range(n_test):
        inv_ref[j * g_rows:(j + 1) * g_rows, :] = gram_buf[j]

    for m in range(n_rs):
        @pl.when(m != me)
        def _():
            rs_copy(m, me).start()
    rs_buf[pl.ds(me, 1)] = part_ref[pl.ds(pl.multiple_of(me * rs_rows, rs_rows), rs_rows), :][None]

    sweep_in_place(inv_ref)

    for m in range(n_rs):
        @pl.when(m != me)
        def _():
            rs_copy(m, me).wait_send()
            rs_copy(m, m).wait_recv()
    owned = rs_buf[0]
    for m in range(1, n_rs):
        owned = owned + rs_buf[m]
    owned_ref[...] = owned


def exchange_and_invert(partial, test_gram, build_gram):
    n_build = lax.axis_size("build")
    n_test = lax.axis_size("test")
    n_rs = n_build * n_test
    rows, rank = partial.shape
    rs_rows = rows // n_rs
    g_rows = rank // n_test
    vmem = pl.BlockSpec(memory_space=pltpu.VMEM)
    f32 = jnp.float32
    return pl.pallas_call(
        functools.partial(tail_kernel, n_build, n_test),
        out_shape=(
            jax.ShapeDtypeStruct((rs_rows, rank), f32),
            jax.ShapeDtypeStruct((rank, rank), f32),
        ),
        in_specs=[vmem, vmem, vmem],
        out_specs=(vmem, vmem),
        scratch_shapes=[
            pltpu.VMEM((n_rs, rs_rows, rank), f32),
            pltpu.VMEM((n_test, g_rows, rank), f32),
            pltpu.VMEM((n_build, g_rows, rank), f32),
            pltpu.VMEM((g_rows, rank), f32),
            pltpu.VMEM((n_test, g_rows, rank), f32),
            pltpu.SemaphoreType.DMA((n_rs,)),
            pltpu.SemaphoreType.DMA((n_rs,)),
            pltpu.SemaphoreType.DMA((n_test,)),
            pltpu.SemaphoreType.DMA((n_test,)),
            pltpu.SemaphoreType.DMA((n_build,)),
            pltpu.SemaphoreType.DMA((n_build,)),
            pltpu.SemaphoreType.DMA((n_test,)),
            pltpu.SemaphoreType.DMA((n_test,)),
        ],
        compiler_params=pltpu.CompilerParams(has_side_effects=True, collective_id=1),
    )(partial, test_gram, build_gram)


def mttkrp_kernel(chunk, n_test_blocks, n_stmt_blocks, slot_tests, slot_builds, slot_stmts,
                  live_count, test_ref, build_ref, tile_ref, out_ref, acc_ref):
    q = pl.program_id(0)
    c = pl.program_id(1)
    n_chunks = pl.num_programs(1)

    @pl.when((q == 0) & (c == 0))
    def _():
        out_ref[...] = jnp.zeros_like(out_ref)

    @pl.when(c == 0)
    def _():
        acc_ref[...] = jnp.zeros_like(acc_ref)

    live = q < live_count[0]

    @pl.when(live)
    def _():
        build_block = build_ref[...].astype(jnp.float32)
        total = acc_ref[...]
        for i in range(chunk):
            test_row = test_ref[i : i + 1, :].astype(jnp.float32)
            khatri_rao = (test_row * build_block).astype(jnp.bfloat16)
            total = total + jnp.dot(tile_ref[i], khatri_rao, preferred_element_type=jnp.float32)
        acc_ref[...] = total

    @pl.when(live & (c == n_chunks - 1))
    def _():
        block = jnp.clip(slot_stmts[q], 0, n_stmt_blocks - 1)
        rows = pl.ds(pl.multiple_of(block * TILE, TILE), TILE)
        out_ref[rows, :] += acc_ref[...]


def local_mttkrp(slot_values, slot_tests, slot_builds, slot_stmts, live_count, test_slab, build_slab):
    slots, width = slot_values.shape[0], slot_values.shape[1]
    rank = test_slab.shape[1]
    per_block = width // CHUNK
    n_test_blocks = test_slab.shape[0] // width
    n_build_blocks = build_slab.shape[0] // width

    def test_map(q, c, tests, builds, stmts, count):
        return (jnp.clip(tests[q], 0, n_test_blocks - 1) * per_block + c, 0)

    def build_map(q, c, tests, builds, stmts, count):
        return (jnp.clip(builds[q], 0, n_build_blocks - 1), 0)

    grid_spec = pltpu.PrefetchScalarGridSpec(
        num_scalar_prefetch=4,
        grid=(slots, per_block),
        in_specs=[
            pl.BlockSpec((CHUNK, rank), test_map),
            pl.BlockSpec((width, rank), build_map),
            pl.BlockSpec((None, CHUNK, width, width), lambda q, c, *info: (q, c, 0, 0)),
        ],
        out_specs=pl.BlockSpec((SB * width, rank), lambda q, c, *info: (0, 0)),
        scratch_shapes=[pltpu.VMEM((width, rank), jnp.float32)],
    )
    return pl.pallas_call(
        functools.partial(mttkrp_kernel, CHUNK, n_test_blocks, SB),
        out_shape=jax.ShapeDtypeStruct((SB * width, rank), jnp.float32),
        grid_spec=grid_spec,
    )(slot_tests, slot_builds, slot_stmts, live_count, test_slab, build_slab, slot_values)


def shards(tile_values, tile_test, tile_stmt, tile_build, tile_count, test_factor, build_factor):
    test_slab, build_slab = gather_factors(test_factor[0], build_factor[0])
    slot_values = tile_values[0, 0, 0]
    tile_width = slot_values.shape[-1]
    running_sum = local_mttkrp(
        slot_values, tile_test[0, 0, 0], tile_build[0, 0, 0], tile_stmt[0, 0, 0],
        tile_count[0, 0], test_slab, build_slab)
    slab_test_gram = jnp.dot(test_slab.T, test_slab, preferred_element_type=jnp.float32)
    slab_build_gram = jnp.dot(build_slab.T, build_slab, preferred_element_type=jnp.float32)
    owned_sums, inverse = exchange_and_invert(running_sum, slab_test_gram, slab_build_gram)
    solved = jnp.dot(owned_sums, inverse, precision=lax.Precision.HIGHEST, preferred_element_type=jnp.float32)
    return solved[None]


def solution(mesh):
    return jax.shard_map(
        shards,
        mesh=mesh,
        in_specs=(
            P("build", "test", "stmt", None, None, None, None),
            P("build", "test", "stmt", None),
            P("build", "test", "stmt", None),
            P("build", "test", "stmt", None),
            P("build", "test", "stmt"),
            P("test", ("build", "stmt"), None),
            P("build", ("test", "stmt"), None),
        ),
        out_specs=P("stmt", ("build", "test"), None),
        check_vma=False,
    )
```

```python
import functools

import jax
import jax.numpy as jnp
from jax import lax
from jax.experimental import pallas as pl
from jax.experimental.pallas import tpu as pltpu
from jax.sharding import PartitionSpec as P

TILE = 128
SB = 2
MESH = pl.DeviceIdType.MESH
CHUNK = 32


def gather_kernel(n_build, n_test, n_stmt, test_in, build_in, test_out, build_out,
                  test_scr, build_scr, local_sem, t1_send, t1_recv, b1_send, b1_recv,
                  t2_send, t2_recv, b2_send, b2_recv):
    b = lax.axis_index("build")
    t = lax.axis_index("test")
    s = lax.axis_index("stmt")

    barrier = pltpu.get_barrier_semaphore()
    for j in range(n_stmt):
        @pl.when(j != s)
        def _():
            pl.semaphore_signal(barrier, 1, device_id=(b, t, j), device_id_type=MESH)
    for j in range(n_build):
        @pl.when(j != b)
        def _():
            pl.semaphore_signal(barrier, 1, device_id=(j, t, s), device_id_type=MESH)
    for j in range(n_test):
        @pl.when(j != t)
        def _():
            pl.semaphore_signal(barrier, 1, device_id=(b, j, s), device_id_type=MESH)
    pl.semaphore_wait(barrier, n_stmt + n_build + n_test - 3)

    def t1(j, slot):
        return pltpu.make_async_remote_copy(
            src_ref=test_in, dst_ref=test_scr.at[b, slot], send_sem=t1_send.at[j],
            recv_sem=t1_recv.at[slot], device_id=(b, t, j), device_id_type=MESH)

    def b1(j, slot):
        return pltpu.make_async_remote_copy(
            src_ref=build_in, dst_ref=build_scr.at[t, slot], send_sem=b1_send.at[j],
            recv_sem=b1_recv.at[slot], device_id=(b, t, j), device_id_type=MESH)

    def t2(j, slot):
        return pltpu.make_async_remote_copy(
            src_ref=test_scr.at[b], dst_ref=test_scr.at[slot], send_sem=t2_send.at[j],
            recv_sem=t2_recv.at[slot], device_id=(j, t, s), device_id_type=MESH)

    def b2(j, slot):
        return pltpu.make_async_remote_copy(
            src_ref=build_scr.at[t], dst_ref=build_scr.at[slot], send_sem=b2_send.at[j],
            recv_sem=b2_recv.at[slot], device_id=(b, j, s), device_id_type=MESH)

    for j in range(n_stmt):
        @pl.when(j != s)
        def _():
            t1(j, s).start()
            b1(j, s).start()
    own_test = pltpu.make_async_copy(test_in, test_scr.at[b, s], local_sem.at[0])
    own_build = pltpu.make_async_copy(build_in, build_scr.at[t, s], local_sem.at[1])
    own_test.start()
    own_build.start()
    own_test.wait()
    own_build.wait()
    for j in range(n_stmt):
        @pl.when(j != s)
        def _():
            t1(j, s).wait_send()
            b1(j, s).wait_send()
            t1(j, j).wait_recv()
            b1(j, j).wait_recv()

    for j in range(n_build):
        @pl.when(j != b)
        def _():
            t2(j, b).start()
    for j in range(n_test):
        @pl.when(j != t)
        def _():
            b2(j, t).start()
    for j in range(n_build):
        @pl.when(j != b)
        def _():
            t2(j, b).wait_send()
            t2(j, j).wait_recv()
    for j in range(n_test):
        @pl.when(j != t)
        def _():
            b2(j, t).wait_send()
            b2(j, j).wait_recv()
    test_out[...] = test_scr[...]
    build_out[...] = build_scr[...]


def gather_factors(test_rows, build_rows):
    n_build = lax.axis_size("build")
    n_test = lax.axis_size("test")
    n_stmt = lax.axis_size("stmt")
    vmem = pl.BlockSpec(memory_space=pltpu.VMEM)
    test_shape = (n_build, n_stmt, *test_rows.shape)
    build_shape = (n_test, n_stmt, *build_rows.shape)
    dma = pltpu.SemaphoreType.DMA
    test_pieces, build_pieces = pl.pallas_call(
        functools.partial(gather_kernel, n_build, n_test, n_stmt),
        out_shape=(
            jax.ShapeDtypeStruct(test_shape, test_rows.dtype),
            jax.ShapeDtypeStruct(build_shape, build_rows.dtype),
        ),
        in_specs=[vmem, vmem],
        out_specs=(vmem, vmem),
        scratch_shapes=[
            pltpu.VMEM(test_shape, test_rows.dtype),
            pltpu.VMEM(build_shape, build_rows.dtype),
            dma((2,)),
            dma((n_stmt,)), dma((n_stmt,)), dma((n_stmt,)), dma((n_stmt,)),
            dma((n_build,)), dma((n_build,)), dma((n_test,)), dma((n_test,)),
        ],
        compiler_params=pltpu.CompilerParams(has_side_effects=True, collective_id=0),
    )(test_rows, build_rows)
    return (
        test_pieces.reshape(-1, test_rows.shape[-1]),
        build_pieces.reshape(-1, build_rows.shape[-1]),
    )


def sweep_in_place(a_ref):
    n = a_ref.shape[0]
    lane = lax.broadcasted_iota(jnp.int32, (1, n), 1)

    def step(k, row):
        is_k = lane == k
        pivot = jnp.sum(jnp.where(is_k, row, 0.0), axis=1, keepdims=True)
        inv = 1.0 / pivot
        scaled = jnp.where(is_k, 1.0 - inv, row * inv)
        column = jnp.transpose(jnp.broadcast_to(row, (TILE, n)))
        following = jnp.minimum(k + 1, n - 1)
        next_factor = jnp.sum(jnp.where(lane == following, row, 0.0), axis=1, keepdims=True)
        next_row = a_ref[pl.ds(following, 1), :] - next_factor * scaled
        for h in range(n // TILE):
            lanes = slice(h * TILE, (h + 1) * TILE)
            a_ref[:, lanes] = a_ref[:, lanes] - column * scaled[:, lanes]
        a_ref[pl.ds(k, 1), :] = jnp.where(is_k, -inv, row * inv)
        return next_row

    lax.fori_loop(0, n, step, a_ref[0:1, :], unroll=16)
    a_ref[...] = -a_ref[...]


def tail_kernel(n_build, n_test, part_ref, test_gram_ref, build_gram_ref, owned_ref, inv_ref,
                rs_buf, test_buf, build_buf, product_buf, gram_buf,
                rs_send, rs_recv, test_send, test_recv, build_send, build_recv,
                gram_send, gram_recv):
    b = lax.axis_index("build")
    t = lax.axis_index("test")
    s = lax.axis_index("stmt")
    n_rs = n_build * n_test
    rs_rows = part_ref.shape[0] // n_rs
    g_rows = test_gram_ref.shape[0] // n_test
    me = b * n_test + t

    def rs_copy(m, dst_slot):
        return pltpu.make_async_remote_copy(
            src_ref=part_ref.at[pl.ds(m * rs_rows, rs_rows)], dst_ref=rs_buf.at[dst_slot],
            send_sem=rs_send.at[m], recv_sem=rs_recv.at[dst_slot],
            device_id=(m // n_test, m % n_test, s), device_id_type=MESH)

    def test_copy(j, dst_slot):
        return pltpu.make_async_remote_copy(
            src_ref=test_gram_ref.at[pl.ds(j * g_rows, g_rows)], dst_ref=test_buf.at[dst_slot],
            send_sem=test_send.at[j], recv_sem=test_recv.at[dst_slot],
            device_id=(b, j, s), device_id_type=MESH)

    def build_copy(j, dst_slot):
        return pltpu.make_async_remote_copy(
            src_ref=build_gram_ref.at[pl.ds(t * g_rows, g_rows)], dst_ref=build_buf.at[dst_slot],
            send_sem=build_send.at[j], recv_sem=build_recv.at[dst_slot],
            device_id=(j, t, s), device_id_type=MESH)

    def gram_copy(j, dst_slot):
        return pltpu.make_async_remote_copy(
            src_ref=product_buf, dst_ref=gram_buf.at[dst_slot],
            send_sem=gram_send.at[j], recv_sem=gram_recv.at[dst_slot],
            device_id=(b, j, s), device_id_type=MESH)

    barrier = pltpu.get_barrier_semaphore()
    for m in range(n_rs):
        @pl.when(m != me)
        def _():
            pl.semaphore_signal(barrier, 1, device_id=(m // n_test, m % n_test, s), device_id_type=MESH)
    pl.semaphore_wait(barrier, n_rs - 1)

    for j in range(n_build):
        @pl.when(j != b)
        def _():
            build_copy(j, b).start()
    for j in range(n_test):
        @pl.when(j != t)
        def _():
            test_copy(j, t).start()
    build_buf[pl.ds(b, 1)] = build_gram_ref[pl.ds(pl.multiple_of(t * g_rows, g_rows), g_rows), :][None]
    test_buf[pl.ds(t, 1)] = test_gram_ref[pl.ds(pl.multiple_of(t * g_rows, g_rows), g_rows), :][None]

    for j in range(n_build):
        @pl.when(j != b)
        def _():
            build_copy(j, b).wait_send()
            build_copy(j, j).wait_recv()
    for j in range(n_test):
        @pl.when(j != t)
        def _():
            test_copy(j, t).wait_send()
            test_copy(j, j).wait_recv()

    test_rows = test_buf[0]
    for j in range(1, n_test):
        test_rows = test_rows + test_buf[j]
    build_rows = build_buf[0]
    for j in range(1, n_build):
        build_rows = build_rows + build_buf[j]
    product_buf[...] = test_rows * build_rows

    for j in range(n_test):
        @pl.when(j != t)
        def _():
            gram_copy(j, t).start()
    gram_buf[pl.ds(t, 1)] = product_buf[...][None]
    for j in range(n_test):
        @pl.when(j != t)
        def _():
            gram_copy(j, t).wait_send()
            gram_copy(j, j).wait_recv()
    for j in range(n_test):
        inv_ref[j * g_rows:(j + 1) * g_rows, :] = gram_buf[j]

    for m in range(n_rs):
        @pl.when(m != me)
        def _():
            rs_copy(m, me).start()
    rs_buf[pl.ds(me, 1)] = part_ref[pl.ds(pl.multiple_of(me * rs_rows, rs_rows), rs_rows), :][None]

    sweep_in_place(inv_ref)

    for m in range(n_rs):
        @pl.when(m != me)
        def _():
            rs_copy(m, me).wait_send()
            rs_copy(m, m).wait_recv()
    owned = rs_buf[0]
    for m in range(1, n_rs):
        owned = owned + rs_buf[m]
    owned_ref[...] = owned


def exchange_and_invert(partial, test_gram, build_gram):
    n_build = lax.axis_size("build")
    n_test = lax.axis_size("test")
    n_rs = n_build * n_test
    rows, rank = partial.shape
    rs_rows = rows // n_rs
    g_rows = rank // n_test
    vmem = pl.BlockSpec(memory_space=pltpu.VMEM)
    f32 = jnp.float32
    return pl.pallas_call(
        functools.partial(tail_kernel, n_build, n_test),
        out_shape=(
            jax.ShapeDtypeStruct((rs_rows, rank), f32),
            jax.ShapeDtypeStruct((rank, rank), f32),
        ),
        in_specs=[vmem, vmem, vmem],
        out_specs=(vmem, vmem),
        scratch_shapes=[
            pltpu.VMEM((n_rs, rs_rows, rank), f32),
            pltpu.VMEM((n_test, g_rows, rank), f32),
            pltpu.VMEM((n_build, g_rows, rank), f32),
            pltpu.VMEM((g_rows, rank), f32),
            pltpu.VMEM((n_test, g_rows, rank), f32),
            pltpu.SemaphoreType.DMA((n_rs,)),
            pltpu.SemaphoreType.DMA((n_rs,)),
            pltpu.SemaphoreType.DMA((n_test,)),
            pltpu.SemaphoreType.DMA((n_test,)),
            pltpu.SemaphoreType.DMA((n_build,)),
            pltpu.SemaphoreType.DMA((n_build,)),
            pltpu.SemaphoreType.DMA((n_test,)),
            pltpu.SemaphoreType.DMA((n_test,)),
        ],
        compiler_params=pltpu.CompilerParams(has_side_effects=True, collective_id=1),
    )(partial, test_gram, build_gram)


def mttkrp_kernel(chunk, n_test_blocks, n_stmt_blocks, slot_tests, slot_builds, slot_stmts,
                  live_count, test_ref, build_ref, tile_ref, out_ref, acc_ref):
    q = pl.program_id(0)
    c = pl.program_id(1)
    n_chunks = pl.num_programs(1)

    @pl.when((q == 0) & (c == 0))
    def _():
        out_ref[...] = jnp.zeros_like(out_ref)

    @pl.when(c == 0)
    def _():
        acc_ref[...] = jnp.zeros_like(acc_ref)

    live = q < live_count[0]

    @pl.when(live)
    def _():
        build_block = build_ref[...].astype(jnp.float32)
        total = acc_ref[...]
        for i in range(chunk):
            test_row = test_ref[i : i + 1, :].astype(jnp.float32)
            khatri_rao = (test_row * build_block).astype(jnp.bfloat16)
            total = total + jnp.dot(tile_ref[i], khatri_rao, preferred_element_type=jnp.float32)
        acc_ref[...] = total

    @pl.when(live & (c == n_chunks - 1))
    def _():
        block = jnp.clip(slot_stmts[q], 0, n_stmt_blocks - 1)
        rows = pl.ds(pl.multiple_of(block * TILE, TILE), TILE)
        out_ref[rows, :] += acc_ref[...]


def local_mttkrp(slot_values, slot_tests, slot_builds, slot_stmts, live_count, test_slab, build_slab):
    slots, width = slot_values.shape[0], slot_values.shape[1]
    rank = test_slab.shape[1]
    per_block = width // CHUNK
    n_test_blocks = test_slab.shape[0] // width
    n_build_blocks = build_slab.shape[0] // width

    def test_map(q, c, tests, builds, stmts, count):
        return (jnp.clip(tests[q], 0, n_test_blocks - 1) * per_block + c, 0)

    def build_map(q, c, tests, builds, stmts, count):
        return (jnp.clip(builds[q], 0, n_build_blocks - 1), 0)

    grid_spec = pltpu.PrefetchScalarGridSpec(
        num_scalar_prefetch=4,
        grid=(slots, per_block),
        in_specs=[
            pl.BlockSpec((CHUNK, rank), test_map),
            pl.BlockSpec((width, rank), build_map),
            pl.BlockSpec((None, CHUNK, width, width), lambda q, c, *info: (q, c, 0, 0)),
        ],
        out_specs=pl.BlockSpec((SB * width, rank), lambda q, c, *info: (0, 0)),
        scratch_shapes=[pltpu.VMEM((width, rank), jnp.float32)],
    )
    return pl.pallas_call(
        functools.partial(mttkrp_kernel, CHUNK, n_test_blocks, SB),
        out_shape=jax.ShapeDtypeStruct((SB * width, rank), jnp.float32),
        grid_spec=grid_spec,
    )(slot_tests, slot_builds, slot_stmts, live_count, test_slab, build_slab, slot_values)


def shards(tile_values, tile_test, tile_stmt, tile_build, tile_count, test_factor, build_factor):
    test_slab, build_slab = gather_factors(test_factor[0], build_factor[0])
    slot_values = tile_values[0, 0, 0]
    running_sum = local_mttkrp(
        slot_values, tile_test[0, 0, 0], tile_build[0, 0, 0], tile_stmt[0, 0, 0],
        tile_count[0, 0], test_slab, build_slab)
    slab_test_gram = jnp.dot(test_slab.T, test_slab, preferred_element_type=jnp.float32)
    slab_build_gram = jnp.dot(build_slab.T, build_slab, preferred_element_type=jnp.float32)
    owned_sums, inverse = exchange_and_invert(running_sum, slab_test_gram, slab_build_gram)
    solved = jnp.dot(owned_sums, inverse, precision=lax.Precision.HIGHEST, preferred_element_type=jnp.float32)
    return solved[None]


def solution(mesh):
    return jax.shard_map(
        shards,
        mesh=mesh,
        in_specs=(
            P("build", "test", "stmt", None, None, None, None),
            P("build", "test", "stmt", None),
            P("build", "test", "stmt", None),
            P("build", "test", "stmt", None),
            P("build", "test", "stmt"),
            P("test", ("build", "stmt"), None),
            P("build", ("test", "stmt"), None),
        ),
        out_specs=P("stmt", ("build", "test"), None),
        check_vma=False,
    )
```

```python
import functools

import jax
import jax.numpy as jnp
from jax import lax
from jax.experimental import pallas as pl
from jax.experimental.pallas import tpu as pltpu
from jax.sharding import PartitionSpec as P

TILE = 128
SB = 2
MESH = pl.DeviceIdType.MESH
CHUNK = 32


def gather_kernel(n_build, n_test, n_stmt, test_in, build_in, test_out, build_out,
                  test_scr, build_scr, local_sem, t1_send, t1_recv, b1_send, b1_recv,
                  t2_send, t2_recv, b2_send, b2_recv):
    b = lax.axis_index("build")
    t = lax.axis_index("test")
    s = lax.axis_index("stmt")

    barrier = pltpu.get_barrier_semaphore()
    for j in range(n_stmt):
        @pl.when(j != s)
        def _():
            pl.semaphore_signal(barrier, 1, device_id=(b, t, j), device_id_type=MESH)
    for j in range(n_build):
        @pl.when(j != b)
        def _():
            pl.semaphore_signal(barrier, 1, device_id=(j, t, s), device_id_type=MESH)
    for j in range(n_test):
        @pl.when(j != t)
        def _():
            pl.semaphore_signal(barrier, 1, device_id=(b, j, s), device_id_type=MESH)
    pl.semaphore_wait(barrier, n_stmt + n_build + n_test - 3)

    def t1(j, slot):
        return pltpu.make_async_remote_copy(
            src_ref=test_in, dst_ref=test_scr.at[b, slot], send_sem=t1_send.at[j],
            recv_sem=t1_recv.at[slot], device_id=(b, t, j), device_id_type=MESH)

    def b1(j, slot):
        return pltpu.make_async_remote_copy(
            src_ref=build_in, dst_ref=build_scr.at[t, slot], send_sem=b1_send.at[j],
            recv_sem=b1_recv.at[slot], device_id=(b, t, j), device_id_type=MESH)

    def t2(j, slot):
        return pltpu.make_async_remote_copy(
            src_ref=test_scr.at[b], dst_ref=test_scr.at[slot], send_sem=t2_send.at[j],
            recv_sem=t2_recv.at[slot], device_id=(j, t, s), device_id_type=MESH)

    def b2(j, slot):
        return pltpu.make_async_remote_copy(
            src_ref=build_scr.at[t], dst_ref=build_scr.at[slot], send_sem=b2_send.at[j],
            recv_sem=b2_recv.at[slot], device_id=(b, j, s), device_id_type=MESH)

    for j in range(n_stmt):
        @pl.when(j != s)
        def _():
            t1(j, s).start()
            b1(j, s).start()
    own_test = pltpu.make_async_copy(test_in, test_scr.at[b, s], local_sem.at[0])
    own_build = pltpu.make_async_copy(build_in, build_scr.at[t, s], local_sem.at[1])
    own_test.start()
    own_build.start()
    own_test.wait()
    own_build.wait()
    for j in range(n_stmt):
        @pl.when(j != s)
        def _():
            t1(j, s).wait_send()
            b1(j, s).wait_send()
            t1(j, j).wait_recv()
            b1(j, j).wait_recv()

    for j in range(n_build):
        @pl.when(j != b)
        def _():
            t2(j, b).start()
    for j in range(n_test):
        @pl.when(j != t)
        def _():
            b2(j, t).start()
    for j in range(n_build):
        @pl.when(j != b)
        def _():
            t2(j, b).wait_send()
            t2(j, j).wait_recv()
    for j in range(n_test):
        @pl.when(j != t)
        def _():
            b2(j, t).wait_send()
            b2(j, j).wait_recv()
    test_out[...] = test_scr[...]
    build_out[...] = build_scr[...]


def gather_factors(test_rows, build_rows):
    n_build = lax.axis_size("build")
    n_test = lax.axis_size("test")
    n_stmt = lax.axis_size("stmt")
    vmem = pl.BlockSpec(memory_space=pltpu.VMEM)
    test_shape = (n_build, n_stmt, *test_rows.shape)
    build_shape = (n_test, n_stmt, *build_rows.shape)
    dma = pltpu.SemaphoreType.DMA
    test_pieces, build_pieces = pl.pallas_call(
        functools.partial(gather_kernel, n_build, n_test, n_stmt),
        out_shape=(
            jax.ShapeDtypeStruct(test_shape, test_rows.dtype),
            jax.ShapeDtypeStruct(build_shape, build_rows.dtype),
        ),
        in_specs=[vmem, vmem],
        out_specs=(vmem, vmem),
        scratch_shapes=[
            pltpu.VMEM(test_shape, test_rows.dtype),
            pltpu.VMEM(build_shape, build_rows.dtype),
            dma((2,)),
            dma((n_stmt,)), dma((n_stmt,)), dma((n_stmt,)), dma((n_stmt,)),
            dma((n_build,)), dma((n_build,)), dma((n_test,)), dma((n_test,)),
        ],
        compiler_params=pltpu.CompilerParams(has_side_effects=True, collective_id=0),
    )(test_rows, build_rows)
    return (
        test_pieces.reshape(-1, test_rows.shape[-1]),
        build_pieces.reshape(-1, build_rows.shape[-1]),
    )


def sweep_in_place(a_ref):
    n = a_ref.shape[0]
    lane = lax.broadcasted_iota(jnp.int32, (1, n), 1)

    def step(k, row):
        is_k = lane == k
        pivot = jnp.sum(jnp.where(is_k, row, 0.0), axis=1, keepdims=True)
        inv = 1.0 / pivot
        scaled = jnp.where(is_k, 1.0 - inv, row * inv)
        column = jnp.transpose(jnp.broadcast_to(row, (TILE, n)))
        following = jnp.minimum(k + 1, n - 1)
        next_factor = jnp.sum(jnp.where(lane == following, row, 0.0), axis=1, keepdims=True)
        next_row = a_ref[pl.ds(following, 1), :] - next_factor * scaled
        for h in range(n // TILE):
            lanes = slice(h * TILE, (h + 1) * TILE)
            a_ref[:, lanes] = a_ref[:, lanes] - column * scaled[:, lanes]
        a_ref[pl.ds(k, 1), :] = jnp.where(is_k, -inv, row * inv)
        return next_row

    lax.fori_loop(0, n, step, a_ref[0:1, :], unroll=32)
    a_ref[...] = -a_ref[...]


def tail_kernel(n_build, n_test, part_ref, test_gram_ref, build_gram_ref, owned_ref, inv_ref,
                rs_buf, test_buf, build_buf, product_buf, gram_buf,
                rs_send, rs_recv, test_send, test_recv, build_send, build_recv,
                gram_send, gram_recv):
    b = lax.axis_index("build")
    t = lax.axis_index("test")
    s = lax.axis_index("stmt")
    n_rs = n_build * n_test
    rs_rows = part_ref.shape[0] // n_rs
    g_rows = test_gram_ref.shape[0] // n_test
    me = b * n_test + t

    def rs_copy(m, dst_slot):
        return pltpu.make_async_remote_copy(
            src_ref=part_ref.at[pl.ds(m * rs_rows, rs_rows)], dst_ref=rs_buf.at[dst_slot],
            send_sem=rs_send.at[m], recv_sem=rs_recv.at[dst_slot],
            device_id=(m // n_test, m % n_test, s), device_id_type=MESH)

    def test_copy(j, dst_slot):
        return pltpu.make_async_remote_copy(
            src_ref=test_gram_ref.at[pl.ds(j * g_rows, g_rows)], dst_ref=test_buf.at[dst_slot],
            send_sem=test_send.at[j], recv_sem=test_recv.at[dst_slot],
            device_id=(b, j, s), device_id_type=MESH)

    def build_copy(j, dst_slot):
        return pltpu.make_async_remote_copy(
            src_ref=build_gram_ref.at[pl.ds(t * g_rows, g_rows)], dst_ref=build_buf.at[dst_slot],
            send_sem=build_send.at[j], recv_sem=build_recv.at[dst_slot],
            device_id=(j, t, s), device_id_type=MESH)

    def gram_copy(j, dst_slot):
        return pltpu.make_async_remote_copy(
            src_ref=product_buf, dst_ref=gram_buf.at[dst_slot],
            send_sem=gram_send.at[j], recv_sem=gram_recv.at[dst_slot],
            device_id=(b, j, s), device_id_type=MESH)

    barrier = pltpu.get_barrier_semaphore()
    for m in range(n_rs):
        @pl.when(m != me)
        def _():
            pl.semaphore_signal(barrier, 1, device_id=(m // n_test, m % n_test, s), device_id_type=MESH)
    pl.semaphore_wait(barrier, n_rs - 1)

    for j in range(n_build):
        @pl.when(j != b)
        def _():
            build_copy(j, b).start()
    for j in range(n_test):
        @pl.when(j != t)
        def _():
            test_copy(j, t).start()
    build_buf[pl.ds(b, 1)] = build_gram_ref[pl.ds(pl.multiple_of(t * g_rows, g_rows), g_rows), :][None]
    test_buf[pl.ds(t, 1)] = test_gram_ref[pl.ds(pl.multiple_of(t * g_rows, g_rows), g_rows), :][None]

    for j in range(n_build):
        @pl.when(j != b)
        def _():
            build_copy(j, b).wait_send()
            build_copy(j, j).wait_recv()
    for j in range(n_test):
        @pl.when(j != t)
        def _():
            test_copy(j, t).wait_send()
            test_copy(j, j).wait_recv()

    test_rows = test_buf[0]
    for j in range(1, n_test):
        test_rows = test_rows + test_buf[j]
    build_rows = build_buf[0]
    for j in range(1, n_build):
        build_rows = build_rows + build_buf[j]
    product_buf[...] = test_rows * build_rows

    for j in range(n_test):
        @pl.when(j != t)
        def _():
            gram_copy(j, t).start()
    gram_buf[pl.ds(t, 1)] = product_buf[...][None]
    for j in range(n_test):
        @pl.when(j != t)
        def _():
            gram_copy(j, t).wait_send()
            gram_copy(j, j).wait_recv()
    for j in range(n_test):
        inv_ref[j * g_rows:(j + 1) * g_rows, :] = gram_buf[j]

    for m in range(n_rs):
        @pl.when(m != me)
        def _():
            rs_copy(m, me).start()
    rs_buf[pl.ds(me, 1)] = part_ref[pl.ds(pl.multiple_of(me * rs_rows, rs_rows), rs_rows), :][None]

    sweep_in_place(inv_ref)

    for m in range(n_rs):
        @pl.when(m != me)
        def _():
            rs_copy(m, me).wait_send()
            rs_copy(m, m).wait_recv()
    owned = rs_buf[0]
    for m in range(1, n_rs):
        owned = owned + rs_buf[m]
    owned_ref[...] = owned


def exchange_and_invert(partial, test_gram, build_gram):
    n_build = lax.axis_size("build")
    n_test = lax.axis_size("test")
    n_rs = n_build * n_test
    rows, rank = partial.shape
    rs_rows = rows // n_rs
    g_rows = rank // n_test
    vmem = pl.BlockSpec(memory_space=pltpu.VMEM)
    f32 = jnp.float32
    return pl.pallas_call(
        functools.partial(tail_kernel, n_build, n_test),
        out_shape=(
            jax.ShapeDtypeStruct((rs_rows, rank), f32),
            jax.ShapeDtypeStruct((rank, rank), f32),
        ),
        in_specs=[vmem, vmem, vmem],
        out_specs=(vmem, vmem),
        scratch_shapes=[
            pltpu.VMEM((n_rs, rs_rows, rank), f32),
            pltpu.VMEM((n_test, g_rows, rank), f32),
            pltpu.VMEM((n_build, g_rows, rank), f32),
            pltpu.VMEM((g_rows, rank), f32),
            pltpu.VMEM((n_test, g_rows, rank), f32),
            pltpu.SemaphoreType.DMA((n_rs,)),
            pltpu.SemaphoreType.DMA((n_rs,)),
            pltpu.SemaphoreType.DMA((n_test,)),
            pltpu.SemaphoreType.DMA((n_test,)),
            pltpu.SemaphoreType.DMA((n_build,)),
            pltpu.SemaphoreType.DMA((n_build,)),
            pltpu.SemaphoreType.DMA((n_test,)),
            pltpu.SemaphoreType.DMA((n_test,)),
        ],
        compiler_params=pltpu.CompilerParams(has_side_effects=True, collective_id=1),
    )(partial, test_gram, build_gram)


def mttkrp_kernel(chunk, n_test_blocks, n_stmt_blocks, slot_tests, slot_builds, slot_stmts,
                  live_count, test_ref, build_ref, tile_ref, out_ref, acc_ref):
    q = pl.program_id(0)
    c = pl.program_id(1)
    n_chunks = pl.num_programs(1)

    @pl.when((q == 0) & (c == 0))
    def _():
        out_ref[...] = jnp.zeros_like(out_ref)

    @pl.when(c == 0)
    def _():
        acc_ref[...] = jnp.zeros_like(acc_ref)

    live = q < live_count[0]

    @pl.when(live)
    def _():
        build_block = build_ref[...].astype(jnp.float32)
        total = acc_ref[...]
        for i in range(chunk):
            test_row = test_ref[i : i + 1, :].astype(jnp.float32)
            khatri_rao = (test_row * build_block).astype(jnp.bfloat16)
            total = total + jnp.dot(tile_ref[i], khatri_rao, preferred_element_type=jnp.float32)
        acc_ref[...] = total

    @pl.when(live & (c == n_chunks - 1))
    def _():
        block = jnp.clip(slot_stmts[q], 0, n_stmt_blocks - 1)
        rows = pl.ds(pl.multiple_of(block * TILE, TILE), TILE)
        out_ref[rows, :] += acc_ref[...]


def local_mttkrp(slot_values, slot_tests, slot_builds, slot_stmts, live_count, test_slab, build_slab):
    slots, width = slot_values.shape[0], slot_values.shape[1]
    rank = test_slab.shape[1]
    per_block = width // CHUNK
    n_test_blocks = test_slab.shape[0] // width
    n_build_blocks = build_slab.shape[0] // width

    def test_map(q, c, tests, builds, stmts, count):
        return (jnp.clip(tests[q], 0, n_test_blocks - 1) * per_block + c, 0)

    def build_map(q, c, tests, builds, stmts, count):
        return (jnp.clip(builds[q], 0, n_build_blocks - 1), 0)

    grid_spec = pltpu.PrefetchScalarGridSpec(
        num_scalar_prefetch=4,
        grid=(slots, per_block),
        in_specs=[
            pl.BlockSpec((CHUNK, rank), test_map),
            pl.BlockSpec((width, rank), build_map),
            pl.BlockSpec((None, CHUNK, width, width), lambda q, c, *info: (q, c, 0, 0)),
        ],
        out_specs=pl.BlockSpec((SB * width, rank), lambda q, c, *info: (0, 0)),
        scratch_shapes=[pltpu.VMEM((width, rank), jnp.float32)],
    )
    return pl.pallas_call(
        functools.partial(mttkrp_kernel, CHUNK, n_test_blocks, SB),
        out_shape=jax.ShapeDtypeStruct((SB * width, rank), jnp.float32),
        grid_spec=grid_spec,
    )(slot_tests, slot_builds, slot_stmts, live_count, test_slab, build_slab, slot_values)


def shards(tile_values, tile_test, tile_stmt, tile_build, tile_count, test_factor, build_factor):
    test_slab, build_slab = gather_factors(test_factor[0], build_factor[0])
    slot_values = tile_values[0, 0, 0]
    running_sum = local_mttkrp(
        slot_values, tile_test[0, 0, 0], tile_build[0, 0, 0], tile_stmt[0, 0, 0],
        tile_count[0, 0], test_slab, build_slab)
    slab_test_gram = jnp.dot(test_slab.T, test_slab, preferred_element_type=jnp.float32)
    slab_build_gram = jnp.dot(build_slab.T, build_slab, preferred_element_type=jnp.float32)
    owned_sums, inverse = exchange_and_invert(running_sum, slab_test_gram, slab_build_gram)
    solved = jnp.dot(owned_sums, inverse, precision=lax.Precision.HIGHEST, preferred_element_type=jnp.float32)
    return solved[None]


def solution(mesh):
    return jax.shard_map(
        shards,
        mesh=mesh,
        in_specs=(
            P("build", "test", "stmt", None, None, None, None),
            P("build", "test", "stmt", None),
            P("build", "test", "stmt", None),
            P("build", "test", "stmt", None),
            P("build", "test", "stmt"),
            P("test", ("build", "stmt"), None),
            P("build", ("test", "stmt"), None),
        ),
        out_specs=P("stmt", ("build", "test"), None),
        check_vma=False,
    )
```

```python
import functools

import jax
import jax.numpy as jnp
from jax import lax
from jax.experimental import pallas as pl
from jax.experimental.pallas import tpu as pltpu
from jax.sharding import PartitionSpec as P

TILE = 128
SB = 2
MESH = pl.DeviceIdType.MESH
CHUNK = 32


def gather_kernel(n_build, n_test, n_stmt, test_in, build_in, test_out, build_out,
                  test_scr, build_scr, local_sem, t1_send, t1_recv, b1_send, b1_recv,
                  t2_send, t2_recv, b2_send, b2_recv):
    b = lax.axis_index("build")
    t = lax.axis_index("test")
    s = lax.axis_index("stmt")

    barrier = pltpu.get_barrier_semaphore()
    for j in range(n_stmt):
        @pl.when(j != s)
        def _():
            pl.semaphore_signal(barrier, 1, device_id=(b, t, j), device_id_type=MESH)
    for j in range(n_build):
        @pl.when(j != b)
        def _():
            pl.semaphore_signal(barrier, 1, device_id=(j, t, s), device_id_type=MESH)
    for j in range(n_test):
        @pl.when(j != t)
        def _():
            pl.semaphore_signal(barrier, 1, device_id=(b, j, s), device_id_type=MESH)
    pl.semaphore_wait(barrier, n_stmt + n_build + n_test - 3)

    def t1(j, slot):
        return pltpu.make_async_remote_copy(
            src_ref=test_in, dst_ref=test_scr.at[b, slot], send_sem=t1_send.at[j],
            recv_sem=t1_recv.at[slot], device_id=(b, t, j), device_id_type=MESH)

    def b1(j, slot):
        return pltpu.make_async_remote_copy(
            src_ref=build_in, dst_ref=build_scr.at[t, slot], send_sem=b1_send.at[j],
            recv_sem=b1_recv.at[slot], device_id=(b, t, j), device_id_type=MESH)

    def t2(j, slot):
        return pltpu.make_async_remote_copy(
            src_ref=test_scr.at[b], dst_ref=test_scr.at[slot], send_sem=t2_send.at[j],
            recv_sem=t2_recv.at[slot], device_id=(j, t, s), device_id_type=MESH)

    def b2(j, slot):
        return pltpu.make_async_remote_copy(
            src_ref=build_scr.at[t], dst_ref=build_scr.at[slot], send_sem=b2_send.at[j],
            recv_sem=b2_recv.at[slot], device_id=(b, j, s), device_id_type=MESH)

    for j in range(n_stmt):
        @pl.when(j != s)
        def _():
            t1(j, s).start()
            b1(j, s).start()
    own_test = pltpu.make_async_copy(test_in, test_scr.at[b, s], local_sem.at[0])
    own_build = pltpu.make_async_copy(build_in, build_scr.at[t, s], local_sem.at[1])
    own_test.start()
    own_build.start()
    own_test.wait()
    own_build.wait()
    for j in range(n_stmt):
        @pl.when(j != s)
        def _():
            t1(j, s).wait_send()
            b1(j, s).wait_send()
            t1(j, j).wait_recv()
            b1(j, j).wait_recv()

    for j in range(n_build):
        @pl.when(j != b)
        def _():
            t2(j, b).start()
    for j in range(n_test):
        @pl.when(j != t)
        def _():
            b2(j, t).start()
    for j in range(n_build):
        @pl.when(j != b)
        def _():
            t2(j, b).wait_send()
            t2(j, j).wait_recv()
    for j in range(n_test):
        @pl.when(j != t)
        def _():
            b2(j, t).wait_send()
            b2(j, j).wait_recv()
    test_out[...] = test_scr[...]
    build_out[...] = build_scr[...]


def gather_factors(test_rows, build_rows):
    n_build = lax.axis_size("build")
    n_test = lax.axis_size("test")
    n_stmt = lax.axis_size("stmt")
    vmem = pl.BlockSpec(memory_space=pltpu.VMEM)
    test_shape = (n_build, n_stmt, *test_rows.shape)
    build_shape = (n_test, n_stmt, *build_rows.shape)
    dma = pltpu.SemaphoreType.DMA
    test_pieces, build_pieces = pl.pallas_call(
        functools.partial(gather_kernel, n_build, n_test, n_stmt),
        out_shape=(
            jax.ShapeDtypeStruct(test_shape, test_rows.dtype),
            jax.ShapeDtypeStruct(build_shape, build_rows.dtype),
        ),
        in_specs=[vmem, vmem],
        out_specs=(vmem, vmem),
        scratch_shapes=[
            pltpu.VMEM(test_shape, test_rows.dtype),
            pltpu.VMEM(build_shape, build_rows.dtype),
            dma((2,)),
            dma((n_stmt,)), dma((n_stmt,)), dma((n_stmt,)), dma((n_stmt,)),
            dma((n_build,)), dma((n_build,)), dma((n_test,)), dma((n_test,)),
        ],
        compiler_params=pltpu.CompilerParams(has_side_effects=True, collective_id=0),
    )(test_rows, build_rows)
    return (
        test_pieces.reshape(-1, test_rows.shape[-1]),
        build_pieces.reshape(-1, build_rows.shape[-1]),
    )


def sweep_in_place(a_ref):
    n = a_ref.shape[0]
    lane = lax.broadcasted_iota(jnp.int32, (1, n), 1)

    def step(k, row):
        is_k = lane == k
        pivot = jnp.sum(jnp.where(is_k, row, 0.0), axis=1, keepdims=True)
        inv = 1.0 / pivot
        scaled = jnp.where(is_k, 1.0 - inv, row * inv)
        column = jnp.transpose(jnp.broadcast_to(row, (TILE, n)))
        following = jnp.minimum(k + 1, n - 1)
        next_factor = jnp.sum(jnp.where(lane == following, row, 0.0), axis=1, keepdims=True)
        next_row = a_ref[pl.ds(following, 1), :] - next_factor * scaled
        for h in range(n // TILE):
            lanes = slice(h * TILE, (h + 1) * TILE)
            a_ref[:, lanes] = a_ref[:, lanes] - column * scaled[:, lanes]
        a_ref[pl.ds(k, 1), :] = jnp.where(is_k, -inv, row * inv)
        return next_row

    lax.fori_loop(0, n, step, a_ref[0:1, :], unroll=64)
    a_ref[...] = -a_ref[...]


def tail_kernel(n_build, n_test, part_ref, test_gram_ref, build_gram_ref, owned_ref, inv_ref,
                rs_buf, test_buf, build_buf, product_buf, gram_buf,
                rs_send, rs_recv, test_send, test_recv, build_send, build_recv,
                gram_send, gram_recv):
    b = lax.axis_index("build")
    t = lax.axis_index("test")
    s = lax.axis_index("stmt")
    n_rs = n_build * n_test
    rs_rows = part_ref.shape[0] // n_rs
    g_rows = test_gram_ref.shape[0] // n_test
    me = b * n_test + t

    def rs_copy(m, dst_slot):
        return pltpu.make_async_remote_copy(
            src_ref=part_ref.at[pl.ds(m * rs_rows, rs_rows)], dst_ref=rs_buf.at[dst_slot],
            send_sem=rs_send.at[m], recv_sem=rs_recv.at[dst_slot],
            device_id=(m // n_test, m % n_test, s), device_id_type=MESH)

    def test_copy(j, dst_slot):
        return pltpu.make_async_remote_copy(
            src_ref=test_gram_ref.at[pl.ds(j * g_rows, g_rows)], dst_ref=test_buf.at[dst_slot],
            send_sem=test_send.at[j], recv_sem=test_recv.at[dst_slot],
            device_id=(b, j, s), device_id_type=MESH)

    def build_copy(j, dst_slot):
        return pltpu.make_async_remote_copy(
            src_ref=build_gram_ref.at[pl.ds(t * g_rows, g_rows)], dst_ref=build_buf.at[dst_slot],
            send_sem=build_send.at[j], recv_sem=build_recv.at[dst_slot],
            device_id=(j, t, s), device_id_type=MESH)

    def gram_copy(j, dst_slot):
        return pltpu.make_async_remote_copy(
            src_ref=product_buf, dst_ref=gram_buf.at[dst_slot],
            send_sem=gram_send.at[j], recv_sem=gram_recv.at[dst_slot],
            device_id=(b, j, s), device_id_type=MESH)

    barrier = pltpu.get_barrier_semaphore()
    for m in range(n_rs):
        @pl.when(m != me)
        def _():
            pl.semaphore_signal(barrier, 1, device_id=(m // n_test, m % n_test, s), device_id_type=MESH)
    pl.semaphore_wait(barrier, n_rs - 1)

    for j in range(n_build):
        @pl.when(j != b)
        def _():
            build_copy(j, b).start()
    for j in range(n_test):
        @pl.when(j != t)
        def _():
            test_copy(j, t).start()
    build_buf[pl.ds(b, 1)] = build_gram_ref[pl.ds(pl.multiple_of(t * g_rows, g_rows), g_rows), :][None]
    test_buf[pl.ds(t, 1)] = test_gram_ref[pl.ds(pl.multiple_of(t * g_rows, g_rows), g_rows), :][None]

    for j in range(n_build):
        @pl.when(j != b)
        def _():
            build_copy(j, b).wait_send()
            build_copy(j, j).wait_recv()
    for j in range(n_test):
        @pl.when(j != t)
        def _():
            test_copy(j, t).wait_send()
            test_copy(j, j).wait_recv()

    test_rows = test_buf[0]
    for j in range(1, n_test):
        test_rows = test_rows + test_buf[j]
    build_rows = build_buf[0]
    for j in range(1, n_build):
        build_rows = build_rows + build_buf[j]
    product_buf[...] = test_rows * build_rows

    for j in range(n_test):
        @pl.when(j != t)
        def _():
            gram_copy(j, t).start()
    gram_buf[pl.ds(t, 1)] = product_buf[...][None]
    for j in range(n_test):
        @pl.when(j != t)
        def _():
            gram_copy(j, t).wait_send()
            gram_copy(j, j).wait_recv()
    for j in range(n_test):
        inv_ref[j * g_rows:(j + 1) * g_rows, :] = gram_buf[j]

    for m in range(n_rs):
        @pl.when(m != me)
        def _():
            rs_copy(m, me).start()
    rs_buf[pl.ds(me, 1)] = part_ref[pl.ds(pl.multiple_of(me * rs_rows, rs_rows), rs_rows), :][None]

    sweep_in_place(inv_ref)

    for m in range(n_rs):
        @pl.when(m != me)
        def _():
            rs_copy(m, me).wait_send()
            rs_copy(m, m).wait_recv()
    owned = rs_buf[0]
    for m in range(1, n_rs):
        owned = owned + rs_buf[m]
    owned_ref[...] = owned


def exchange_and_invert(partial, test_gram, build_gram):
    n_build = lax.axis_size("build")
    n_test = lax.axis_size("test")
    n_rs = n_build * n_test
    rows, rank = partial.shape
    rs_rows = rows // n_rs
    g_rows = rank // n_test
    vmem = pl.BlockSpec(memory_space=pltpu.VMEM)
    f32 = jnp.float32
    return pl.pallas_call(
        functools.partial(tail_kernel, n_build, n_test),
        out_shape=(
            jax.ShapeDtypeStruct((rs_rows, rank), f32),
            jax.ShapeDtypeStruct((rank, rank), f32),
        ),
        in_specs=[vmem, vmem, vmem],
        out_specs=(vmem, vmem),
        scratch_shapes=[
            pltpu.VMEM((n_rs, rs_rows, rank), f32),
            pltpu.VMEM((n_test, g_rows, rank), f32),
            pltpu.VMEM((n_build, g_rows, rank), f32),
            pltpu.VMEM((g_rows, rank), f32),
            pltpu.VMEM((n_test, g_rows, rank), f32),
            pltpu.SemaphoreType.DMA((n_rs,)),
            pltpu.SemaphoreType.DMA((n_rs,)),
            pltpu.SemaphoreType.DMA((n_test,)),
            pltpu.SemaphoreType.DMA((n_test,)),
            pltpu.SemaphoreType.DMA((n_build,)),
            pltpu.SemaphoreType.DMA((n_build,)),
            pltpu.SemaphoreType.DMA((n_test,)),
            pltpu.SemaphoreType.DMA((n_test,)),
        ],
        compiler_params=pltpu.CompilerParams(has_side_effects=True, collective_id=1),
    )(partial, test_gram, build_gram)


def mttkrp_kernel(chunk, n_test_blocks, n_stmt_blocks, slot_tests, slot_builds, slot_stmts,
                  live_count, test_ref, build_ref, tile_ref, out_ref, acc_ref):
    q = pl.program_id(0)
    c = pl.program_id(1)
    n_chunks = pl.num_programs(1)

    @pl.when((q == 0) & (c == 0))
    def _():
        out_ref[...] = jnp.zeros_like(out_ref)

    @pl.when(c == 0)
    def _():
        acc_ref[...] = jnp.zeros_like(acc_ref)

    live = q < live_count[0]

    @pl.when(live)
    def _():
        build_block = build_ref[...].astype(jnp.float32)
        total = acc_ref[...]
        for i in range(chunk):
            test_row = test_ref[i : i + 1, :].astype(jnp.float32)
            khatri_rao = (test_row * build_block).astype(jnp.bfloat16)
            total = total + jnp.dot(tile_ref[i], khatri_rao, preferred_element_type=jnp.float32)
        acc_ref[...] = total

    @pl.when(live & (c == n_chunks - 1))
    def _():
        block = jnp.clip(slot_stmts[q], 0, n_stmt_blocks - 1)
        rows = pl.ds(pl.multiple_of(block * TILE, TILE), TILE)
        out_ref[rows, :] += acc_ref[...]


def local_mttkrp(slot_values, slot_tests, slot_builds, slot_stmts, live_count, test_slab, build_slab):
    slots, width = slot_values.shape[0], slot_values.shape[1]
    rank = test_slab.shape[1]
    per_block = width // CHUNK
    n_test_blocks = test_slab.shape[0] // width
    n_build_blocks = build_slab.shape[0] // width

    def test_map(q, c, tests, builds, stmts, count):
        return (jnp.clip(tests[q], 0, n_test_blocks - 1) * per_block + c, 0)

    def build_map(q, c, tests, builds, stmts, count):
        return (jnp.clip(builds[q], 0, n_build_blocks - 1), 0)

    grid_spec = pltpu.PrefetchScalarGridSpec(
        num_scalar_prefetch=4,
        grid=(slots, per_block),
        in_specs=[
            pl.BlockSpec((CHUNK, rank), test_map),
            pl.BlockSpec((width, rank), build_map),
            pl.BlockSpec((None, CHUNK, width, width), lambda q, c, *info: (q, c, 0, 0)),
        ],
        out_specs=pl.BlockSpec((SB * width, rank), lambda q, c, *info: (0, 0)),
        scratch_shapes=[pltpu.VMEM((width, rank), jnp.float32)],
    )
    return pl.pallas_call(
        functools.partial(mttkrp_kernel, CHUNK, n_test_blocks, SB),
        out_shape=jax.ShapeDtypeStruct((SB * width, rank), jnp.float32),
        grid_spec=grid_spec,
    )(slot_tests, slot_builds, slot_stmts, live_count, test_slab, build_slab, slot_values)


def shards(tile_values, tile_test, tile_stmt, tile_build, tile_count, test_factor, build_factor):
    test_slab, build_slab = gather_factors(test_factor[0], build_factor[0])
    slot_values = tile_values[0, 0, 0]
    running_sum = local_mttkrp(
        slot_values, tile_test[0, 0, 0], tile_build[0, 0, 0], tile_stmt[0, 0, 0],
        tile_count[0, 0], test_slab, build_slab)
    slab_test_gram = jnp.dot(test_slab.T, test_slab, preferred_element_type=jnp.float32)
    slab_build_gram = jnp.dot(build_slab.T, build_slab, preferred_element_type=jnp.float32)
    owned_sums, inverse = exchange_and_invert(running_sum, slab_test_gram, slab_build_gram)
    solved = jnp.dot(owned_sums, inverse, precision=lax.Precision.HIGHEST, preferred_element_type=jnp.float32)
    return solved[None]


def solution(mesh):
    return jax.shard_map(
        shards,
        mesh=mesh,
        in_specs=(
            P("build", "test", "stmt", None, None, None, None),
            P("build", "test", "stmt", None),
            P("build", "test", "stmt", None),
            P("build", "test", "stmt", None),
            P("build", "test", "stmt"),
            P("test", ("build", "stmt"), None),
            P("build", ("test", "stmt"), None),
        ),
        out_specs=P("stmt", ("build", "test"), None),
        check_vma=False,
    )
```

```python
import functools

import jax
import jax.numpy as jnp
from jax import lax
from jax.experimental import pallas as pl
from jax.experimental.pallas import tpu as pltpu
from jax.sharding import PartitionSpec as P

TILE = 128
SB = 2
MESH = pl.DeviceIdType.MESH
CHUNK = 32


def gather_kernel(n_build, n_test, n_stmt, test_in, build_in, test_out, build_out,
                  test_scr, build_scr, local_sem, t1_send, t1_recv, b1_send, b1_recv,
                  t2_send, t2_recv, b2_send, b2_recv):
    b = lax.axis_index("build")
    t = lax.axis_index("test")
    s = lax.axis_index("stmt")

    barrier = pltpu.get_barrier_semaphore()
    for j in range(n_stmt):
        @pl.when(j != s)
        def _():
            pl.semaphore_signal(barrier, 1, device_id=(b, t, j), device_id_type=MESH)
    for j in range(n_build):
        @pl.when(j != b)
        def _():
            pl.semaphore_signal(barrier, 1, device_id=(j, t, s), device_id_type=MESH)
    for j in range(n_test):
        @pl.when(j != t)
        def _():
            pl.semaphore_signal(barrier, 1, device_id=(b, j, s), device_id_type=MESH)
    pl.semaphore_wait(barrier, n_stmt + n_build + n_test - 3)

    def t1(j, slot):
        return pltpu.make_async_remote_copy(
            src_ref=test_in, dst_ref=test_scr.at[b, slot], send_sem=t1_send.at[j],
            recv_sem=t1_recv.at[slot], device_id=(b, t, j), device_id_type=MESH)

    def b1(j, slot):
        return pltpu.make_async_remote_copy(
            src_ref=build_in, dst_ref=build_scr.at[t, slot], send_sem=b1_send.at[j],
            recv_sem=b1_recv.at[slot], device_id=(b, t, j), device_id_type=MESH)

    def t2(j, slot):
        return pltpu.make_async_remote_copy(
            src_ref=test_scr.at[b], dst_ref=test_scr.at[slot], send_sem=t2_send.at[j],
            recv_sem=t2_recv.at[slot], device_id=(j, t, s), device_id_type=MESH)

    def b2(j, slot):
        return pltpu.make_async_remote_copy(
            src_ref=build_scr.at[t], dst_ref=build_scr.at[slot], send_sem=b2_send.at[j],
            recv_sem=b2_recv.at[slot], device_id=(b, j, s), device_id_type=MESH)

    for j in range(n_stmt):
        @pl.when(j != s)
        def _():
            t1(j, s).start()
            b1(j, s).start()
    own_test = pltpu.make_async_copy(test_in, test_scr.at[b, s], local_sem.at[0])
    own_build = pltpu.make_async_copy(build_in, build_scr.at[t, s], local_sem.at[1])
    own_test.start()
    own_build.start()
    own_test.wait()
    own_build.wait()
    for j in range(n_stmt):
        @pl.when(j != s)
        def _():
            t1(j, s).wait_send()
            b1(j, s).wait_send()
            t1(j, j).wait_recv()
            b1(j, j).wait_recv()

    for j in range(n_build):
        @pl.when(j != b)
        def _():
            t2(j, b).start()
    for j in range(n_test):
        @pl.when(j != t)
        def _():
            b2(j, t).start()
    for j in range(n_build):
        @pl.when(j != b)
        def _():
            t2(j, b).wait_send()
            t2(j, j).wait_recv()
    for j in range(n_test):
        @pl.when(j != t)
        def _():
            b2(j, t).wait_send()
            b2(j, j).wait_recv()
    test_out[...] = test_scr[...]
    build_out[...] = build_scr[...]


def gather_factors(test_rows, build_rows):
    n_build = lax.axis_size("build")
    n_test = lax.axis_size("test")
    n_stmt = lax.axis_size("stmt")
    vmem = pl.BlockSpec(memory_space=pltpu.VMEM)
    test_shape = (n_build, n_stmt, *test_rows.shape)
    build_shape = (n_test, n_stmt, *build_rows.shape)
    dma = pltpu.SemaphoreType.DMA
    test_pieces, build_pieces = pl.pallas_call(
        functools.partial(gather_kernel, n_build, n_test, n_stmt),
        out_shape=(
            jax.ShapeDtypeStruct(test_shape, test_rows.dtype),
            jax.ShapeDtypeStruct(build_shape, build_rows.dtype),
        ),
        in_specs=[vmem, vmem],
        out_specs=(vmem, vmem),
        scratch_shapes=[
            pltpu.VMEM(test_shape, test_rows.dtype),
            pltpu.VMEM(build_shape, build_rows.dtype),
            dma((2,)),
            dma((n_stmt,)), dma((n_stmt,)), dma((n_stmt,)), dma((n_stmt,)),
            dma((n_build,)), dma((n_build,)), dma((n_test,)), dma((n_test,)),
        ],
        compiler_params=pltpu.CompilerParams(has_side_effects=True, collective_id=0),
    )(test_rows, build_rows)
    return (
        test_pieces.reshape(-1, test_rows.shape[-1]),
        build_pieces.reshape(-1, build_rows.shape[-1]),
    )


def sweep_in_place(a_ref):
    n = a_ref.shape[0]
    lane = lax.broadcasted_iota(jnp.int32, (1, n), 1)

    def step(k, row):
        is_k = lane == k
        pivot = jnp.sum(jnp.where(is_k, row, 0.0), axis=1, keepdims=True)
        inv = 1.0 / pivot
        scaled = jnp.where(is_k, 1.0 - inv, row * inv)
        column = jnp.transpose(jnp.broadcast_to(row, (TILE, n)))
        following = jnp.minimum(k + 1, n - 1)
        next_factor = jnp.sum(jnp.where(lane == following, row, 0.0), axis=1, keepdims=True)
        next_row = a_ref[pl.ds(following, 1), :] - next_factor * scaled
        for h in range(n // TILE):
            lanes = slice(h * TILE, (h + 1) * TILE)
            a_ref[:, lanes] = a_ref[:, lanes] - column * scaled[:, lanes]
        a_ref[pl.ds(k, 1), :] = jnp.where(is_k, -inv, row * inv)
        return next_row

    lax.fori_loop(0, n, step, a_ref[0:1, :], unroll=128)
    a_ref[...] = -a_ref[...]


def tail_kernel(n_build, n_test, part_ref, test_gram_ref, build_gram_ref, owned_ref, inv_ref,
                rs_buf, test_buf, build_buf, product_buf, gram_buf,
                rs_send, rs_recv, test_send, test_recv, build_send, build_recv,
                gram_send, gram_recv):
    b = lax.axis_index("build")
    t = lax.axis_index("test")
    s = lax.axis_index("stmt")
    n_rs = n_build * n_test
    rs_rows = part_ref.shape[0] // n_rs
    g_rows = test_gram_ref.shape[0] // n_test
    me = b * n_test + t

    def rs_copy(m, dst_slot):
        return pltpu.make_async_remote_copy(
            src_ref=part_ref.at[pl.ds(m * rs_rows, rs_rows)], dst_ref=rs_buf.at[dst_slot],
            send_sem=rs_send.at[m], recv_sem=rs_recv.at[dst_slot],
            device_id=(m // n_test, m % n_test, s), device_id_type=MESH)

    def test_copy(j, dst_slot):
        return pltpu.make_async_remote_copy(
            src_ref=test_gram_ref.at[pl.ds(j * g_rows, g_rows)], dst_ref=test_buf.at[dst_slot],
            send_sem=test_send.at[j], recv_sem=test_recv.at[dst_slot],
            device_id=(b, j, s), device_id_type=MESH)

    def build_copy(j, dst_slot):
        return pltpu.make_async_remote_copy(
            src_ref=build_gram_ref.at[pl.ds(t * g_rows, g_rows)], dst_ref=build_buf.at[dst_slot],
            send_sem=build_send.at[j], recv_sem=build_recv.at[dst_slot],
            device_id=(j, t, s), device_id_type=MESH)

    def gram_copy(j, dst_slot):
        return pltpu.make_async_remote_copy(
            src_ref=product_buf, dst_ref=gram_buf.at[dst_slot],
            send_sem=gram_send.at[j], recv_sem=gram_recv.at[dst_slot],
            device_id=(b, j, s), device_id_type=MESH)

    barrier = pltpu.get_barrier_semaphore()
    for m in range(n_rs):
        @pl.when(m != me)
        def _():
            pl.semaphore_signal(barrier, 1, device_id=(m // n_test, m % n_test, s), device_id_type=MESH)
    pl.semaphore_wait(barrier, n_rs - 1)

    for j in range(n_build):
        @pl.when(j != b)
        def _():
            build_copy(j, b).start()
    for j in range(n_test):
        @pl.when(j != t)
        def _():
            test_copy(j, t).start()
    build_buf[pl.ds(b, 1)] = build_gram_ref[pl.ds(pl.multiple_of(t * g_rows, g_rows), g_rows), :][None]
    test_buf[pl.ds(t, 1)] = test_gram_ref[pl.ds(pl.multiple_of(t * g_rows, g_rows), g_rows), :][None]

    for j in range(n_build):
        @pl.when(j != b)
        def _():
            build_copy(j, b).wait_send()
            build_copy(j, j).wait_recv()
    for j in range(n_test):
        @pl.when(j != t)
        def _():
            test_copy(j, t).wait_send()
            test_copy(j, j).wait_recv()

    test_rows = test_buf[0]
    for j in range(1, n_test):
        test_rows = test_rows + test_buf[j]
    build_rows = build_buf[0]
    for j in range(1, n_build):
        build_rows = build_rows + build_buf[j]
    product_buf[...] = test_rows * build_rows

    for j in range(n_test):
        @pl.when(j != t)
        def _():
            gram_copy(j, t).start()
    gram_buf[pl.ds(t, 1)] = product_buf[...][None]
    for j in range(n_test):
        @pl.when(j != t)
        def _():
            gram_copy(j, t).wait_send()
            gram_copy(j, j).wait_recv()
    for j in range(n_test):
        inv_ref[j * g_rows:(j + 1) * g_rows, :] = gram_buf[j]

    for m in range(n_rs):
        @pl.when(m != me)
        def _():
            rs_copy(m, me).start()
    rs_buf[pl.ds(me, 1)] = part_ref[pl.ds(pl.multiple_of(me * rs_rows, rs_rows), rs_rows), :][None]

    sweep_in_place(inv_ref)

    for m in range(n_rs):
        @pl.when(m != me)
        def _():
            rs_copy(m, me).wait_send()
            rs_copy(m, m).wait_recv()
    owned = rs_buf[0]
    for m in range(1, n_rs):
        owned = owned + rs_buf[m]
    owned_ref[...] = owned


def exchange_and_invert(partial, test_gram, build_gram):
    n_build = lax.axis_size("build")
    n_test = lax.axis_size("test")
    n_rs = n_build * n_test
    rows, rank = partial.shape
    rs_rows = rows // n_rs
    g_rows = rank // n_test
    vmem = pl.BlockSpec(memory_space=pltpu.VMEM)
    f32 = jnp.float32
    return pl.pallas_call(
        functools.partial(tail_kernel, n_build, n_test),
        out_shape=(
            jax.ShapeDtypeStruct((rs_rows, rank), f32),
            jax.ShapeDtypeStruct((rank, rank), f32),
        ),
        in_specs=[vmem, vmem, vmem],
        out_specs=(vmem, vmem),
        scratch_shapes=[
            pltpu.VMEM((n_rs, rs_rows, rank), f32),
            pltpu.VMEM((n_test, g_rows, rank), f32),
            pltpu.VMEM((n_build, g_rows, rank), f32),
            pltpu.VMEM((g_rows, rank), f32),
            pltpu.VMEM((n_test, g_rows, rank), f32),
            pltpu.SemaphoreType.DMA((n_rs,)),
            pltpu.SemaphoreType.DMA((n_rs,)),
            pltpu.SemaphoreType.DMA((n_test,)),
            pltpu.SemaphoreType.DMA((n_test,)),
            pltpu.SemaphoreType.DMA((n_build,)),
            pltpu.SemaphoreType.DMA((n_build,)),
            pltpu.SemaphoreType.DMA((n_test,)),
            pltpu.SemaphoreType.DMA((n_test,)),
        ],
        compiler_params=pltpu.CompilerParams(has_side_effects=True, collective_id=1),
    )(partial, test_gram, build_gram)


def mttkrp_kernel(chunk, n_test_blocks, n_stmt_blocks, slot_tests, slot_builds, slot_stmts,
                  live_count, test_ref, build_ref, tile_ref, out_ref, acc_ref):
    q = pl.program_id(0)
    c = pl.program_id(1)
    n_chunks = pl.num_programs(1)

    @pl.when((q == 0) & (c == 0))
    def _():
        out_ref[...] = jnp.zeros_like(out_ref)

    @pl.when(c == 0)
    def _():
        acc_ref[...] = jnp.zeros_like(acc_ref)

    live = q < live_count[0]

    @pl.when(live)
    def _():
        build_block = build_ref[...].astype(jnp.float32)
        total = acc_ref[...]
        for i in range(chunk):
            test_row = test_ref[i : i + 1, :].astype(jnp.float32)
            khatri_rao = (test_row * build_block).astype(jnp.bfloat16)
            total = total + jnp.dot(tile_ref[i], khatri_rao, preferred_element_type=jnp.float32)
        acc_ref[...] = total

    @pl.when(live & (c == n_chunks - 1))
    def _():
        block = jnp.clip(slot_stmts[q], 0, n_stmt_blocks - 1)
        rows = pl.ds(pl.multiple_of(block * TILE, TILE), TILE)
        out_ref[rows, :] += acc_ref[...]


def local_mttkrp(slot_values, slot_tests, slot_builds, slot_stmts, live_count, test_slab, build_slab):
    slots, width = slot_values.shape[0], slot_values.shape[1]
    rank = test_slab.shape[1]
    per_block = width // CHUNK
    n_test_blocks = test_slab.shape[0] // width
    n_build_blocks = build_slab.shape[0] // width

    def test_map(q, c, tests, builds, stmts, count):
        return (jnp.clip(tests[q], 0, n_test_blocks - 1) * per_block + c, 0)

    def build_map(q, c, tests, builds, stmts, count):
        return (jnp.clip(builds[q], 0, n_build_blocks - 1), 0)

    grid_spec = pltpu.PrefetchScalarGridSpec(
        num_scalar_prefetch=4,
        grid=(slots, per_block),
        in_specs=[
            pl.BlockSpec((CHUNK, rank), test_map),
            pl.BlockSpec((width, rank), build_map),
            pl.BlockSpec((None, CHUNK, width, width), lambda q, c, *info: (q, c, 0, 0)),
        ],
        out_specs=pl.BlockSpec((SB * width, rank), lambda q, c, *info: (0, 0)),
        scratch_shapes=[pltpu.VMEM((width, rank), jnp.float32)],
    )
    return pl.pallas_call(
        functools.partial(mttkrp_kernel, CHUNK, n_test_blocks, SB),
        out_shape=jax.ShapeDtypeStruct((SB * width, rank), jnp.float32),
        grid_spec=grid_spec,
    )(slot_tests, slot_builds, slot_stmts, live_count, test_slab, build_slab, slot_values)


def shards(tile_values, tile_test, tile_stmt, tile_build, tile_count, test_factor, build_factor):
    test_slab, build_slab = gather_factors(test_factor[0], build_factor[0])
    slot_values = tile_values[0, 0, 0]
    running_sum = local_mttkrp(
        slot_values, tile_test[0, 0, 0], tile_build[0, 0, 0], tile_stmt[0, 0, 0],
        tile_count[0, 0], test_slab, build_slab)
    slab_test_gram = jnp.dot(test_slab.T, test_slab, preferred_element_type=jnp.float32)
    slab_build_gram = jnp.dot(build_slab.T, build_slab, preferred_element_type=jnp.float32)
    owned_sums, inverse = exchange_and_invert(running_sum, slab_test_gram, slab_build_gram)
    solved = jnp.dot(owned_sums, inverse, precision=lax.Precision.HIGHEST, preferred_element_type=jnp.float32)
    return solved[None]


def solution(mesh):
    return jax.shard_map(
        shards,
        mesh=mesh,
        in_specs=(
            P("build", "test", "stmt", None, None, None, None),
            P("build", "test", "stmt", None),
            P("build", "test", "stmt", None),
            P("build", "test", "stmt", None),
            P("build", "test", "stmt"),
            P("test", ("build", "stmt"), None),
            P("build", ("test", "stmt"), None),
        ),
        out_specs=P("stmt", ("build", "test"), None),
        check_vma=False,
    )
```

```python
import functools

import jax
import jax.numpy as jnp
from jax import lax
from jax.experimental import pallas as pl
from jax.experimental.pallas import tpu as pltpu
from jax.sharding import PartitionSpec as P

TILE = 128
SB = 2
MESH = pl.DeviceIdType.MESH
CHUNK = 64


def gather_kernel(n_build, n_test, n_stmt, test_in, build_in, test_out, build_out,
                  test_scr, build_scr, local_sem, t1_send, t1_recv, b1_send, b1_recv,
                  t2_send, t2_recv, b2_send, b2_recv):
    b = lax.axis_index("build")
    t = lax.axis_index("test")
    s = lax.axis_index("stmt")

    barrier = pltpu.get_barrier_semaphore()
    for j in range(n_stmt):
        @pl.when(j != s)
        def _():
            pl.semaphore_signal(barrier, 1, device_id=(b, t, j), device_id_type=MESH)
    for j in range(n_build):
        @pl.when(j != b)
        def _():
            pl.semaphore_signal(barrier, 1, device_id=(j, t, s), device_id_type=MESH)
    for j in range(n_test):
        @pl.when(j != t)
        def _():
            pl.semaphore_signal(barrier, 1, device_id=(b, j, s), device_id_type=MESH)
    pl.semaphore_wait(barrier, n_stmt + n_build + n_test - 3)

    def t1(j, slot):
        return pltpu.make_async_remote_copy(
            src_ref=test_in, dst_ref=test_scr.at[b, slot], send_sem=t1_send.at[j],
            recv_sem=t1_recv.at[slot], device_id=(b, t, j), device_id_type=MESH)

    def b1(j, slot):
        return pltpu.make_async_remote_copy(
            src_ref=build_in, dst_ref=build_scr.at[t, slot], send_sem=b1_send.at[j],
            recv_sem=b1_recv.at[slot], device_id=(b, t, j), device_id_type=MESH)

    def t2(j, slot):
        return pltpu.make_async_remote_copy(
            src_ref=test_scr.at[b], dst_ref=test_scr.at[slot], send_sem=t2_send.at[j],
            recv_sem=t2_recv.at[slot], device_id=(j, t, s), device_id_type=MESH)

    def b2(j, slot):
        return pltpu.make_async_remote_copy(
            src_ref=build_scr.at[t], dst_ref=build_scr.at[slot], send_sem=b2_send.at[j],
            recv_sem=b2_recv.at[slot], device_id=(b, j, s), device_id_type=MESH)

    for j in range(n_stmt):
        @pl.when(j != s)
        def _():
            t1(j, s).start()
            b1(j, s).start()
    own_test = pltpu.make_async_copy(test_in, test_scr.at[b, s], local_sem.at[0])
    own_build = pltpu.make_async_copy(build_in, build_scr.at[t, s], local_sem.at[1])
    own_test.start()
    own_build.start()
    own_test.wait()
    own_build.wait()
    for j in range(n_stmt):
        @pl.when(j != s)
        def _():
            t1(j, s).wait_send()
            b1(j, s).wait_send()
            t1(j, j).wait_recv()
            b1(j, j).wait_recv()

    for j in range(n_build):
        @pl.when(j != b)
        def _():
            t2(j, b).start()
    for j in range(n_test):
        @pl.when(j != t)
        def _():
            b2(j, t).start()
    for j in range(n_build):
        @pl.when(j != b)
        def _():
            t2(j, b).wait_send()
            t2(j, j).wait_recv()
    for j in range(n_test):
        @pl.when(j != t)
        def _():
            b2(j, t).wait_send()
            b2(j, j).wait_recv()
    test_out[...] = test_scr[...]
    build_out[...] = build_scr[...]


def gather_factors(test_rows, build_rows):
    n_build = lax.axis_size("build")
    n_test = lax.axis_size("test")
    n_stmt = lax.axis_size("stmt")
    vmem = pl.BlockSpec(memory_space=pltpu.VMEM)
    test_shape = (n_build, n_stmt, *test_rows.shape)
    build_shape = (n_test, n_stmt, *build_rows.shape)
    dma = pltpu.SemaphoreType.DMA
    test_pieces, build_pieces = pl.pallas_call(
        functools.partial(gather_kernel, n_build, n_test, n_stmt),
        out_shape=(
            jax.ShapeDtypeStruct(test_shape, test_rows.dtype),
            jax.ShapeDtypeStruct(build_shape, build_rows.dtype),
        ),
        in_specs=[vmem, vmem],
        out_specs=(vmem, vmem),
        scratch_shapes=[
            pltpu.VMEM(test_shape, test_rows.dtype),
            pltpu.VMEM(build_shape, build_rows.dtype),
            dma((2,)),
            dma((n_stmt,)), dma((n_stmt,)), dma((n_stmt,)), dma((n_stmt,)),
            dma((n_build,)), dma((n_build,)), dma((n_test,)), dma((n_test,)),
        ],
        compiler_params=pltpu.CompilerParams(has_side_effects=True, collective_id=0),
    )(test_rows, build_rows)
    return (
        test_pieces.reshape(-1, test_rows.shape[-1]),
        build_pieces.reshape(-1, build_rows.shape[-1]),
    )


def sweep_in_place(a_ref):
    n = a_ref.shape[0]
    lane = lax.broadcasted_iota(jnp.int32, (1, n), 1)

    def step(k, row):
        is_k = lane == k
        pivot = jnp.sum(jnp.where(is_k, row, 0.0), axis=1, keepdims=True)
        inv = 1.0 / pivot
        scaled = jnp.where(is_k, 1.0 - inv, row * inv)
        column = jnp.transpose(jnp.broadcast_to(row, (TILE, n)))
        following = jnp.minimum(k + 1, n - 1)
        next_factor = jnp.sum(jnp.where(lane == following, row, 0.0), axis=1, keepdims=True)
        next_row = a_ref[pl.ds(following, 1), :] - next_factor * scaled
        for h in range(n // TILE):
            lanes = slice(h * TILE, (h + 1) * TILE)
            a_ref[:, lanes] = a_ref[:, lanes] - column * scaled[:, lanes]
        a_ref[pl.ds(k, 1), :] = jnp.where(is_k, -inv, row * inv)
        return next_row

    lax.fori_loop(0, n, step, a_ref[0:1, :], unroll=128)
    a_ref[...] = -a_ref[...]


def tail_kernel(n_build, n_test, part_ref, test_gram_ref, build_gram_ref, owned_ref, inv_ref,
                rs_buf, test_buf, build_buf, product_buf, gram_buf,
                rs_send, rs_recv, test_send, test_recv, build_send, build_recv,
                gram_send, gram_recv):
    b = lax.axis_index("build")
    t = lax.axis_index("test")
    s = lax.axis_index("stmt")
    n_rs = n_build * n_test
    rs_rows = part_ref.shape[0] // n_rs
    g_rows = test_gram_ref.shape[0] // n_test
    me = b * n_test + t

    def rs_copy(m, dst_slot):
        return pltpu.make_async_remote_copy(
            src_ref=part_ref.at[pl.ds(m * rs_rows, rs_rows)], dst_ref=rs_buf.at[dst_slot],
            send_sem=rs_send.at[m], recv_sem=rs_recv.at[dst_slot],
            device_id=(m // n_test, m % n_test, s), device_id_type=MESH)

    def test_copy(j, dst_slot):
        return pltpu.make_async_remote_copy(
            src_ref=test_gram_ref.at[pl.ds(j * g_rows, g_rows)], dst_ref=test_buf.at[dst_slot],
            send_sem=test_send.at[j], recv_sem=test_recv.at[dst_slot],
            device_id=(b, j, s), device_id_type=MESH)

    def build_copy(j, dst_slot):
        return pltpu.make_async_remote_copy(
            src_ref=build_gram_ref.at[pl.ds(t * g_rows, g_rows)], dst_ref=build_buf.at[dst_slot],
            send_sem=build_send.at[j], recv_sem=build_recv.at[dst_slot],
            device_id=(j, t, s), device_id_type=MESH)

    def gram_copy(j, dst_slot):
        return pltpu.make_async_remote_copy(
            src_ref=product_buf, dst_ref=gram_buf.at[dst_slot],
            send_sem=gram_send.at[j], recv_sem=gram_recv.at[dst_slot],
            device_id=(b, j, s), device_id_type=MESH)

    barrier = pltpu.get_barrier_semaphore()
    for m in range(n_rs):
        @pl.when(m != me)
        def _():
            pl.semaphore_signal(barrier, 1, device_id=(m // n_test, m % n_test, s), device_id_type=MESH)
    pl.semaphore_wait(barrier, n_rs - 1)

    for j in range(n_build):
        @pl.when(j != b)
        def _():
            build_copy(j, b).start()
    for j in range(n_test):
        @pl.when(j != t)
        def _():
            test_copy(j, t).start()
    build_buf[pl.ds(b, 1)] = build_gram_ref[pl.ds(pl.multiple_of(t * g_rows, g_rows), g_rows), :][None]
    test_buf[pl.ds(t, 1)] = test_gram_ref[pl.ds(pl.multiple_of(t * g_rows, g_rows), g_rows), :][None]

    for j in range(n_build):
        @pl.when(j != b)
        def _():
            build_copy(j, b).wait_send()
            build_copy(j, j).wait_recv()
    for j in range(n_test):
        @pl.when(j != t)
        def _():
            test_copy(j, t).wait_send()
            test_copy(j, j).wait_recv()

    test_rows = test_buf[0]
    for j in range(1, n_test):
        test_rows = test_rows + test_buf[j]
    build_rows = build_buf[0]
    for j in range(1, n_build):
        build_rows = build_rows + build_buf[j]
    product_buf[...] = test_rows * build_rows

    for j in range(n_test):
        @pl.when(j != t)
        def _():
            gram_copy(j, t).start()
    gram_buf[pl.ds(t, 1)] = product_buf[...][None]
    for j in range(n_test):
        @pl.when(j != t)
        def _():
            gram_copy(j, t).wait_send()
            gram_copy(j, j).wait_recv()
    for j in range(n_test):
        inv_ref[j * g_rows:(j + 1) * g_rows, :] = gram_buf[j]

    for m in range(n_rs):
        @pl.when(m != me)
        def _():
            rs_copy(m, me).start()
    rs_buf[pl.ds(me, 1)] = part_ref[pl.ds(pl.multiple_of(me * rs_rows, rs_rows), rs_rows), :][None]

    sweep_in_place(inv_ref)

    for m in range(n_rs):
        @pl.when(m != me)
        def _():
            rs_copy(m, me).wait_send()
            rs_copy(m, m).wait_recv()
    owned = rs_buf[0]
    for m in range(1, n_rs):
        owned = owned + rs_buf[m]
    owned_ref[...] = owned


def exchange_and_invert(partial, test_gram, build_gram):
    n_build = lax.axis_size("build")
    n_test = lax.axis_size("test")
    n_rs = n_build * n_test
    rows, rank = partial.shape
    rs_rows = rows // n_rs
    g_rows = rank // n_test
    vmem = pl.BlockSpec(memory_space=pltpu.VMEM)
    f32 = jnp.float32
    return pl.pallas_call(
        functools.partial(tail_kernel, n_build, n_test),
        out_shape=(
            jax.ShapeDtypeStruct((rs_rows, rank), f32),
            jax.ShapeDtypeStruct((rank, rank), f32),
        ),
        in_specs=[vmem, vmem, vmem],
        out_specs=(vmem, vmem),
        scratch_shapes=[
            pltpu.VMEM((n_rs, rs_rows, rank), f32),
            pltpu.VMEM((n_test, g_rows, rank), f32),
            pltpu.VMEM((n_build, g_rows, rank), f32),
            pltpu.VMEM((g_rows, rank), f32),
            pltpu.VMEM((n_test, g_rows, rank), f32),
            pltpu.SemaphoreType.DMA((n_rs,)),
            pltpu.SemaphoreType.DMA((n_rs,)),
            pltpu.SemaphoreType.DMA((n_test,)),
            pltpu.SemaphoreType.DMA((n_test,)),
            pltpu.SemaphoreType.DMA((n_build,)),
            pltpu.SemaphoreType.DMA((n_build,)),
            pltpu.SemaphoreType.DMA((n_test,)),
            pltpu.SemaphoreType.DMA((n_test,)),
        ],
        compiler_params=pltpu.CompilerParams(has_side_effects=True, collective_id=1),
    )(partial, test_gram, build_gram)


def mttkrp_kernel(chunk, n_test_blocks, n_stmt_blocks, slot_tests, slot_builds, slot_stmts,
                  live_count, test_ref, build_ref, tile_ref, out_ref, acc_ref):
    q = pl.program_id(0)
    c = pl.program_id(1)
    n_chunks = pl.num_programs(1)

    @pl.when((q == 0) & (c == 0))
    def _():
        out_ref[...] = jnp.zeros_like(out_ref)

    @pl.when(c == 0)
    def _():
        acc_ref[...] = jnp.zeros_like(acc_ref)

    live = q < live_count[0]

    @pl.when(live)
    def _():
        build_block = build_ref[...].astype(jnp.float32)
        total = acc_ref[...]
        for i in range(chunk):
            test_row = test_ref[i : i + 1, :].astype(jnp.float32)
            khatri_rao = (test_row * build_block).astype(jnp.bfloat16)
            total = total + jnp.dot(tile_ref[i], khatri_rao, preferred_element_type=jnp.float32)
        acc_ref[...] = total

    @pl.when(live & (c == n_chunks - 1))
    def _():
        block = jnp.clip(slot_stmts[q], 0, n_stmt_blocks - 1)
        rows = pl.ds(pl.multiple_of(block * TILE, TILE), TILE)
        out_ref[rows, :] += acc_ref[...]


def local_mttkrp(slot_values, slot_tests, slot_builds, slot_stmts, live_count, test_slab, build_slab):
    slots, width = slot_values.shape[0], slot_values.shape[1]
    rank = test_slab.shape[1]
    per_block = width // CHUNK
    n_test_blocks = test_slab.shape[0] // width
    n_build_blocks = build_slab.shape[0] // width

    def test_map(q, c, tests, builds, stmts, count):
        return (jnp.clip(tests[q], 0, n_test_blocks - 1) * per_block + c, 0)

    def build_map(q, c, tests, builds, stmts, count):
        return (jnp.clip(builds[q], 0, n_build_blocks - 1), 0)

    grid_spec = pltpu.PrefetchScalarGridSpec(
        num_scalar_prefetch=4,
        grid=(slots, per_block),
        in_specs=[
            pl.BlockSpec((CHUNK, rank), test_map),
            pl.BlockSpec((width, rank), build_map),
            pl.BlockSpec((None, CHUNK, width, width), lambda q, c, *info: (q, c, 0, 0)),
        ],
        out_specs=pl.BlockSpec((SB * width, rank), lambda q, c, *info: (0, 0)),
        scratch_shapes=[pltpu.VMEM((width, rank), jnp.float32)],
    )
    return pl.pallas_call(
        functools.partial(mttkrp_kernel, CHUNK, n_test_blocks, SB),
        out_shape=jax.ShapeDtypeStruct((SB * width, rank), jnp.float32),
        grid_spec=grid_spec,
    )(slot_tests, slot_builds, slot_stmts, live_count, test_slab, build_slab, slot_values)


def shards(tile_values, tile_test, tile_stmt, tile_build, tile_count, test_factor, build_factor):
    test_slab, build_slab = gather_factors(test_factor[0], build_factor[0])
    slot_values = tile_values[0, 0, 0]
    running_sum = local_mttkrp(
        slot_values, tile_test[0, 0, 0], tile_build[0, 0, 0], tile_stmt[0, 0, 0],
        tile_count[0, 0], test_slab, build_slab)
    slab_test_gram = jnp.dot(test_slab.T, test_slab, preferred_element_type=jnp.float32)
    slab_build_gram = jnp.dot(build_slab.T, build_slab, preferred_element_type=jnp.float32)
    owned_sums, inverse = exchange_and_invert(running_sum, slab_test_gram, slab_build_gram)
    solved = jnp.dot(owned_sums, inverse, precision=lax.Precision.HIGHEST, preferred_element_type=jnp.float32)
    return solved[None]


def solution(mesh):
    return jax.shard_map(
        shards,
        mesh=mesh,
        in_specs=(
            P("build", "test", "stmt", None, None, None, None),
            P("build", "test", "stmt", None),
            P("build", "test", "stmt", None),
            P("build", "test", "stmt", None),
            P("build", "test", "stmt"),
            P("test", ("build", "stmt"), None),
            P("build", ("test", "stmt"), None),
        ),
        out_specs=P("stmt", ("build", "test"), None),
        check_vma=False,
    )
```

```python
import functools

import jax
import jax.numpy as jnp
from jax import lax
from jax.experimental import pallas as pl
from jax.experimental.pallas import tpu as pltpu
from jax.sharding import PartitionSpec as P

TILE = 128
SB = 2
MESH = pl.DeviceIdType.MESH
CHUNK = 128


def gather_kernel(n_build, n_test, n_stmt, test_in, build_in, test_out, build_out,
                  test_scr, build_scr, local_sem, t1_send, t1_recv, b1_send, b1_recv,
                  t2_send, t2_recv, b2_send, b2_recv):
    b = lax.axis_index("build")
    t = lax.axis_index("test")
    s = lax.axis_index("stmt")

    barrier = pltpu.get_barrier_semaphore()
    for j in range(n_stmt):
        @pl.when(j != s)
        def _():
            pl.semaphore_signal(barrier, 1, device_id=(b, t, j), device_id_type=MESH)
    for j in range(n_build):
        @pl.when(j != b)
        def _():
            pl.semaphore_signal(barrier, 1, device_id=(j, t, s), device_id_type=MESH)
    for j in range(n_test):
        @pl.when(j != t)
        def _():
            pl.semaphore_signal(barrier, 1, device_id=(b, j, s), device_id_type=MESH)
    pl.semaphore_wait(barrier, n_stmt + n_build + n_test - 3)

    def t1(j, slot):
        return pltpu.make_async_remote_copy(
            src_ref=test_in, dst_ref=test_scr.at[b, slot], send_sem=t1_send.at[j],
            recv_sem=t1_recv.at[slot], device_id=(b, t, j), device_id_type=MESH)

    def b1(j, slot):
        return pltpu.make_async_remote_copy(
            src_ref=build_in, dst_ref=build_scr.at[t, slot], send_sem=b1_send.at[j],
            recv_sem=b1_recv.at[slot], device_id=(b, t, j), device_id_type=MESH)

    def t2(j, slot):
        return pltpu.make_async_remote_copy(
            src_ref=test_scr.at[b], dst_ref=test_scr.at[slot], send_sem=t2_send.at[j],
            recv_sem=t2_recv.at[slot], device_id=(j, t, s), device_id_type=MESH)

    def b2(j, slot):
        return pltpu.make_async_remote_copy(
            src_ref=build_scr.at[t], dst_ref=build_scr.at[slot], send_sem=b2_send.at[j],
            recv_sem=b2_recv.at[slot], device_id=(b, j, s), device_id_type=MESH)

    for j in range(n_stmt):
        @pl.when(j != s)
        def _():
            t1(j, s).start()
            b1(j, s).start()
    own_test = pltpu.make_async_copy(test_in, test_scr.at[b, s], local_sem.at[0])
    own_build = pltpu.make_async_copy(build_in, build_scr.at[t, s], local_sem.at[1])
    own_test.start()
    own_build.start()
    own_test.wait()
    own_build.wait()
    for j in range(n_stmt):
        @pl.when(j != s)
        def _():
            t1(j, s).wait_send()
            b1(j, s).wait_send()
            t1(j, j).wait_recv()
            b1(j, j).wait_recv()

    for j in range(n_build):
        @pl.when(j != b)
        def _():
            t2(j, b).start()
    for j in range(n_test):
        @pl.when(j != t)
        def _():
            b2(j, t).start()
    for j in range(n_build):
        @pl.when(j != b)
        def _():
            t2(j, b).wait_send()
            t2(j, j).wait_recv()
    for j in range(n_test):
        @pl.when(j != t)
        def _():
            b2(j, t).wait_send()
            b2(j, j).wait_recv()
    test_out[...] = test_scr[...]
    build_out[...] = build_scr[...]


def gather_factors(test_rows, build_rows):
    n_build = lax.axis_size("build")
    n_test = lax.axis_size("test")
    n_stmt = lax.axis_size("stmt")
    vmem = pl.BlockSpec(memory_space=pltpu.VMEM)
    test_shape = (n_build, n_stmt, *test_rows.shape)
    build_shape = (n_test, n_stmt, *build_rows.shape)
    dma = pltpu.SemaphoreType.DMA
    test_pieces, build_pieces = pl.pallas_call(
        functools.partial(gather_kernel, n_build, n_test, n_stmt),
        out_shape=(
            jax.ShapeDtypeStruct(test_shape, test_rows.dtype),
            jax.ShapeDtypeStruct(build_shape, build_rows.dtype),
        ),
        in_specs=[vmem, vmem],
        out_specs=(vmem, vmem),
        scratch_shapes=[
            pltpu.VMEM(test_shape, test_rows.dtype),
            pltpu.VMEM(build_shape, build_rows.dtype),
            dma((2,)),
            dma((n_stmt,)), dma((n_stmt,)), dma((n_stmt,)), dma((n_stmt,)),
            dma((n_build,)), dma((n_build,)), dma((n_test,)), dma((n_test,)),
        ],
        compiler_params=pltpu.CompilerParams(has_side_effects=True, collective_id=0),
    )(test_rows, build_rows)
    return (
        test_pieces.reshape(-1, test_rows.shape[-1]),
        build_pieces.reshape(-1, build_rows.shape[-1]),
    )


def sweep_in_place(a_ref):
    n = a_ref.shape[0]
    lane = lax.broadcasted_iota(jnp.int32, (1, n), 1)

    def step(k, row):
        is_k = lane == k
        pivot = jnp.sum(jnp.where(is_k, row, 0.0), axis=1, keepdims=True)
        inv = 1.0 / pivot
        scaled = jnp.where(is_k, 1.0 - inv, row * inv)
        column = jnp.transpose(jnp.broadcast_to(row, (TILE, n)))
        following = jnp.minimum(k + 1, n - 1)
        next_factor = jnp.sum(jnp.where(lane == following, row, 0.0), axis=1, keepdims=True)
        next_row = a_ref[pl.ds(following, 1), :] - next_factor * scaled
        for h in range(n // TILE):
            lanes = slice(h * TILE, (h + 1) * TILE)
            a_ref[:, lanes] = a_ref[:, lanes] - column * scaled[:, lanes]
        a_ref[pl.ds(k, 1), :] = jnp.where(is_k, -inv, row * inv)
        return next_row

    lax.fori_loop(0, n, step, a_ref[0:1, :], unroll=128)
    a_ref[...] = -a_ref[...]


def tail_kernel(n_build, n_test, part_ref, test_gram_ref, build_gram_ref, owned_ref, inv_ref,
                rs_buf, test_buf, build_buf, product_buf, gram_buf,
                rs_send, rs_recv, test_send, test_recv, build_send, build_recv,
                gram_send, gram_recv):
    b = lax.axis_index("build")
    t = lax.axis_index("test")
    s = lax.axis_index("stmt")
    n_rs = n_build * n_test
    rs_rows = part_ref.shape[0] // n_rs
    g_rows = test_gram_ref.shape[0] // n_test
    me = b * n_test + t

    def rs_copy(m, dst_slot):
        return pltpu.make_async_remote_copy(
            src_ref=part_ref.at[pl.ds(m * rs_rows, rs_rows)], dst_ref=rs_buf.at[dst_slot],
            send_sem=rs_send.at[m], recv_sem=rs_recv.at[dst_slot],
            device_id=(m // n_test, m % n_test, s), device_id_type=MESH)

    def test_copy(j, dst_slot):
        return pltpu.make_async_remote_copy(
            src_ref=test_gram_ref.at[pl.ds(j * g_rows, g_rows)], dst_ref=test_buf.at[dst_slot],
            send_sem=test_send.at[j], recv_sem=test_recv.at[dst_slot],
            device_id=(b, j, s), device_id_type=MESH)

    def build_copy(j, dst_slot):
        return pltpu.make_async_remote_copy(
            src_ref=build_gram_ref.at[pl.ds(t * g_rows, g_rows)], dst_ref=build_buf.at[dst_slot],
            send_sem=build_send.at[j], recv_sem=build_recv.at[dst_slot],
            device_id=(j, t, s), device_id_type=MESH)

    def gram_copy(j, dst_slot):
        return pltpu.make_async_remote_copy(
            src_ref=product_buf, dst_ref=gram_buf.at[dst_slot],
            send_sem=gram_send.at[j], recv_sem=gram_recv.at[dst_slot],
            device_id=(b, j, s), device_id_type=MESH)

    barrier = pltpu.get_barrier_semaphore()
    for m in range(n_rs):
        @pl.when(m != me)
        def _():
            pl.semaphore_signal(barrier, 1, device_id=(m // n_test, m % n_test, s), device_id_type=MESH)
    pl.semaphore_wait(barrier, n_rs - 1)

    for j in range(n_build):
        @pl.when(j != b)
        def _():
            build_copy(j, b).start()
    for j in range(n_test):
        @pl.when(j != t)
        def _():
            test_copy(j, t).start()
    build_buf[pl.ds(b, 1)] = build_gram_ref[pl.ds(pl.multiple_of(t * g_rows, g_rows), g_rows), :][None]
    test_buf[pl.ds(t, 1)] = test_gram_ref[pl.ds(pl.multiple_of(t * g_rows, g_rows), g_rows), :][None]

    for j in range(n_build):
        @pl.when(j != b)
        def _():
            build_copy(j, b).wait_send()
            build_copy(j, j).wait_recv()
    for j in range(n_test):
        @pl.when(j != t)
        def _():
            test_copy(j, t).wait_send()
            test_copy(j, j).wait_recv()

    test_rows = test_buf[0]
    for j in range(1, n_test):
        test_rows = test_rows + test_buf[j]
    build_rows = build_buf[0]
    for j in range(1, n_build):
        build_rows = build_rows + build_buf[j]
    product_buf[...] = test_rows * build_rows

    for j in range(n_test):
        @pl.when(j != t)
        def _():
            gram_copy(j, t).start()
    gram_buf[pl.ds(t, 1)] = product_buf[...][None]
    for j in range(n_test):
        @pl.when(j != t)
        def _():
            gram_copy(j, t).wait_send()
            gram_copy(j, j).wait_recv()
    for j in range(n_test):
        inv_ref[j * g_rows:(j + 1) * g_rows, :] = gram_buf[j]

    for m in range(n_rs):
        @pl.when(m != me)
        def _():
            rs_copy(m, me).start()
    rs_buf[pl.ds(me, 1)] = part_ref[pl.ds(pl.multiple_of(me * rs_rows, rs_rows), rs_rows), :][None]

    sweep_in_place(inv_ref)

    for m in range(n_rs):
        @pl.when(m != me)
        def _():
            rs_copy(m, me).wait_send()
            rs_copy(m, m).wait_recv()
    owned = rs_buf[0]
    for m in range(1, n_rs):
        owned = owned + rs_buf[m]
    owned_ref[...] = owned


def exchange_and_invert(partial, test_gram, build_gram):
    n_build = lax.axis_size("build")
    n_test = lax.axis_size("test")
    n_rs = n_build * n_test
    rows, rank = partial.shape
    rs_rows = rows // n_rs
    g_rows = rank // n_test
    vmem = pl.BlockSpec(memory_space=pltpu.VMEM)
    f32 = jnp.float32
    return pl.pallas_call(
        functools.partial(tail_kernel, n_build, n_test),
        out_shape=(
            jax.ShapeDtypeStruct((rs_rows, rank), f32),
            jax.ShapeDtypeStruct((rank, rank), f32),
        ),
        in_specs=[vmem, vmem, vmem],
        out_specs=(vmem, vmem),
        scratch_shapes=[
            pltpu.VMEM((n_rs, rs_rows, rank), f32),
            pltpu.VMEM((n_test, g_rows, rank), f32),
            pltpu.VMEM((n_build, g_rows, rank), f32),
            pltpu.VMEM((g_rows, rank), f32),
            pltpu.VMEM((n_test, g_rows, rank), f32),
            pltpu.SemaphoreType.DMA((n_rs,)),
            pltpu.SemaphoreType.DMA((n_rs,)),
            pltpu.SemaphoreType.DMA((n_test,)),
            pltpu.SemaphoreType.DMA((n_test,)),
            pltpu.SemaphoreType.DMA((n_build,)),
            pltpu.SemaphoreType.DMA((n_build,)),
            pltpu.SemaphoreType.DMA((n_test,)),
            pltpu.SemaphoreType.DMA((n_test,)),
        ],
        compiler_params=pltpu.CompilerParams(has_side_effects=True, collective_id=1),
    )(partial, test_gram, build_gram)


def mttkrp_kernel(chunk, n_test_blocks, n_stmt_blocks, slot_tests, slot_builds, slot_stmts,
                  live_count, test_ref, build_ref, tile_ref, out_ref, acc_ref):
    q = pl.program_id(0)
    c = pl.program_id(1)
    n_chunks = pl.num_programs(1)

    @pl.when((q == 0) & (c == 0))
    def _():
        out_ref[...] = jnp.zeros_like(out_ref)

    @pl.when(c == 0)
    def _():
        acc_ref[...] = jnp.zeros_like(acc_ref)

    live = q < live_count[0]

    @pl.when(live)
    def _():
        build_block = build_ref[...].astype(jnp.float32)
        total = acc_ref[...]
        for i in range(chunk):
            test_row = test_ref[i : i + 1, :].astype(jnp.float32)
            khatri_rao = (test_row * build_block).astype(jnp.bfloat16)
            total = total + jnp.dot(tile_ref[i], khatri_rao, preferred_element_type=jnp.float32)
        acc_ref[...] = total

    @pl.when(live & (c == n_chunks - 1))
    def _():
        block = jnp.clip(slot_stmts[q], 0, n_stmt_blocks - 1)
        rows = pl.ds(pl.multiple_of(block * TILE, TILE), TILE)
        out_ref[rows, :] += acc_ref[...]


def local_mttkrp(slot_values, slot_tests, slot_builds, slot_stmts, live_count, test_slab, build_slab):
    slots, width = slot_values.shape[0], slot_values.shape[1]
    rank = test_slab.shape[1]
    per_block = width // CHUNK
    n_test_blocks = test_slab.shape[0] // width
    n_build_blocks = build_slab.shape[0] // width

    def test_map(q, c, tests, builds, stmts, count):
        return (jnp.clip(tests[q], 0, n_test_blocks - 1) * per_block + c, 0)

    def build_map(q, c, tests, builds, stmts, count):
        return (jnp.clip(builds[q], 0, n_build_blocks - 1), 0)

    grid_spec = pltpu.PrefetchScalarGridSpec(
        num_scalar_prefetch=4,
        grid=(slots, per_block),
        in_specs=[
            pl.BlockSpec((CHUNK, rank), test_map),
            pl.BlockSpec((width, rank), build_map),
            pl.BlockSpec((None, CHUNK, width, width), lambda q, c, *info: (q, c, 0, 0)),
        ],
        out_specs=pl.BlockSpec((SB * width, rank), lambda q, c, *info: (0, 0)),
        scratch_shapes=[pltpu.VMEM((width, rank), jnp.float32)],
    )
    return pl.pallas_call(
        functools.partial(mttkrp_kernel, CHUNK, n_test_blocks, SB),
        out_shape=jax.ShapeDtypeStruct((SB * width, rank), jnp.float32),
        grid_spec=grid_spec,
    )(slot_tests, slot_builds, slot_stmts, live_count, test_slab, build_slab, slot_values)


def shards(tile_values, tile_test, tile_stmt, tile_build, tile_count, test_factor, build_factor):
    test_slab, build_slab = gather_factors(test_factor[0], build_factor[0])
    slot_values = tile_values[0, 0, 0]
    running_sum = local_mttkrp(
        slot_values, tile_test[0, 0, 0], tile_build[0, 0, 0], tile_stmt[0, 0, 0],
        tile_count[0, 0], test_slab, build_slab)
    slab_test_gram = jnp.dot(test_slab.T, test_slab, preferred_element_type=jnp.float32)
    slab_build_gram = jnp.dot(build_slab.T, build_slab, preferred_element_type=jnp.float32)
    owned_sums, inverse = exchange_and_invert(running_sum, slab_test_gram, slab_build_gram)
    solved = jnp.dot(owned_sums, inverse, precision=lax.Precision.HIGHEST, preferred_element_type=jnp.float32)
    return solved[None]


def solution(mesh):
    return jax.shard_map(
        shards,
        mesh=mesh,
        in_specs=(
            P("build", "test", "stmt", None, None, None, None),
            P("build", "test", "stmt", None),
            P("build", "test", "stmt", None),
            P("build", "test", "stmt", None),
            P("build", "test", "stmt"),
            P("test", ("build", "stmt"), None),
            P("build", ("test", "stmt"), None),
        ),
        out_specs=P("stmt", ("build", "test"), None),
        check_vma=False,
    )
```

```python
import functools

import jax
import jax.numpy as jnp
from jax import lax
from jax.experimental import pallas as pl
from jax.experimental.pallas import tpu as pltpu
from jax.sharding import PartitionSpec as P

TILE = 128
SB = 2
MESH = pl.DeviceIdType.MESH
CHUNK = 128


def gather_kernel(n_build, n_test, n_stmt, test_in, build_in, test_out, build_out,
                  test_scr, build_scr, local_sem, t1_send, t1_recv, b1_send, b1_recv,
                  t2_send, t2_recv, b2_send, b2_recv):
    b = lax.axis_index("build")
    t = lax.axis_index("test")
    s = lax.axis_index("stmt")

    barrier = pltpu.get_barrier_semaphore()
    for j in range(n_stmt):
        @pl.when(j != s)
        def _():
            pl.semaphore_signal(barrier, 1, device_id=(b, t, j), device_id_type=MESH)
    for j in range(n_build):
        @pl.when(j != b)
        def _():
            pl.semaphore_signal(barrier, 1, device_id=(j, t, s), device_id_type=MESH)
    for j in range(n_test):
        @pl.when(j != t)
        def _():
            pl.semaphore_signal(barrier, 1, device_id=(b, j, s), device_id_type=MESH)
    pl.semaphore_wait(barrier, n_stmt + n_build + n_test - 3)

    def t1(j, slot):
        return pltpu.make_async_remote_copy(
            src_ref=test_in, dst_ref=test_scr.at[b, slot], send_sem=t1_send.at[j],
            recv_sem=t1_recv.at[slot], device_id=(b, t, j), device_id_type=MESH)

    def b1(j, slot):
        return pltpu.make_async_remote_copy(
            src_ref=build_in, dst_ref=build_scr.at[t, slot], send_sem=b1_send.at[j],
            recv_sem=b1_recv.at[slot], device_id=(b, t, j), device_id_type=MESH)

    def t2(j, slot):
        return pltpu.make_async_remote_copy(
            src_ref=test_scr.at[b], dst_ref=test_scr.at[slot], send_sem=t2_send.at[j],
            recv_sem=t2_recv.at[slot], device_id=(j, t, s), device_id_type=MESH)

    def b2(j, slot):
        return pltpu.make_async_remote_copy(
            src_ref=build_scr.at[t], dst_ref=build_scr.at[slot], send_sem=b2_send.at[j],
            recv_sem=b2_recv.at[slot], device_id=(b, j, s), device_id_type=MESH)

    for j in range(n_stmt):
        @pl.when(j != s)
        def _():
            t1(j, s).start()
            b1(j, s).start()
    own_test = pltpu.make_async_copy(test_in, test_scr.at[b, s], local_sem.at[0])
    own_build = pltpu.make_async_copy(build_in, build_scr.at[t, s], local_sem.at[1])
    own_test.start()
    own_build.start()
    own_test.wait()
    own_build.wait()
    for j in range(n_stmt):
        @pl.when(j != s)
        def _():
            t1(j, s).wait_send()
            b1(j, s).wait_send()
            t1(j, j).wait_recv()
            b1(j, j).wait_recv()

    for j in range(n_build):
        @pl.when(j != b)
        def _():
            t2(j, b).start()
    for j in range(n_test):
        @pl.when(j != t)
        def _():
            b2(j, t).start()
    for j in range(n_build):
        @pl.when(j != b)
        def _():
            t2(j, b).wait_send()
            t2(j, j).wait_recv()
    for j in range(n_test):
        @pl.when(j != t)
        def _():
            b2(j, t).wait_send()
            b2(j, j).wait_recv()
    test_out[...] = test_scr[...]
    build_out[...] = build_scr[...]


def gather_factors(test_rows, build_rows):
    n_build = lax.axis_size("build")
    n_test = lax.axis_size("test")
    n_stmt = lax.axis_size("stmt")
    vmem = pl.BlockSpec(memory_space=pltpu.VMEM)
    test_shape = (n_build, n_stmt, *test_rows.shape)
    build_shape = (n_test, n_stmt, *build_rows.shape)
    dma = pltpu.SemaphoreType.DMA
    test_pieces, build_pieces = pl.pallas_call(
        functools.partial(gather_kernel, n_build, n_test, n_stmt),
        out_shape=(
            jax.ShapeDtypeStruct(test_shape, test_rows.dtype),
            jax.ShapeDtypeStruct(build_shape, build_rows.dtype),
        ),
        in_specs=[vmem, vmem],
        out_specs=(vmem, vmem),
        scratch_shapes=[
            pltpu.VMEM(test_shape, test_rows.dtype),
            pltpu.VMEM(build_shape, build_rows.dtype),
            dma((2,)),
            dma((n_stmt,)), dma((n_stmt,)), dma((n_stmt,)), dma((n_stmt,)),
            dma((n_build,)), dma((n_build,)), dma((n_test,)), dma((n_test,)),
        ],
        compiler_params=pltpu.CompilerParams(has_side_effects=True, collective_id=0),
    )(test_rows, build_rows)
    return (
        test_pieces.reshape(-1, test_rows.shape[-1]),
        build_pieces.reshape(-1, build_rows.shape[-1]),
    )


def sweep_in_place(a_ref):
    n = a_ref.shape[0]
    lane = lax.broadcasted_iota(jnp.int32, (1, n), 1)

    def step(k, row):
        is_k = lane == k
        pivot = jnp.sum(jnp.where(is_k, row, 0.0), axis=1, keepdims=True)
        inv = 1.0 / pivot
        scaled = jnp.where(is_k, 1.0 - inv, row * inv)
        column = jnp.transpose(jnp.broadcast_to(row, (TILE, n)))
        following = jnp.minimum(k + 1, n - 1)
        next_factor = jnp.sum(jnp.where(lane == following, row, 0.0), axis=1, keepdims=True)
        next_row = a_ref[pl.ds(following, 1), :] - next_factor * scaled
        for h in range(n // TILE):
            lanes = slice(h * TILE, (h + 1) * TILE)
            a_ref[:, lanes] = a_ref[:, lanes] - column * scaled[:, lanes]
        a_ref[pl.ds(k, 1), :] = jnp.where(is_k, -inv, row * inv)
        return next_row

    lax.fori_loop(0, n, step, a_ref[0:1, :], unroll=256)
    a_ref[...] = -a_ref[...]


def tail_kernel(n_build, n_test, part_ref, test_gram_ref, build_gram_ref, owned_ref, inv_ref,
                rs_buf, test_buf, build_buf, product_buf, gram_buf,
                rs_send, rs_recv, test_send, test_recv, build_send, build_recv,
                gram_send, gram_recv):
    b = lax.axis_index("build")
    t = lax.axis_index("test")
    s = lax.axis_index("stmt")
    n_rs = n_build * n_test
    rs_rows = part_ref.shape[0] // n_rs
    g_rows = test_gram_ref.shape[0] // n_test
    me = b * n_test + t

    def rs_copy(m, dst_slot):
        return pltpu.make_async_remote_copy(
            src_ref=part_ref.at[pl.ds(m * rs_rows, rs_rows)], dst_ref=rs_buf.at[dst_slot],
            send_sem=rs_send.at[m], recv_sem=rs_recv.at[dst_slot],
            device_id=(m // n_test, m % n_test, s), device_id_type=MESH)

    def test_copy(j, dst_slot):
        return pltpu.make_async_remote_copy(
            src_ref=test_gram_ref.at[pl.ds(j * g_rows, g_rows)], dst_ref=test_buf.at[dst_slot],
            send_sem=test_send.at[j], recv_sem=test_recv.at[dst_slot],
            device_id=(b, j, s), device_id_type=MESH)

    def build_copy(j, dst_slot):
        return pltpu.make_async_remote_copy(
            src_ref=build_gram_ref.at[pl.ds(t * g_rows, g_rows)], dst_ref=build_buf.at[dst_slot],
            send_sem=build_send.at[j], recv_sem=build_recv.at[dst_slot],
            device_id=(j, t, s), device_id_type=MESH)

    def gram_copy(j, dst_slot):
        return pltpu.make_async_remote_copy(
            src_ref=product_buf, dst_ref=gram_buf.at[dst_slot],
            send_sem=gram_send.at[j], recv_sem=gram_recv.at[dst_slot],
            device_id=(b, j, s), device_id_type=MESH)

    barrier = pltpu.get_barrier_semaphore()
    for m in range(n_rs):
        @pl.when(m != me)
        def _():
            pl.semaphore_signal(barrier, 1, device_id=(m // n_test, m % n_test, s), device_id_type=MESH)
    pl.semaphore_wait(barrier, n_rs - 1)

    for j in range(n_build):
        @pl.when(j != b)
        def _():
            build_copy(j, b).start()
    for j in range(n_test):
        @pl.when(j != t)
        def _():
            test_copy(j, t).start()
    build_buf[pl.ds(b, 1)] = build_gram_ref[pl.ds(pl.multiple_of(t * g_rows, g_rows), g_rows), :][None]
    test_buf[pl.ds(t, 1)] = test_gram_ref[pl.ds(pl.multiple_of(t * g_rows, g_rows), g_rows), :][None]

    for j in range(n_build):
        @pl.when(j != b)
        def _():
            build_copy(j, b).wait_send()
            build_copy(j, j).wait_recv()
    for j in range(n_test):
        @pl.when(j != t)
        def _():
            test_copy(j, t).wait_send()
            test_copy(j, j).wait_recv()

    test_rows = test_buf[0]
    for j in range(1, n_test):
        test_rows = test_rows + test_buf[j]
    build_rows = build_buf[0]
    for j in range(1, n_build):
        build_rows = build_rows + build_buf[j]
    product_buf[...] = test_rows * build_rows

    for j in range(n_test):
        @pl.when(j != t)
        def _():
            gram_copy(j, t).start()
    gram_buf[pl.ds(t, 1)] = product_buf[...][None]
    for j in range(n_test):
        @pl.when(j != t)
        def _():
            gram_copy(j, t).wait_send()
            gram_copy(j, j).wait_recv()
    for j in range(n_test):
        inv_ref[j * g_rows:(j + 1) * g_rows, :] = gram_buf[j]

    for m in range(n_rs):
        @pl.when(m != me)
        def _():
            rs_copy(m, me).start()
    rs_buf[pl.ds(me, 1)] = part_ref[pl.ds(pl.multiple_of(me * rs_rows, rs_rows), rs_rows), :][None]

    sweep_in_place(inv_ref)

    for m in range(n_rs):
        @pl.when(m != me)
        def _():
            rs_copy(m, me).wait_send()
            rs_copy(m, m).wait_recv()
    owned = rs_buf[0]
    for m in range(1, n_rs):
        owned = owned + rs_buf[m]
    owned_ref[...] = owned


def exchange_and_invert(partial, test_gram, build_gram):
    n_build = lax.axis_size("build")
    n_test = lax.axis_size("test")
    n_rs = n_build * n_test
    rows, rank = partial.shape
    rs_rows = rows // n_rs
    g_rows = rank // n_test
    vmem = pl.BlockSpec(memory_space=pltpu.VMEM)
    f32 = jnp.float32
    return pl.pallas_call(
        functools.partial(tail_kernel, n_build, n_test),
        out_shape=(
            jax.ShapeDtypeStruct((rs_rows, rank), f32),
            jax.ShapeDtypeStruct((rank, rank), f32),
        ),
        in_specs=[vmem, vmem, vmem],
        out_specs=(vmem, vmem),
        scratch_shapes=[
            pltpu.VMEM((n_rs, rs_rows, rank), f32),
            pltpu.VMEM((n_test, g_rows, rank), f32),
            pltpu.VMEM((n_build, g_rows, rank), f32),
            pltpu.VMEM((g_rows, rank), f32),
            pltpu.VMEM((n_test, g_rows, rank), f32),
            pltpu.SemaphoreType.DMA((n_rs,)),
            pltpu.SemaphoreType.DMA((n_rs,)),
            pltpu.SemaphoreType.DMA((n_test,)),
            pltpu.SemaphoreType.DMA((n_test,)),
            pltpu.SemaphoreType.DMA((n_build,)),
            pltpu.SemaphoreType.DMA((n_build,)),
            pltpu.SemaphoreType.DMA((n_test,)),
            pltpu.SemaphoreType.DMA((n_test,)),
        ],
        compiler_params=pltpu.CompilerParams(has_side_effects=True, collective_id=1),
    )(partial, test_gram, build_gram)


def mttkrp_kernel(chunk, n_test_blocks, n_stmt_blocks, slot_tests, slot_builds, slot_stmts,
                  live_count, test_ref, build_ref, tile_ref, out_ref, acc_ref):
    q = pl.program_id(0)
    c = pl.program_id(1)
    n_chunks = pl.num_programs(1)

    @pl.when((q == 0) & (c == 0))
    def _():
        out_ref[...] = jnp.zeros_like(out_ref)

    @pl.when(c == 0)
    def _():
        acc_ref[...] = jnp.zeros_like(acc_ref)

    live = q < live_count[0]

    @pl.when(live)
    def _():
        build_block = build_ref[...].astype(jnp.float32)
        total = acc_ref[...]
        for i in range(chunk):
            test_row = test_ref[i : i + 1, :].astype(jnp.float32)
            khatri_rao = (test_row * build_block).astype(jnp.bfloat16)
            total = total + jnp.dot(tile_ref[i], khatri_rao, preferred_element_type=jnp.float32)
        acc_ref[...] = total

    @pl.when(live & (c == n_chunks - 1))
    def _():
        block = jnp.clip(slot_stmts[q], 0, n_stmt_blocks - 1)
        rows = pl.ds(pl.multiple_of(block * TILE, TILE), TILE)
        out_ref[rows, :] += acc_ref[...]


def local_mttkrp(slot_values, slot_tests, slot_builds, slot_stmts, live_count, test_slab, build_slab):
    slots, width = slot_values.shape[0], slot_values.shape[1]
    rank = test_slab.shape[1]
    per_block = width // CHUNK
    n_test_blocks = test_slab.shape[0] // width
    n_build_blocks = build_slab.shape[0] // width

    def test_map(q, c, tests, builds, stmts, count):
        return (jnp.clip(tests[q], 0, n_test_blocks - 1) * per_block + c, 0)

    def build_map(q, c, tests, builds, stmts, count):
        return (jnp.clip(builds[q], 0, n_build_blocks - 1), 0)

    grid_spec = pltpu.PrefetchScalarGridSpec(
        num_scalar_prefetch=4,
        grid=(slots, per_block),
        in_specs=[
            pl.BlockSpec((CHUNK, rank), test_map),
            pl.BlockSpec((width, rank), build_map),
            pl.BlockSpec((None, CHUNK, width, width), lambda q, c, *info: (q, c, 0, 0)),
        ],
        out_specs=pl.BlockSpec((SB * width, rank), lambda q, c, *info: (0, 0)),
        scratch_shapes=[pltpu.VMEM((width, rank), jnp.float32)],
    )
    return pl.pallas_call(
        functools.partial(mttkrp_kernel, CHUNK, n_test_blocks, SB),
        out_shape=jax.ShapeDtypeStruct((SB * width, rank), jnp.float32),
        grid_spec=grid_spec,
    )(slot_tests, slot_builds, slot_stmts, live_count, test_slab, build_slab, slot_values)


def shards(tile_values, tile_test, tile_stmt, tile_build, tile_count, test_factor, build_factor):
    test_slab, build_slab = gather_factors(test_factor[0], build_factor[0])
    slot_values = tile_values[0, 0, 0]
    running_sum = local_mttkrp(
        slot_values, tile_test[0, 0, 0], tile_build[0, 0, 0], tile_stmt[0, 0, 0],
        tile_count[0, 0], test_slab, build_slab)
    slab_test_gram = jnp.dot(test_slab.T, test_slab, preferred_element_type=jnp.float32)
    slab_build_gram = jnp.dot(build_slab.T, build_slab, preferred_element_type=jnp.float32)
    owned_sums, inverse = exchange_and_invert(running_sum, slab_test_gram, slab_build_gram)
    solved = jnp.dot(owned_sums, inverse, precision=lax.Precision.HIGHEST, preferred_element_type=jnp.float32)
    return solved[None]


def solution(mesh):
    return jax.shard_map(
        shards,
        mesh=mesh,
        in_specs=(
            P("build", "test", "stmt", None, None, None, None),
            P("build", "test", "stmt", None),
            P("build", "test", "stmt", None),
            P("build", "test", "stmt", None),
            P("build", "test", "stmt"),
            P("test", ("build", "stmt"), None),
            P("build", ("test", "stmt"), None),
        ),
        out_specs=P("stmt", ("build", "test"), None),
        check_vma=False,
    )
```
